128 devices in a mesh: row: 8 (over y_hi, x), col: 16 (over y_lo, z, core).
Axes of the slice: x: 4, y: 4 (y_hi: 2, y_lo: 2; y = y_hi * 2 + y_lo), z: 4, core: 2. Of those that a mesh axis runs over, the one named last changes fastest.
Arguments:
- eigvecs: float32 [512, 65536], P(('row', 'col')), may hold values from -6 to 6
- reflectors: float32 [24, 256, 128], replicated, as said below
- offsets: int32 [24], replicated, may hold values from 0 to 65280, as said below
- lengths: int32 [24], replicated, may hold values from 128 to 256, as said below
- panels: float32 [65536, 1024], P(('row', 'col')), as said below
Outputs:
- vectors: float32 [512, 65536], P(('row', 'col'))
The draws below stay inside these ranges and needn't reach their ends.
Inputs may be any that keep to these rules, and one draw needn't show every extreme that they name: `reflectors`: block b's column c is zero in rows above c and in rows c + 128 and below, and 1 in row c. `panels`: column c is zero in rows above 128 + c and 1 in row 128 + c. `offsets`: both ends are reached in every draw. `lengths`: both ends are reached in every draw.
All inputs are finite; a program needn't handle non-finite values.
Results may differ from the reference program's by a relative error of at most 0.0003.
Values sent between devices are 32-bit elements; how exact they have to be, the bound alone decides.
No kernel may reach another device: no remote copies, remote signals or barrier semaphores. Data moves between devices by JAX's collectives and lax.ppermute only.
A program may use at most 128 MiB of HBM per device.

```python
import jax
import jax.numpy as jnp
from jax import lax

N = 65536
B = 128
NBLK = 24
NPAN = 8
K = 512


def draw_reflectors(key, part):
    row_index = jnp.arange(2 * B)[None, :, None]
    column = jnp.arange(B)[None, None, :]
    noise = 0.05 * jax.random.normal(key, (NBLK, 2 * B, B), jnp.float32)
    inside = (row_index > column) & (row_index < column + B)
    return jnp.where(row_index == column, 1.0, jnp.where(inside, noise, 0.0)).astype(jnp.float32)


def draw_panels(key, part):
    row_index = jnp.arange(N)[:, None]
    leading = B + jnp.arange(NPAN * B)[None, :]
    noise = jax.random.normal(key, (N, NPAN * B), jnp.float32)
    return jnp.where(row_index == leading, 1.0, jnp.where(row_index > leading, noise, 0.0)).astype(jnp.float32)


def draw_offsets(key, part):
    values = jax.random.randint(jax.random.fold_in(key, 11), (NBLK,), 0, N - 2 * B + 1, jnp.int32)
    return values.at[0].set(N - 2 * B).at[NBLK - 1].set(0)


def draw_lengths(key, part):
    values = jax.random.randint(jax.random.fold_in(key, 23), (NBLK,), B, 2 * B + 1, jnp.int32)
    return values.at[1].set(2 * B).at[2].set(B)


def levels(own_key, shape, cuts, smallest, high):
    def one(position, blocks):
        steps = jax.random.uniform(jax.random.fold_in(jax.random.fold_in(own_key, 6), position), (blocks,), jnp.float32, smallest / len(cuts), high / len(cuts))
        return jnp.repeat(jnp.exp(steps), shape[position] // blocks).reshape((-1,) + (1,) * (len(shape) - position - 1))

    gain = one(*cuts[0])
    for cut in cuts[1:]:
        gain = gain * one(*cut)
    return gain


def scatter_about(own_key, dims, scale, most, split=(), held_as=jnp.bfloat16):
    gain = levels(own_key, dims, split, -0.22, 0.18) if split else 1.0
    array = jax.random.normal(own_key, dims, jnp.float32) * scale * gain
    return jnp.minimum(jnp.maximum(array, -most), most).astype(held_as)


def setup_inputs(seed: int = 0) -> dict:
    keys = jax.random.split(jax.random.key(seed), 6)
    eigvecs = scatter_about(keys[0], (K, N), 1.0, 6.0, ((0, 128),), jnp.float32)
    reflectors = draw_reflectors(jax.random.fold_in(keys[5], 71), 0)
    offsets = draw_offsets(jax.random.fold_in(keys[5], 71), 0)
    lengths = draw_lengths(jax.random.fold_in(keys[5], 71), 0)
    panels = draw_panels(jax.random.fold_in(keys[5], 71), 0)
    return dict(eigvecs=eigvecs, reflectors=reflectors, offsets=offsets, lengths=lengths, panels=panels)


exact_mode = lax.Precision.HIGHEST


def unit_inverse(triangle):
    dimension = triangle.shape[-1]
    identity = jnp.eye(dimension, dtype=triangle.dtype)
    diagonal = jnp.sum(triangle * identity, axis=-1)
    nilpotent = triangle / diagonal[..., :, None] - identity
    result = identity - nilpotent
    power = nilpotent
    reach = 2
    while reach < dimension:
        power = jnp.matmul(power, power, precision=exact_mode)
        result = result + jnp.matmul(result, power, precision=exact_mode)
        reach = reach * 2
    return result / diagonal[..., None, :]


def wy_inverse(correlation, width):
    dimension = correlation.shape[-1]
    identity = jnp.eye(dimension, dtype=correlation.dtype)
    triangle = jnp.triu(correlation, 1) + 0.5 * correlation * identity
    count = dimension // width
    if count == 1:
        return unit_inverse(triangle)
    diagonal_blocks = jnp.stack([triangle[i * width:(i + 1) * width, i * width:(i + 1) * width] for i in range(count)])
    inverses = unit_inverse(diagonal_blocks)
    columns = []
    for j in range(count):
        pieces = [None] * count
        pieces[j] = inverses[j]
        for i in range(j - 1, -1, -1):
            total = jnp.zeros((width, width), correlation.dtype)
            for k in range(i + 1, j + 1):
                total = total + jnp.dot(triangle[i * width:(i + 1) * width, k * width:(k + 1) * width], pieces[k], precision=exact_mode)
            pieces[i] = -jnp.dot(inverses[i], total, precision=exact_mode)
        for i in range(j + 1, count):
            pieces[i] = jnp.zeros((width, width), correlation.dtype)
        columns.append(jnp.concatenate(pieces, axis=0))
    return jnp.concatenate(columns, axis=1)


def chase_blocks(current, reflectors, offsets, lengths):
    extent = reflectors.shape[1]
    row_index = jnp.arange(extent, dtype=jnp.int32)[None, :, None]
    masked = jnp.where(row_index < lengths[:, None, None], reflectors, jnp.zeros((), reflectors.dtype))
    correlations = jnp.einsum("brc,brd->bcd", masked, masked, precision=exact_mode)
    factors = wy_inverse(correlations, reflectors.shape[2])

    def apply_block(carried, scanned):
        vectors, factor, offset = scanned
        window = lax.dynamic_slice_in_dim(carried, offset.astype(jnp.int32), extent, 1)
        projected = jnp.dot(window, vectors, precision=exact_mode)
        window = window - jnp.dot(jnp.dot(projected, factor.T, precision=exact_mode), vectors.T, precision=exact_mode)
        return lax.dynamic_update_slice_in_dim(carried, window, offset.astype(jnp.int32), 1), None

    result, unused = lax.scan(apply_block, current, (masked, factors, offsets))
    return result


def reference(eigvecs, reflectors, offsets, lengths, panels):
    current = chase_blocks(eigvecs, reflectors, offsets, lengths)
    panel_factors = wy_inverse(jnp.dot(panels.T, panels, precision=exact_mode), B)
    for panel_index in range(NPAN - 1, -1, -1):
        column_start = panel_index * B
        vectors = panels[:, column_start:column_start + B]
        factor = panel_factors[column_start:column_start + B, column_start:column_start + B]
        projected = jnp.dot(current, vectors, precision=exact_mode)
        current = current - jnp.dot(jnp.dot(projected, factor.T, precision=exact_mode), vectors.T, precision=exact_mode)
    return current
```

```python
import jax
import jax.numpy as jnp
from jax import lax
from jax.experimental import pallas as pl
from jax.experimental.pallas import tpu as pltpu
from jax.sharding import Mesh, PartitionSpec as P

F32 = jnp.float32
BF16 = jnp.bfloat16
AXES = ("yh", "x", "yl", "z", "c")
CHIPS = ("yh", "x", "yl", "z")
VMEM_LIMIT = 48 * 1024 * 1024

NN = (((1,), (0,)), ((), ()))
NT = (((1,), (1,)), ((), ()))
TN = (((0,), (0,)), ((), ()))


def dg(a, b, dims=NN):
    return lax.dot_general(a, b, dims, preferred_element_type=F32)


def split(a):
    high = a.astype(BF16)
    low = (a - high.astype(F32)).astype(BF16)
    return high, low


def dot3(a, b, dims=NN):
    (ah, al), (bh, bl) = a, b
    return dg(ah, bh, dims) + (dg(ah, bl, dims) + dg(al, bh, dims))


def dot3_stacked(a, b):
    (ah, al), (bh, bl) = a, b
    return dg(jnp.concatenate([ah, ah, al], axis=1), jnp.concatenate([bh, bl, bh], axis=0))


def iotas(n):
    return (
        lax.broadcasted_iota(jnp.int32, (n, n), 0),
        lax.broadcasted_iota(jnp.int32, (n, n), 1),
    )


def inverse_of_half(grams):
    n = grams[0].shape[0]
    row, col = iotas(n)
    eye = (row == col).astype(F32)
    upper = row < col
    inverses, strict, scale = [], [], []
    for gram in grams:
        diagonal = gram * (0.5 * eye)
        by_row = jnp.sum(diagonal, axis=1, keepdims=True)
        by_col = jnp.sum(diagonal, axis=0, keepdims=True)
        nil = jnp.where(upper, gram / by_row, 0.0)
        strict.append(nil)
        scale.append(1.0 / by_col)
        first = ((row ^ col) == 1) & ((row & 1) == 0)
        inverses.append(eye - jnp.where(first, nil, 0.0))
    size = 2
    while size < n:
        corner = ((row // (2 * size)) == (col // (2 * size))) & ((row & size) == 0) & ((col & size) != 0)
        halves = [split(x) for x in inverses]
        corners = [split(jnp.where(corner, nil, 0.0)) for nil in strict]
        middles = [split(dot3_stacked(x, m)) for x, m in zip(halves, corners)]
        inverses = [x - dot3_stacked(y, h) for x, y, h in zip(inverses, middles, halves)]
        size *= 2
    return [x * s for x, s in zip(inverses, scale)]


TOGETHER = 4


def chase_kernel(offsets, lengths, e_ref, m_ref, o_ref, kh_ref, kl_ref):
    blocks, extent, width = m_ref.shape
    o_ref[...] = e_ref[...]
    row = lax.broadcasted_iota(jnp.int32, (extent, width), 0)

    def prepare(group, carry):
        masked = []
        for u in range(TOGETHER):
            b = group * TOGETHER + u
            masked.append(split(jnp.where(row < lengths[b], m_ref[b], 0.0)))
        grams = [dot3(m, m, TN) for m in masked]
        factors = [split(f) for f in inverse_of_half(grams)]
        lefts = [split(dot3(m, f, NT)) for m, f in zip(masked, factors)]
        for u in range(TOGETHER):
            high, low = split(dot3(lefts[u], masked[u], NT))
            b = group * TOGETHER + u
            kh_ref[b] = high
            kl_ref[b] = low
        return carry

    lax.fori_loop(0, blocks // TOGETHER, prepare, 0)

    rows = e_ref.shape[1]
    tiles = e_ref.shape[0]
    lane = lax.broadcasted_iota(jnp.int32, (rows, 128), 1)

    def step(b, carry):
        offset = offsets[b]
        tile = jnp.minimum(offset // 128, tiles - 3)
        shift = offset - tile * 128
        v0, v1, v2 = o_ref[tile], o_ref[tile + 1], o_ref[tile + 2]
        left = (128 - shift) & 127
        r0 = pltpu.roll(v0, left, 1)
        r1 = pltpu.roll(v1, left, 1)
        r2 = pltpu.roll(v2, left, 1)
        inside = lane < 128 - shift
        window = jnp.concatenate([jnp.where(inside, r0, r1), jnp.where(inside, r1, r2)], axis=1)
        high = window.astype(BF16).astype(F32)
        both = jnp.concatenate([high, window - high], axis=0).astype(BF16)
        change = dg(both, kh_ref[b]) + dg(both, kl_ref[b])
        change = change[:rows] + change[rows:]
        right = shift & 127
        q0 = pltpu.roll(change[:, :128], right, 1)
        q1 = pltpu.roll(change[:, 128:], right, 1)
        after = lane >= shift
        o_ref[tile] = v0 - jnp.where(after, q0, 0.0)
        o_ref[tile + 1] = v1 - jnp.where(after, q1, q0)
        o_ref[tile + 2] = v2 - jnp.where(after, 0.0, q1)
        return carry

    lax.fori_loop(0, blocks, step, 0)


def vmem():
    return pl.BlockSpec(memory_space=pltpu.VMEM)


def smem():
    return pl.BlockSpec(memory_space=pltpu.SMEM)


def params():
    return pltpu.CompilerParams(vmem_limit_bytes=VMEM_LIMIT)


def chase(tiles, reflectors, offsets, lengths):
    blocks, extent, width = reflectors.shape
    return pl.pallas_call(
        chase_kernel,
        out_shape=jax.ShapeDtypeStruct(tiles.shape, F32),
        in_specs=[smem(), smem(), vmem(), vmem()],
        out_specs=vmem(),
        scratch_shapes=[pltpu.VMEM((blocks, extent, extent), BF16)] * 2,
        compiler_params=params(),
        cost_estimate=pl.CostEstimate(flops=20 * 10**9, bytes_accessed=5 << 20, transcendentals=0),
        name="chase",
    )(offsets, lengths, tiles, reflectors)


WIDE = 256
PAIRS = [(i, j) for i in range(4) for j in range(i, 4)]


def gram_kernel(v_ref, g_ref):
    halves = [split(v_ref[:, i * WIDE : (i + 1) * WIDE]) for i in range(4)]
    for at, (i, j) in enumerate(PAIRS):
        block = dot3(halves[i], halves[j], TN)
        for h in range(2):
            g_ref[pl.ds((at * 2 + h) * WIDE, WIDE), :] = block[:, h * 128 : (h + 1) * 128]


def gram(panels):
    return pl.pallas_call(
        gram_kernel,
        out_shape=jax.ShapeDtypeStruct((len(PAIRS) * 2 * WIDE, 128), F32),
        in_specs=[vmem()],
        out_specs=vmem(),
        compiler_params=params(),
        cost_estimate=pl.CostEstimate(flops=2 * 10**9, bytes_accessed=4 << 20, transcendentals=0),
        name="gram",
    )(panels)


def factor_kernel(g_ref, th_ref, tl_ref, sh_ref, sl_ref):
    def block(at):
        return jnp.concatenate(
            [g_ref[pl.ds((at * 2 + h) * WIDE, WIDE), :] for h in range(2)], axis=1
        )

    other = 0
    diagonals = []
    for at, (i, j) in enumerate(PAIRS):
        if i == j:
            diagonals.append(block(at))
        else:
            high, low = split(block(at).T)
            sh_ref[other] = high
            sl_ref[other] = low
            other += 1
    small = []
    for d in diagonals:
        small.extend([d[:128, :128], d[128:, 128:]])
    inverses = inverse_of_half(small[:4]) + inverse_of_half(small[4:])
    for p, d in enumerate(diagonals):
        a, c = inverses[2 * p], inverses[2 * p + 1]
        corner = -dot3_stacked(split(dot3_stacked(split(a), split(d[:128, 128:]))), split(c))
        whole = jnp.concatenate(
            [
                jnp.concatenate([a.T, jnp.zeros((128, 128), F32)], axis=1),
                jnp.concatenate([corner.T, c.T], axis=1),
            ],
            axis=0,
        )
        high, low = split(whole)
        th_ref[p] = high
        tl_ref[p] = low


def factor(g):
    shapes = [(4, WIDE, WIDE)] * 2 + [(6, WIDE, WIDE)] * 2
    return pl.pallas_call(
        factor_kernel,
        out_shape=[jax.ShapeDtypeStruct(s, BF16) for s in shapes],
        in_specs=[vmem()],
        out_specs=[vmem()] * 4,
        compiler_params=params(),
        cost_estimate=pl.CostEstimate(flops=8 * 10**9, bytes_accessed=5 << 20, transcendentals=0),
        name="factor",
    )(g)


def rows_of(ref, j):
    return jnp.concatenate([ref[pl.ds(j * 4 + r, 64, stride=32), :] for r in range(4)], axis=0)


def project_kernel(core, e_ref, own_ref, other_ref, p_ref):
    c = core[0]
    total = [jnp.zeros((256, WIDE), F32) for _ in range(4)]
    for v_ref, first in ((own_ref, 4 * c), (other_ref, 4 - 4 * c)):
        left = split(jnp.concatenate([rows_of(e_ref, first + k) for k in range(4)], axis=1))
        for n in range(4):
            total[n] += dot3(left, split(v_ref[:, n * WIDE : (n + 1) * WIDE]))
    for n in range(8):
        block = total[n // 2][:, (n % 2) * 128 : (n % 2) * 128 + 128]
        for r in range(4):
            p_ref[pl.ds(n * 4 + r, 64, stride=32), :] = block[r * 64 : (r + 1) * 64]


def project(core, e, own, other):
    return pl.pallas_call(
        project_kernel,
        out_shape=jax.ShapeDtypeStruct(e.shape, F32),
        in_specs=[smem(), vmem(), vmem(), vmem()],
        out_specs=vmem(),
        compiler_params=params(),
        cost_estimate=pl.CostEstimate(flops=2 * 10**9, bytes_accessed=6 << 20, transcendentals=0),
        name="project",
    )(core, e, own, other)


def solve_kernel(p_ref, th_ref, tl_ref, sh_ref, sl_ref, w_ref):
    total = p_ref[0]
    for s in range(1, p_ref.shape[0]):
        total = total + p_ref[s]
    rest = [
        jnp.concatenate([total[8 * p : 8 * p + 4], total[8 * p + 4 : 8 * p + 8]], axis=1)
        for p in range(4)
    ]

    def times(a, bh, bl):
        high = a.astype(BF16).astype(F32)
        both = jnp.concatenate([high, a - high], axis=0).astype(BF16)
        product = dg(both, bh) + dg(both, bl)
        return product[:4] + product[4:]

    others = [(i, j) for (i, j) in PAIRS if i != j]
    pieces = [None] * 4
    for q in range(3, -1, -1):
        solved = times(rest[q], th_ref[q], tl_ref[q])
        pieces[q] = jnp.concatenate([solved[:, :128], solved[:, 128:]], axis=0)
        for p in range(q):
            at = others.index((p, q))
            rest[p] = rest[p] - times(solved, sh_ref[at], sl_ref[at])
    result = jnp.concatenate(pieces, axis=0)
    w_ref[...] = jnp.broadcast_to(result[None], w_ref.shape)


def solve(p, factors):
    return pl.pallas_call(
        solve_kernel,
        out_shape=jax.ShapeDtypeStruct(p.shape, F32),
        in_specs=[vmem()] * 5,
        out_specs=vmem(),
        compiler_params=params(),
        cost_estimate=pl.CostEstimate(flops=10**9, bytes_accessed=4 << 20, transcendentals=0),
        name="solve",
    )(p, *factors)


def update_kernel(core, e_ref, w_ref, own_ref, other_ref, o_ref):
    c = core[0]
    left = split(jnp.concatenate([rows_of(w_ref, n) for n in range(8)], axis=1))
    for v_ref, first in ((own_ref, 4 * c), (other_ref, 4 - 4 * c)):
        for k in range(2):
            change = dot3(left, split(v_ref[k * WIDE : (k + 1) * WIDE, :]), NT)
            for h in range(2):
                j = first + 2 * k + h
                for r in range(4):
                    at = pl.ds(j * 4 + r, 64, stride=32)
                    o_ref[at, :] = e_ref[at, :] - change[r * 64 : (r + 1) * 64, h * 128 : (h + 1) * 128]


def update(core, e, w, own, other):
    return pl.pallas_call(
        update_kernel,
        out_shape=jax.ShapeDtypeStruct(e.shape, F32),
        in_specs=[smem(), vmem(), vmem(), vmem(), vmem()],
        out_specs=vmem(),
        compiler_params=params(),
        cost_estimate=pl.CostEstimate(flops=2 * 10**9, bytes_accessed=7 << 20, transcendentals=0),
        name="update",
    )(core, e, w, own, other)


def to_chips(a):
    return lax.all_to_all(a, CHIPS, split_axis=0, concat_axis=0, tiled=True)


def body(eigvecs, reflectors, offsets, lengths, panels):
    core = lax.axis_index("c").astype(jnp.int32).reshape(1)
    other = lax.ppermute(panels, "c", [(0, 1), (1, 0)])
    partial = gram(panels).reshape(128, 40, 128)
    partial = lax.all_to_all(partial, AXES, split_axis=0, concat_axis=0, tiled=True)
    share = jnp.sum(partial, axis=0)
    whole = jnp.broadcast_to(share[None], (128, 40, 128))
    whole = lax.all_to_all(whole, AXES, split_axis=0, concat_axis=0, tiled=True)
    factors = factor(whole.reshape(5120, 128))

    tiles = eigvecs.reshape(4, 512, 128).transpose(1, 0, 2)
    chased = chase(tiles, reflectors, offsets, lengths)
    mine = to_chips(chased.reshape(64, 32, 128)).reshape(2048, 128)
    projected = to_chips(project(core, mine, panels, other).reshape(64, 32, 128))
    weights = to_chips(solve(projected, factors)).reshape(2048, 128)
    result = to_chips(update(core, mine, weights, panels, other).reshape(64, 32, 128))
    return result.reshape(512, 4, 128).transpose(1, 0, 2).reshape(4, 65536)


def solution(mesh):
    fine = Mesh(mesh.devices.reshape(2, 4, 2, 4, 2), AXES)
    return jax.shard_map(
        body,
        mesh=fine,
        in_specs=(P(AXES, None), P(), P(), P(), P(AXES, None)),
        out_specs=P(AXES, None),
        check_vma=False,
    )
```

```python
import jax
import jax.numpy as jnp
from jax import lax
from jax.experimental import pallas as pl
from jax.experimental.pallas import tpu as pltpu
from jax.sharding import Mesh, PartitionSpec as P

F32 = jnp.float32
BF16 = jnp.bfloat16
AXES = ("yh", "x", "yl", "z", "c")
CHIPS = ("yh", "x", "yl", "z")
VMEM_LIMIT = 20 * 1024 * 1024

NN = (((1,), (0,)), ((), ()))
NT = (((1,), (1,)), ((), ()))
TN = (((0,), (0,)), ((), ()))


def dg(a, b, dims=NN):
    return lax.dot_general(a, b, dims, preferred_element_type=F32)


def split(a):
    high = a.astype(BF16)
    low = (a - high.astype(F32)).astype(BF16)
    return high, low


def dot3(a, b, dims=NN):
    (ah, al), (bh, bl) = a, b
    return dg(ah, bh, dims) + (dg(ah, bl, dims) + dg(al, bh, dims))


def dot3_stacked(a, b):
    (ah, al), (bh, bl) = a, b
    return dg(jnp.concatenate([ah, ah, al], axis=1), jnp.concatenate([bh, bl, bh], axis=0))


def iotas(n):
    return (
        lax.broadcasted_iota(jnp.int32, (n, n), 0),
        lax.broadcasted_iota(jnp.int32, (n, n), 1),
    )


def inverse_of_half(grams):
    n = grams[0].shape[0]
    row, col = iotas(n)
    eye = (row == col).astype(F32)
    upper = row < col
    inverses, strict, scale = [], [], []
    for gram in grams:
        diagonal = gram * (0.5 * eye)
        by_row = jnp.sum(diagonal, axis=1, keepdims=True)
        by_col = jnp.sum(diagonal, axis=0, keepdims=True)
        nil = jnp.where(upper, gram / by_row, 0.0)
        strict.append(nil)
        scale.append(1.0 / by_col)
        first = ((row ^ col) == 1) & ((row & 1) == 0)
        inverses.append(eye - jnp.where(first, nil, 0.0))
    size = 2
    while size < n:
        corner = ((row // (2 * size)) == (col // (2 * size))) & ((row & size) == 0) & ((col & size) != 0)
        halves = [split(x) for x in inverses]
        corners = [split(jnp.where(corner, nil, 0.0)) for nil in strict]
        middles = [split(dot3_stacked(x, m)) for x, m in zip(halves, corners)]
        inverses = [x - dot3_stacked(y, h) for x, y, h in zip(inverses, middles, halves)]
        size *= 2
    return [x * s for x, s in zip(inverses, scale)]


TOGETHER = 4


def place(tile):
    return (tile // 8) * 18 + tile % 8


def chase_kernel(offsets, lengths, e_ref, m_ref, o_ref, kh_ref, kl_ref):
    blocks, extent, width = m_ref.shape
    tiles, rows = e_ref.shape[0], e_ref.shape[1]
    for s in range(tiles // 8):
        o_ref[s * 18 : s * 18 + 8] = e_ref[s * 8 : s * 8 + 8]
    row = lax.broadcasted_iota(jnp.int32, (extent, width), 0)

    def prepare(group, carry):
        masked = []
        for u in range(TOGETHER):
            b = group * TOGETHER + u
            masked.append(split(jnp.where(row < lengths[b], m_ref[b], 0.0)))
        grams = [dot3(m, m, TN) for m in masked]
        factors = [split(f) for f in inverse_of_half(grams)]
        lefts = [split(dot3(m, f, NT)) for m, f in zip(masked, factors)]
        for u in range(TOGETHER):
            high, low = split(dot3(lefts[u], masked[u], NT))
            b = group * TOGETHER + u
            kh_ref[b] = high
            kl_ref[b] = low
        return carry

    lax.fori_loop(0, blocks // TOGETHER, prepare, 0)
    lane = lax.broadcasted_iota(jnp.int32, (rows, 128), 1)

    def step(b, carry):
        offset = offsets[b]
        tile = jnp.minimum(offset // 128, tiles - 3)
        shift = offset - tile * 128
        at = [place(tile + k) for k in range(3)]
        v0, v1, v2 = [o_ref[k] for k in at]
        left = (128 - shift) & 127
        r0 = pltpu.roll(v0, left, 1)
        r1 = pltpu.roll(v1, left, 1)
        r2 = pltpu.roll(v2, left, 1)
        inside = lane < 128 - shift
        window = jnp.concatenate([jnp.where(inside, r0, r1), jnp.where(inside, r1, r2)], axis=1)
        high = window.astype(BF16).astype(F32)
        both = jnp.concatenate([high, window - high], axis=0).astype(BF16)
        change = dg(both, kh_ref[b]) + dg(both, kl_ref[b])
        change = change[:rows] + change[rows:]
        right = shift & 127
        q0 = pltpu.roll(change[:, :128], right, 1)
        q1 = pltpu.roll(change[:, 128:], right, 1)
        after = lane >= shift
        o_ref[at[0]] = v0 - jnp.where(after, q0, 0.0)
        o_ref[at[1]] = v1 - jnp.where(after, q1, q0)
        o_ref[at[2]] = v2 - jnp.where(after, 0.0, q1)
        return carry

    lax.fori_loop(0, blocks, step, 0)


def join_kernel(e_ref, g_ref, o_ref, share_ref, sems):
    chips = o_ref.shape[0] // 18
    share = g_ref[0:10]
    for s in range(1, chips):
        share = share + g_ref[s * 10 : s * 10 + 10]
    share_ref[...] = share
    copies = [
        pltpu.make_async_copy(share_ref, o_ref.at[pl.ds(s * 18 + 8, 10)], sems.at[s])
        for s in range(chips)
    ]
    for copy in copies:
        copy.start()
    for copy in copies:
        copy.wait()


def vmem():
    return pl.BlockSpec(memory_space=pltpu.VMEM)


def smem():
    return pl.BlockSpec(memory_space=pltpu.SMEM)


def params():
    return pltpu.CompilerParams(vmem_limit_bytes=VMEM_LIMIT)


def hbm():
    return pl.BlockSpec(memory_space=pltpu.HBM)


def chase(tiles, reflectors, offsets, lengths):
    blocks, extent, width = reflectors.shape
    return pl.pallas_call(
        chase_kernel,
        out_shape=jax.ShapeDtypeStruct((64 * 18, 4, 128), F32),
        in_specs=[smem(), smem(), vmem(), vmem()],
        out_specs=vmem(),
        scratch_shapes=[pltpu.VMEM((blocks, extent, extent), BF16)] * 2,
        compiler_params=params(),
        cost_estimate=pl.CostEstimate(flops=20 * 10**9, bytes_accessed=6 << 20, transcendentals=0),
        name="chase",
    )(offsets, lengths, tiles, reflectors)


def join(chased, parts):
    return pl.pallas_call(
        join_kernel,
        out_shape=jax.ShapeDtypeStruct(chased.shape, F32),
        in_specs=[hbm(), vmem()],
        out_specs=hbm(),
        scratch_shapes=[pltpu.VMEM((10, 4, 128), F32), pltpu.SemaphoreType.DMA((64,))],
        input_output_aliases={0: 0},
        compiler_params=params(),
        cost_estimate=pl.CostEstimate(flops=10**6, bytes_accessed=3 << 20, transcendentals=0),
        name="join",
    )(chased, parts)


WIDE = 256
ORDER = ((0, 1, 2, 3), (2, 0, 3, 1))
LOCAL = ((0, 1), (1, 2), (2, 3), (1, 1), (2, 2))
MADE = [(ORDER[c][i], ORDER[c][j]) for c in range(2) for (i, j) in LOCAL]
UPPER = [(i, j) for i in range(4) for j in range(i + 1, 4)]


def gram_kernel(core, own_ref, other_ref, g_ref):
    c = core[0]
    order = (2 * c, 1 - c, 2 + c, 3 - 2 * c)
    blocks = [None] * len(LOCAL)
    for ref in (own_ref, other_ref):
        halves = [split(ref[:, pl.ds(pl.multiple_of(o * WIDE, WIDE), WIDE)]) for o in order]
        for at, (i, j) in enumerate(LOCAL):
            block = dot3(halves[i], halves[j], TN)
            blocks[at] = block if blocks[at] is None else blocks[at] + block
    for at, block in enumerate(blocks):
        for h in range(2):
            g_ref[pl.ds((at * 2 + h) * WIDE, WIDE), :] = block[:, h * 128 : (h + 1) * 128]


def gram(core, own, other):
    return pl.pallas_call(
        gram_kernel,
        out_shape=jax.ShapeDtypeStruct((len(LOCAL) * 2 * WIDE, 128), F32),
        in_specs=[smem(), vmem(), vmem()],
        out_specs=vmem(),
        compiler_params=params(),
        cost_estimate=pl.CostEstimate(flops=2 * 10**9, bytes_accessed=5 << 20, transcendentals=0),
        name="gram",
    )(core, own, other)


def factor_kernel(core, own_ref, other_ref, th_ref, tl_ref, sh_ref, sl_ref):
    first = core[0] == 0

    def block(c, at):
        halves = []
        for h in range(2):
            rows = pl.ds((at * 2 + h) * WIDE, WIDE)
            mine, theirs = own_ref[rows, :], other_ref[rows, :]
            halves.append(jnp.where(first, mine, theirs) if c == 0 else jnp.where(first, theirs, mine))
        return jnp.concatenate(halves, axis=1)

    diagonals = [None] * 4
    for at, (i, j) in enumerate(MADE):
        value = block(at // len(LOCAL), at % len(LOCAL))
        if i == j:
            diagonals[i] = value
        else:
            high, low = split(value.T if i < j else value)
            slot = UPPER.index((min(i, j), max(i, j)))
            sh_ref[slot] = high
            sl_ref[slot] = low
    small = []
    for d in diagonals:
        small.extend([d[:128, :128], d[128:, 128:]])
    inverses = inverse_of_half(small[:4]) + inverse_of_half(small[4:])
    for p, d in enumerate(diagonals):
        a, c = inverses[2 * p], inverses[2 * p + 1]
        corner = -dot3_stacked(split(dot3_stacked(split(a), split(d[:128, 128:]))), split(c))
        whole = jnp.concatenate(
            [
                jnp.concatenate([a.T, jnp.zeros((128, 128), F32)], axis=1),
                jnp.concatenate([corner.T, c.T], axis=1),
            ],
            axis=0,
        )
        high, low = split(whole)
        th_ref[p] = high
        tl_ref[p] = low


def factor(core, own, other):
    shapes = [(4, WIDE, WIDE)] * 2 + [(6, WIDE, WIDE)] * 2
    return pl.pallas_call(
        factor_kernel,
        out_shape=[jax.ShapeDtypeStruct(s, BF16) for s in shapes],
        in_specs=[smem(), vmem(), vmem()],
        out_specs=[vmem()] * 4,
        compiler_params=params(),
        cost_estimate=pl.CostEstimate(flops=8 * 10**9, bytes_accessed=5 << 20, transcendentals=0),
        name="factor",
    )(core, own, other)


def rows_of(ref, j):
    stride = ref.shape[0] // 64
    return jnp.concatenate([ref[pl.ds(j * 4 + r, 64, stride=stride), :] for r in range(4)], axis=0)


def project_kernel(core, e_ref, own_ref, other_ref, p_ref):
    c = core[0]
    total = [jnp.zeros((256, WIDE), F32) for _ in range(4)]
    for v_ref, first in ((own_ref, 4 * c), (other_ref, 4 - 4 * c)):
        left = split(jnp.concatenate([rows_of(e_ref, first + k) for k in range(4)], axis=1))
        for n in range(4):
            total[n] += dot3(left, split(v_ref[:, n * WIDE : (n + 1) * WIDE]))
    for n in range(8):
        block = total[n // 2][:, (n % 2) * 128 : (n % 2) * 128 + 128]
        for r in range(4):
            p_ref[pl.ds(n * 4 + r, 64, stride=32), :] = block[r * 64 : (r + 1) * 64]


def project(core, e, own, other):
    return pl.pallas_call(
        project_kernel,
        out_shape=jax.ShapeDtypeStruct((2048, 128), F32),
        in_specs=[smem(), vmem(), vmem(), vmem()],
        out_specs=vmem(),
        compiler_params=params(),
        cost_estimate=pl.CostEstimate(flops=2 * 10**9, bytes_accessed=6 << 20, transcendentals=0),
        name="project",
    )(core, e, own, other)


def solve_kernel(p_ref, th_hbm, tl_hbm, sh_hbm, sl_hbm, w_ref, th_ref, tl_ref, sh_ref, sl_ref, sems):
    pairs = ((th_hbm, th_ref), (tl_hbm, tl_ref), (sh_hbm, sh_ref), (sl_hbm, sl_ref))
    copies = [pltpu.make_async_copy(a, b, sems.at[i]) for i, (a, b) in enumerate(pairs)]
    for copy in copies:
        copy.start()
    total = p_ref[0]
    for s in range(1, p_ref.shape[0]):
        total = total + p_ref[s]
    rest = [
        jnp.concatenate([total[8 * p : 8 * p + 4], total[8 * p + 4 : 8 * p + 8]], axis=1)
        for p in range(4)
    ]

    def times(a, bh, bl):
        high = a.astype(BF16).astype(F32)
        both = jnp.concatenate([high, a - high], axis=0).astype(BF16)
        product = dg(both, bh) + dg(both, bl)
        return product[:4] + product[4:]

    for copy in copies:
        copy.wait()
    pieces = [None] * 4
    for q in range(3, -1, -1):
        solved = times(rest[q], th_ref[q], tl_ref[q])
        pieces[q] = jnp.concatenate([solved[:, :128], solved[:, 128:]], axis=0)
        for p in range(q):
            at = UPPER.index((p, q))
            rest[p] = rest[p] - times(solved, sh_ref[at], sl_ref[at])
    result = jnp.concatenate(pieces, axis=0)
    w_ref[...] = jnp.broadcast_to(result[None], w_ref.shape)


def solve(p, factors):
    return pl.pallas_call(
        solve_kernel,
        out_shape=jax.ShapeDtypeStruct(p.shape, F32),
        in_specs=[vmem()] + [hbm()] * 4,
        out_specs=vmem(),
        scratch_shapes=[pltpu.VMEM((n, WIDE, WIDE), BF16) for n in (4, 4, 6, 6)]
        + [pltpu.SemaphoreType.DMA((4,))],
        compiler_params=params(),
        cost_estimate=pl.CostEstimate(flops=10**9, bytes_accessed=4 << 20, transcendentals=0),
        name="solve",
    )(p, *factors)


def update_kernel(core, e_ref, w_ref, own_ref, other_ref, o_ref):
    c = core[0]
    left = split(jnp.concatenate([rows_of(w_ref, n) for n in range(8)], axis=1))
    for v_ref, first in ((own_ref, 4 * c), (other_ref, 4 - 4 * c)):
        for k in range(2):
            change = dot3(left, split(v_ref[k * WIDE : (k + 1) * WIDE, :]), NT)
            for h in range(2):
                j = first + 2 * k + h
                for r in range(4):
                    before = e_ref[pl.ds(j * 4 + r, 64, stride=e_ref.shape[0] // 64), :]
                    part = change[r * 64 : (r + 1) * 64, h * 128 : (h + 1) * 128]
                    o_ref[pl.ds(j * 4 + r, 64, stride=32), :] = before - part


def update(core, e, w, own, other):
    return pl.pallas_call(
        update_kernel,
        out_shape=jax.ShapeDtypeStruct((2048, 128), F32),
        in_specs=[smem(), vmem(), vmem(), vmem(), vmem()],
        out_specs=vmem(),
        compiler_params=params(),
        cost_estimate=pl.CostEstimate(flops=2 * 10**9, bytes_accessed=7 << 20, transcendentals=0),
        name="update",
    )(core, e, w, own, other)


def to_chips(a):
    return lax.all_to_all(a, CHIPS, split_axis=0, concat_axis=0, tiled=True)


def swap_cores(a):
    return lax.ppermute(a, "c", [(0, 1), (1, 0)])


def body(eigvecs, reflectors, offsets, lengths, panels):
    core = lax.axis_index("c").astype(jnp.int32).reshape(1)
    other = swap_cores(panels)
    parts = to_chips(gram(core, panels, other).reshape(64, 40, 128))
    tiles = eigvecs.reshape(4, 512, 128).transpose(1, 0, 2)
    chased = chase(tiles, reflectors, offsets, lengths)
    sent = join(chased, parts.reshape(640, 4, 128))
    mine = to_chips(sent.reshape(64, 72, 128))
    half = mine[:, 32:].reshape(2560, 128)
    factors = factor(core, half, swap_cores(half))
    mine = mine.reshape(4608, 128)
    projected = to_chips(project(core, mine, panels, other).reshape(64, 32, 128))
    weights = to_chips(solve(projected, factors)).reshape(2048, 128)
    result = to_chips(update(core, mine, weights, panels, other).reshape(64, 32, 128))
    return result.reshape(64, 8, 4, 128).transpose(2, 0, 1, 3).reshape(4, 65536)


def solution(mesh):
    fine = Mesh(mesh.devices.reshape(2, 4, 2, 4, 2), AXES)
    return jax.shard_map(
        body,
        mesh=fine,
        in_specs=(P(AXES, None), P(), P(), P(), P(AXES, None)),
        out_specs=P(AXES, None),
        check_vma=False,
    )
```

```python
import jax
import jax.numpy as jnp
from jax import lax
from jax.experimental import pallas as pl
from jax.experimental.pallas import tpu as pltpu
from jax.sharding import Mesh, PartitionSpec as P

F32 = jnp.float32
BF16 = jnp.bfloat16
AXES = ("yh", "x", "yl", "z", "c")
CHIPS = ("yh", "x", "yl", "z")
VMEM_LIMIT = 20 * 1024 * 1024
LARGE = 58 * 1024 * 1024

NN = (((1,), (0,)), ((), ()))
NT = (((1,), (1,)), ((), ()))
TN = (((0,), (0,)), ((), ()))


def dg(a, b, dims=NN):
    return lax.dot_general(a, b, dims, preferred_element_type=F32)


def split(a):
    high = a.astype(BF16)
    low = (a - high.astype(F32)).astype(BF16)
    return high, low


def dot3(a, b, dims=NN):
    (ah, al), (bh, bl) = a, b
    return dg(ah, bh, dims) + (dg(ah, bl, dims) + dg(al, bh, dims))


def dot3_stacked(a, b):
    (ah, al), (bh, bl) = a, b
    return dg(jnp.concatenate([ah, ah, al], axis=1), jnp.concatenate([bh, bl, bh], axis=0))


def iotas(n):
    return (
        lax.broadcasted_iota(jnp.int32, (n, n), 0),
        lax.broadcasted_iota(jnp.int32, (n, n), 1),
    )


def inverse_of_half(grams):
    n = grams[0].shape[0]
    row, col = iotas(n)
    eye = (row == col).astype(F32)
    upper = row < col
    inverses, strict, scale = [], [], []
    for gram in grams:
        diagonal = gram * (0.5 * eye)
        by_row = jnp.sum(diagonal, axis=1, keepdims=True)
        by_col = jnp.sum(diagonal, axis=0, keepdims=True)
        nil = jnp.where(upper, gram / by_row, 0.0)
        strict.append(nil)
        scale.append(1.0 / by_col)
        first = ((row ^ col) == 1) & ((row & 1) == 0)
        inverses.append(eye - jnp.where(first, nil, 0.0))
    size = 2
    while size < n:
        corner = ((row // (2 * size)) == (col // (2 * size))) & ((row & size) == 0) & ((col & size) != 0)
        halves = [split(x) for x in inverses]
        corners = [split(jnp.where(corner, nil, 0.0)) for nil in strict]
        middles = [split(dot3_stacked(x, m)) for x, m in zip(halves, corners)]
        inverses = [x - dot3_stacked(y, h) for x, y, h in zip(inverses, middles, halves)]
        size *= 2
    return [x * s for x, s in zip(inverses, scale)]


TOGETHER = 4


def masked_block(lengths, m_ref, b):
    row = lax.broadcasted_iota(jnp.int32, m_ref.shape[1:], 0)
    return split(jnp.where(row < lengths[b], m_ref[b], 0.0))


def invert_kernel(lengths, m_ref, fh_ref, fl_ref):
    def group_of(group, carry):
        blocks = [group * TOGETHER + u for u in range(TOGETHER)]
        masked = [masked_block(lengths, m_ref, b) for b in blocks]
        grams = [dot3(m, m, TN) for m in masked]
        for b, f in zip(blocks, inverse_of_half(grams)):
            fh_ref[b], fl_ref[b] = split(f)
        return carry

    lax.fori_loop(0, m_ref.shape[0] // TOGETHER, group_of, 0)


def chase_kernel(offsets, lengths, e_ref, m_ref, fh_ref, fl_ref, o_ref, kh_ref, kl_ref):
    blocks = m_ref.shape[0]
    tiles, rows = e_ref.shape[0], e_ref.shape[1]
    o_ref[...] = e_ref[...]

    def group_of(group, carry):
        at = [group * TOGETHER + u for u in range(TOGETHER)]
        masked = [masked_block(lengths, m_ref, b) for b in at]
        lefts = [split(dot3(m, (fh_ref[b], fl_ref[b]), NT)) for m, b in zip(masked, at)]
        for left, m, b in zip(lefts, masked, at):
            kh_ref[b], kl_ref[b] = split(dot3(left, m, NT))
        return carry

    lax.fori_loop(0, blocks // TOGETHER, group_of, 0)
    lane = lax.broadcasted_iota(jnp.int32, (rows, 128), 1)

    def step(b, carry):
        offset = offsets[b]
        tile = jnp.minimum(offset // 128, tiles - 3)
        shift = offset - tile * 128
        v0, v1, v2 = o_ref[tile], o_ref[tile + 1], o_ref[tile + 2]
        left = (128 - shift) & 127
        r0 = pltpu.roll(v0, left, 1)
        r1 = pltpu.roll(v1, left, 1)
        r2 = pltpu.roll(v2, left, 1)
        inside = lane < 128 - shift
        window = jnp.concatenate([jnp.where(inside, r0, r1), jnp.where(inside, r1, r2)], axis=1)
        high = window.astype(BF16).astype(F32)
        both = jnp.concatenate([high, window - high], axis=0).astype(BF16)
        change = dg(both, kh_ref[b]) + dg(both, kl_ref[b])
        change = change[:rows] + change[rows:]
        right = shift & 127
        q0 = pltpu.roll(change[:, :128], right, 1)
        q1 = pltpu.roll(change[:, 128:], right, 1)
        after = lane >= shift
        o_ref[tile] = v0 - jnp.where(after, q0, 0.0)
        o_ref[tile + 1] = v1 - jnp.where(after, q1, q0)
        o_ref[tile + 2] = v2 - jnp.where(after, 0.0, q1)
        return carry

    lax.fori_loop(0, blocks, step, 0)


def share_kernel(g_ref, o_ref):
    sums = [g_ref[k] for k in range(4)]
    for s in range(4, g_ref.shape[0]):
        sums[s % 4] = sums[s % 4] + g_ref[s]
    total = (sums[0] + sums[1]) + (sums[2] + sums[3])
    o_ref[...] = jnp.broadcast_to(total[None], o_ref.shape)


def vmem():
    return pl.BlockSpec(memory_space=pltpu.VMEM)


def smem():
    return pl.BlockSpec(memory_space=pltpu.SMEM)


def params():
    return pltpu.CompilerParams(vmem_limit_bytes=VMEM_LIMIT)


def hbm():
    return pl.BlockSpec(memory_space=pltpu.HBM)


def invert(reflectors, lengths):
    blocks, extent, width = reflectors.shape
    shape = jax.ShapeDtypeStruct((blocks, width, width), BF16)
    return pl.pallas_call(
        invert_kernel,
        out_shape=[shape, shape],
        in_specs=[smem(), vmem()],
        out_specs=[vmem()] * 2,
        compiler_params=params(),
        cost_estimate=pl.CostEstimate(flops=10 * 10**9, bytes_accessed=5 << 20, transcendentals=0),
        name="invert",
    )(lengths, reflectors)


def chase(tiles, reflectors, offsets, lengths, fh, fl):
    blocks, extent, width = reflectors.shape
    return pl.pallas_call(
        chase_kernel,
        out_shape=jax.ShapeDtypeStruct(tiles.shape, F32),
        in_specs=[smem(), smem()] + [vmem()] * 4,
        out_specs=vmem(),
        scratch_shapes=[pltpu.VMEM((blocks, extent, extent), BF16)] * 2,
        compiler_params=params(),
        cost_estimate=pl.CostEstimate(flops=10 * 10**9, bytes_accessed=7 << 20, transcendentals=0),
        name="chase",
    )(offsets, lengths, tiles, reflectors, fh, fl)


def share(parts):
    return pl.pallas_call(
        share_kernel,
        out_shape=jax.ShapeDtypeStruct(parts.shape, F32),
        in_specs=[vmem()],
        out_specs=vmem(),
        compiler_params=params(),
        cost_estimate=pl.CostEstimate(flops=10**6, bytes_accessed=3 << 20, transcendentals=0),
        name="share",
    )(parts)


WIDE = 256
ORDER = ((0, 1, 2, 3), (2, 0, 3, 1))
LOCAL = ((0, 1), (1, 2), (2, 3), (1, 1), (2, 2))
MADE = [(ORDER[c][i], ORDER[c][j]) for c in range(2) for (i, j) in LOCAL]
UPPER = [(i, j) for i in range(4) for j in range(i + 1, 4)]


def gram_kernel(core, v_ref, *refs):
    c = core[0]
    g_ref = refs[-1]
    order = (2 * c, 1 - c, 2 + c, 3 - 2 * c)
    halves = [split(v_ref[:, pl.ds(pl.multiple_of(o * WIDE, WIDE), WIDE)]) for o in order]
    for at, (i, j) in enumerate(LOCAL):
        block = dot3(halves[i], halves[j], TN)
        for h in range(2):
            rows = pl.ds((at * 2 + h) * WIDE, WIDE)
            part = block[:, h * 128 : (h + 1) * 128]
            g_ref[rows, :] = part + refs[0][rows, :] if len(refs) == 2 else part


def gram(core, panels, *before):
    return pl.pallas_call(
        gram_kernel,
        out_shape=jax.ShapeDtypeStruct((len(LOCAL) * 2 * WIDE, 128), F32),
        in_specs=[smem(), vmem()] + [vmem()] * len(before),
        out_specs=vmem(),
        compiler_params=params(),
        cost_estimate=pl.CostEstimate(flops=10**9, bytes_accessed=4 << 20, transcendentals=0),
        name="gram",
    )(core, panels, *before)


def factor_kernel(core, own_ref, other_ref, th_ref, tl_ref, sh_ref, sl_ref):
    first = core[0] == 0

    def block(c, at):
        halves = []
        for h in range(2):
            rows = pl.ds((at * 2 + h) * WIDE, WIDE)
            mine, theirs = own_ref[rows, :], other_ref[rows, :]
            halves.append(jnp.where(first, mine, theirs) if c == 0 else jnp.where(first, theirs, mine))
        return jnp.concatenate(halves, axis=1)

    diagonals = [None] * 4
    for at, (i, j) in enumerate(MADE):
        value = block(at // len(LOCAL), at % len(LOCAL))
        if i == j:
            diagonals[i] = value
        else:
            high, low = split(value.T if i < j else value)
            slot = UPPER.index((min(i, j), max(i, j)))
            sh_ref[slot] = high
            sl_ref[slot] = low
    small = []
    for d in diagonals:
        small.extend([d[:128, :128], d[128:, 128:]])
    inverses = inverse_of_half(small[:4]) + inverse_of_half(small[4:])
    for p, d in enumerate(diagonals):
        a, c = inverses[2 * p], inverses[2 * p + 1]
        corner = -dot3_stacked(split(dot3_stacked(split(a), split(d[:128, 128:]))), split(c))
        whole = jnp.concatenate(
            [
                jnp.concatenate([a.T, jnp.zeros((128, 128), F32)], axis=1),
                jnp.concatenate([corner.T, c.T], axis=1),
            ],
            axis=0,
        )
        high, low = split(whole)
        th_ref[p] = high
        tl_ref[p] = low


def factor(core, own, other):
    shapes = [(4, WIDE, WIDE)] * 2 + [(6, WIDE, WIDE)] * 2
    return pl.pallas_call(
        factor_kernel,
        out_shape=[jax.ShapeDtypeStruct(s, BF16) for s in shapes],
        in_specs=[smem(), vmem(), vmem()],
        out_specs=[vmem()] * 4,
        compiler_params=params(),
        cost_estimate=pl.CostEstimate(flops=8 * 10**9, bytes_accessed=5 << 20, transcendentals=0),
        name="factor",
    )(core, own, other)


def rows_of(ref, j):
    stride = ref.shape[0] // 64
    return jnp.concatenate([ref[pl.ds(j * 4 + r, 64, stride=stride), :] for r in range(4)], axis=0)


def project_kernel(core, e_ref, own_hbm, other_hbm, p_ref, v_ref, sems):
    c = core[0]
    copies = []
    for n in range(4):
        columns = pl.ds(n * WIDE, WIDE)
        for side, ref in enumerate((own_hbm, other_hbm)):
            copy = pltpu.make_async_copy(ref.at[:, columns], v_ref.at[side, :, columns], sems.at[side, n])
            copy.start()
            copies.append(copy)
    lefts = [
        split(jnp.concatenate([rows_of(e_ref, first + k) for k in range(4)], axis=1))
        for first in (4 * c, 4 - 4 * c)
    ]
    for n in range(4):
        columns = pl.ds(n * WIDE, WIDE)
        total = None
        for side in range(2):
            copies[2 * n + side].wait()
            part = dot3(lefts[side], split(v_ref[side, :, columns]))
            total = part if total is None else total + part
        for h in range(2):
            for r in range(4):
                p_ref[pl.ds((2 * n + h) * 4 + r, 64, stride=32), :] = total[
                    r * 64 : (r + 1) * 64, h * 128 : (h + 1) * 128
                ]


def project(core, e, own, other):
    return pl.pallas_call(
        project_kernel,
        out_shape=jax.ShapeDtypeStruct((2048, 128), F32),
        in_specs=[smem(), vmem(), hbm(), hbm()],
        out_specs=vmem(),
        scratch_shapes=[pltpu.VMEM((2,) + own.shape, F32), pltpu.SemaphoreType.DMA((2, 4))],
        compiler_params=pltpu.CompilerParams(vmem_limit_bytes=LARGE),
        cost_estimate=pl.CostEstimate(flops=2 * 10**9, bytes_accessed=6 << 20, transcendentals=0),
        name="project",
    )(core, e, own, other)


def solve_kernel(p_ref, th_hbm, tl_hbm, sh_hbm, sl_hbm, w_ref, th_ref, tl_ref, sh_ref, sl_ref, sems):
    pairs = ((th_hbm, th_ref), (tl_hbm, tl_ref), (sh_hbm, sh_ref), (sl_hbm, sl_ref))
    copies = [pltpu.make_async_copy(a, b, sems.at[i]) for i, (a, b) in enumerate(pairs)]
    for copy in copies:
        copy.start()
    total = p_ref[0]
    for s in range(1, p_ref.shape[0]):
        total = total + p_ref[s]
    rest = [
        jnp.concatenate([total[8 * p : 8 * p + 4], total[8 * p + 4 : 8 * p + 8]], axis=1)
        for p in range(4)
    ]

    def times(a, bh, bl):
        high = a.astype(BF16).astype(F32)
        both = jnp.concatenate([high, a - high], axis=0).astype(BF16)
        product = dg(both, bh) + dg(both, bl)
        return product[:4] + product[4:]

    for copy in copies:
        copy.wait()
    pieces = [None] * 4
    for q in range(3, -1, -1):
        solved = times(rest[q], th_ref[q], tl_ref[q])
        pieces[q] = jnp.concatenate([solved[:, :128], solved[:, 128:]], axis=0)
        for p in range(q):
            at = UPPER.index((p, q))
            rest[p] = rest[p] - times(solved, sh_ref[at], sl_ref[at])
    result = jnp.concatenate(pieces, axis=0)
    w_ref[...] = jnp.broadcast_to(result[None], w_ref.shape)


def solve(p, factors):
    return pl.pallas_call(
        solve_kernel,
        out_shape=jax.ShapeDtypeStruct(p.shape, F32),
        in_specs=[vmem()] + [hbm()] * 4,
        out_specs=vmem(),
        scratch_shapes=[pltpu.VMEM((n, WIDE, WIDE), BF16) for n in (4, 4, 6, 6)]
        + [pltpu.SemaphoreType.DMA((4,))],
        compiler_params=pltpu.CompilerParams(vmem_limit_bytes=LARGE),
        cost_estimate=pl.CostEstimate(flops=10**9, bytes_accessed=4 << 20, transcendentals=0),
        name="solve",
    )(p, *factors)


def update_kernel(core, e_ref, w_ref, own_ref, other_ref, o_ref):
    c = core[0]
    left = split(jnp.concatenate([rows_of(w_ref, n) for n in range(8)], axis=1))
    for v_ref, first in ((own_ref, 4 * c), (other_ref, 4 - 4 * c)):
        for k in range(2):
            change = dot3(left, split(v_ref[k * WIDE : (k + 1) * WIDE, :]), NT)
            for h in range(2):
                j = first + 2 * k + h
                for r in range(4):
                    before = e_ref[pl.ds(j * 4 + r, 64, stride=e_ref.shape[0] // 64), :]
                    part = change[r * 64 : (r + 1) * 64, h * 128 : (h + 1) * 128]
                    o_ref[pl.ds(j * 4 + r, 64, stride=32), :] = before - part


def update(core, e, w, own, other):
    return pl.pallas_call(
        update_kernel,
        out_shape=jax.ShapeDtypeStruct((2048, 128), F32),
        in_specs=[smem(), vmem(), vmem(), vmem(), vmem()],
        out_specs=vmem(),
        compiler_params=params(),
        cost_estimate=pl.CostEstimate(flops=2 * 10**9, bytes_accessed=7 << 20, transcendentals=0),
        name="update",
    )(core, e, w, own, other)


def to_chips(a):
    return lax.all_to_all(a, CHIPS, split_axis=0, concat_axis=0, tiled=True)


def swap_cores(a):
    return lax.ppermute(a, "c", [(0, 1), (1, 0)])


def body(eigvecs, reflectors, offsets, lengths, panels):
    core = lax.axis_index("c").astype(jnp.int32).reshape(1)
    other = swap_cores(panels)
    parts = to_chips(gram(core, other, gram(core, panels)).reshape(64, 40, 128))
    factors = invert(reflectors, lengths)
    copies = share(parts)
    copies, factors = lax.optimization_barrier((copies, factors))
    half = to_chips(copies).reshape(2560, 128)
    tiles = eigvecs.reshape(4, 512, 128).transpose(1, 0, 2)
    chased = chase(tiles, reflectors, offsets, lengths, *factors)
    chased, half = lax.optimization_barrier((chased, half))
    mine = to_chips(chased.reshape(64, 32, 128)).reshape(2048, 128)
    solvers = factor(core, half, swap_cores(half))
    mine, solvers = lax.optimization_barrier((mine, solvers))
    projected = to_chips(project(core, mine, panels, other).reshape(64, 32, 128))
    weights = to_chips(solve(projected, solvers)).reshape(2048, 128)
    result = to_chips(update(core, mine, weights, panels, other).reshape(64, 32, 128))
    return result.reshape(64, 8, 4, 128).transpose(2, 0, 1, 3).reshape(4, 65536)


def solution(mesh):
    fine = Mesh(mesh.devices.reshape(2, 4, 2, 4, 2), AXES)
    return jax.shard_map(
        body,
        mesh=fine,
        in_specs=(P(AXES, None), P(), P(), P(), P(AXES, None)),
        out_specs=P(AXES, None),
        check_vma=False,
    )
```

```python
import jax
import jax.numpy as jnp
from jax import lax
from jax.experimental import pallas as pl
from jax.experimental.pallas import tpu as pltpu
from jax.sharding import Mesh, PartitionSpec as P

F32 = jnp.float32
BF16 = jnp.bfloat16
AXES = ("yh", "x", "yl", "z", "c")
CHIPS = ("yh", "x", "yl", "z")
VMEM_LIMIT = 20 * 1024 * 1024

NN = (((1,), (0,)), ((), ()))
NT = (((1,), (1,)), ((), ()))
TN = (((0,), (0,)), ((), ()))


def dg(a, b, dims=NN):
    return lax.dot_general(a, b, dims, preferred_element_type=F32)


def split(a):
    high = a.astype(BF16)
    low = (a - high.astype(F32)).astype(BF16)
    return high, low


def dot3(a, b, dims=NN):
    (ah, al), (bh, bl) = a, b
    return dg(ah, bh, dims) + (dg(ah, bl, dims) + dg(al, bh, dims))


def dot4(a, b):
    n = b[0].shape[1]
    right = jnp.concatenate(b, axis=1)
    both = dg(jnp.concatenate(a, axis=1), jnp.concatenate([right, right], axis=0))
    return both[:, :n] + both[:, n:]


def dot4_nt(a, b):
    n = b[0].shape[0]
    right = jnp.concatenate(b, axis=0)
    both = dg(jnp.concatenate(a, axis=1), jnp.concatenate([right, right], axis=1), NT)
    return both[:, :n] + both[:, n:]


def iotas(n):
    return (
        lax.broadcasted_iota(jnp.int32, (n, n), 0),
        lax.broadcasted_iota(jnp.int32, (n, n), 1),
    )


def inverse_of_half(grams):
    n = grams[0].shape[0]
    row, col = iotas(n)
    eye = (row == col).astype(F32)
    upper = row < col
    inverses, strict, scale = [], [], []
    for gram in grams:
        diagonal = gram * (0.5 * eye)
        by_row = jnp.sum(diagonal, axis=1, keepdims=True)
        by_col = jnp.sum(diagonal, axis=0, keepdims=True)
        nil = jnp.where(upper, gram / by_row, 0.0)
        strict.append(nil)
        scale.append(1.0 / by_col)
        first = ((row ^ col) == 1) & ((row & 1) == 0)
        inverses.append(eye - jnp.where(first, nil, 0.0))
    size = 2
    while size < n:
        corner = ((row // (2 * size)) == (col // (2 * size))) & ((row & size) == 0) & ((col & size) != 0)
        halves = [split(x) for x in inverses]
        corners = [split(jnp.where(corner, nil, 0.0)) for nil in strict]
        middles = [split(dot4(x, m)) for x, m in zip(halves, corners)]
        inverses = [x - dot4(y, h) for x, y, h in zip(inverses, middles, halves)]
        size *= 2
    return [x * s for x, s in zip(inverses, scale)]


TOGETHER = 8


def masked_block(lengths, m_ref, b):
    row = lax.broadcasted_iota(jnp.int32, m_ref.shape[1:], 0)
    return split(jnp.where(row < lengths[b], m_ref[b], 0.0))


def gram_of(m):
    width = m[0].shape[1]
    both = dg(m[0], jnp.concatenate(m, axis=1), TN)
    return both[:, :width] + both[:, width:] + dg(m[1], m[0], TN)


def invert_kernel(lengths, m_ref, fh_ref, fl_ref):
    def group_of(group, carry):
        blocks = [group * TOGETHER + u for u in range(TOGETHER)]
        masked = [masked_block(lengths, m_ref, b) for b in blocks]
        grams = [gram_of(m) for m in masked]
        for b, f in zip(blocks, inverse_of_half(grams)):
            fh_ref[b], fl_ref[b] = split(f)
        return carry

    lax.fori_loop(0, m_ref.shape[0] // TOGETHER, group_of, 0)


def chase_kernel(offsets, lengths, e_ref, m_ref, fh_ref, fl_ref, o_ref, kh_ref, kl_ref):
    blocks = m_ref.shape[0]
    tiles, rows = e_ref.shape[0], e_ref.shape[1]
    o_ref[...] = e_ref[...]

    def group_of(group, carry):
        at = [group * TOGETHER + u for u in range(TOGETHER)]
        masked = [masked_block(lengths, m_ref, b) for b in at]
        lefts = [split(dot4_nt(m, (fh_ref[b], fl_ref[b]))) for m, b in zip(masked, at)]
        for left, m, b in zip(lefts, masked, at):
            kh_ref[b], kl_ref[b] = split(dot4_nt(left, m))
        return carry

    lax.fori_loop(0, blocks // TOGETHER, group_of, 0)
    lane = lax.broadcasted_iota(jnp.int32, (rows, 128), 1)

    def step(b, carry):
        offset = offsets[b]
        tile = jnp.minimum(offset // 128, tiles - 3)
        shift = offset - tile * 128
        v0, v1, v2 = o_ref[tile], o_ref[tile + 1], o_ref[tile + 2]
        left = (128 - shift) & 127
        r0 = pltpu.roll(v0, left, 1)
        r1 = pltpu.roll(v1, left, 1)
        r2 = pltpu.roll(v2, left, 1)
        inside = lane < 128 - shift
        window = jnp.concatenate([jnp.where(inside, r0, r1), jnp.where(inside, r1, r2)], axis=1)
        high = window.astype(BF16).astype(F32)
        both = jnp.concatenate([high, window - high], axis=0).astype(BF16)
        change = dg(both, kh_ref[b]) + dg(both, kl_ref[b])
        change = change[:rows] + change[rows:]
        right = shift & 127
        q0 = pltpu.roll(change[:, :128], right, 1)
        q1 = pltpu.roll(change[:, 128:], right, 1)
        after = lane >= shift
        o_ref[tile] = v0 - jnp.where(after, q0, 0.0)
        o_ref[tile + 1] = v1 - jnp.where(after, q1, q0)
        o_ref[tile + 2] = v2 - jnp.where(after, 0.0, q1)
        return carry

    lax.fori_loop(0, blocks, step, 0)


def share_kernel(g_ref, o_ref):
    sums = [g_ref[k] for k in range(4)]
    for s in range(4, g_ref.shape[0]):
        sums[s % 4] = sums[s % 4] + g_ref[s]
    total = (sums[0] + sums[1]) + (sums[2] + sums[3])
    o_ref[...] = jnp.broadcast_to(total[None], o_ref.shape)


def vmem():
    return pl.BlockSpec(memory_space=pltpu.VMEM)


def smem():
    return pl.BlockSpec(memory_space=pltpu.SMEM)


def params():
    return pltpu.CompilerParams(vmem_limit_bytes=VMEM_LIMIT)


def hbm():
    return pl.BlockSpec(memory_space=pltpu.HBM)


def invert(reflectors, lengths):
    blocks, extent, width = reflectors.shape
    shape = jax.ShapeDtypeStruct((blocks, width, width), BF16)
    return pl.pallas_call(
        invert_kernel,
        out_shape=[shape, shape],
        in_specs=[smem(), vmem()],
        out_specs=[vmem()] * 2,
        compiler_params=params(),
        cost_estimate=pl.CostEstimate(flops=10 * 10**9, bytes_accessed=5 << 20, transcendentals=0),
        name="invert",
    )(lengths, reflectors)


def chase(tiles, reflectors, offsets, lengths, fh, fl):
    blocks, extent, width = reflectors.shape
    return pl.pallas_call(
        chase_kernel,
        out_shape=jax.ShapeDtypeStruct(tiles.shape, F32),
        in_specs=[smem(), smem()] + [vmem()] * 4,
        out_specs=vmem(),
        scratch_shapes=[pltpu.VMEM((blocks, extent, extent), BF16)] * 2,
        compiler_params=params(),
        cost_estimate=pl.CostEstimate(flops=10 * 10**9, bytes_accessed=7 << 20, transcendentals=0),
        name="chase",
    )(offsets, lengths, tiles, reflectors, fh, fl)


def share(parts):
    return pl.pallas_call(
        share_kernel,
        out_shape=jax.ShapeDtypeStruct(parts.shape, F32),
        in_specs=[vmem()],
        out_specs=vmem(),
        compiler_params=params(),
        cost_estimate=pl.CostEstimate(flops=10**6, bytes_accessed=3 << 20, transcendentals=0),
        name="share",
    )(parts)


WIDE = 256
ORDER = ((0, 1, 2, 3), (2, 0, 3, 1))
LOCAL = ((0, 1), (1, 2), (2, 3), (1, 1), (2, 2))
MADE = [(ORDER[c][i], ORDER[c][j]) for c in range(2) for (i, j) in LOCAL]
UPPER = [(i, j) for i in range(4) for j in range(i + 1, 4)]


def gram_kernel(core, v_ref, *refs):
    c = core[0]
    g_ref = refs[-1]
    order = (2 * c, 1 - c, 2 + c, 3 - 2 * c)
    halves = [split(v_ref[:, pl.ds(pl.multiple_of(o * WIDE, WIDE), WIDE)]) for o in order]
    for at, (i, j) in enumerate(LOCAL):
        block = dot3(halves[i], halves[j], TN)
        for h in range(2):
            rows = pl.ds((at * 2 + h) * WIDE, WIDE)
            part = block[:, h * 128 : (h + 1) * 128]
            g_ref[rows, :] = part + refs[0][rows, :] if len(refs) == 2 else part


def gram(core, panels, *before):
    return pl.pallas_call(
        gram_kernel,
        out_shape=jax.ShapeDtypeStruct((len(LOCAL) * 2 * WIDE, 128), F32),
        in_specs=[smem(), vmem()] + [vmem()] * len(before),
        out_specs=vmem(),
        compiler_params=params(),
        cost_estimate=pl.CostEstimate(flops=10**9, bytes_accessed=4 << 20, transcendentals=0),
        name="gram",
    )(core, panels, *before)


def factor_kernel(core, own_ref, other_ref, th_ref, tl_ref, sh_ref, sl_ref):
    first = core[0] == 0

    def block(c, at):
        halves = []
        for h in range(2):
            rows = pl.ds((at * 2 + h) * WIDE, WIDE)
            mine, theirs = own_ref[rows, :], other_ref[rows, :]
            halves.append(jnp.where(first, mine, theirs) if c == 0 else jnp.where(first, theirs, mine))
        return jnp.concatenate(halves, axis=1)

    diagonals = [None] * 4
    for at, (i, j) in enumerate(MADE):
        value = block(at // len(LOCAL), at % len(LOCAL))
        if i == j:
            diagonals[i] = value
        else:
            high, low = split(value.T if i < j else value)
            slot = UPPER.index((min(i, j), max(i, j)))
            sh_ref[slot] = high
            sl_ref[slot] = low
    small = []
    for d in diagonals:
        small.extend([d[:128, :128], d[128:, 128:]])
    inverses = inverse_of_half(small[:4]) + inverse_of_half(small[4:])
    for p, d in enumerate(diagonals):
        a, c = inverses[2 * p], inverses[2 * p + 1]
        corner = -dot4(split(dot4(split(a), split(d[:128, 128:]))), split(c))
        whole = jnp.concatenate(
            [
                jnp.concatenate([a.T, jnp.zeros((128, 128), F32)], axis=1),
                jnp.concatenate([corner.T, c.T], axis=1),
            ],
            axis=0,
        )
        high, low = split(whole)
        th_ref[p] = high
        tl_ref[p] = low


def factor(core, own, other):
    shapes = [(4, WIDE, WIDE)] * 2 + [(6, WIDE, WIDE)] * 2
    return pl.pallas_call(
        factor_kernel,
        out_shape=[jax.ShapeDtypeStruct(s, BF16) for s in shapes],
        in_specs=[smem(), vmem(), vmem()],
        out_specs=[vmem()] * 4,
        compiler_params=params(),
        cost_estimate=pl.CostEstimate(flops=8 * 10**9, bytes_accessed=5 << 20, transcendentals=0),
        name="factor",
    )(core, own, other)


def rows_of(ref, j):
    stride = ref.shape[0] // 64
    return jnp.concatenate([ref[pl.ds(j * 4 + r, 64, stride=stride), :] for r in range(4)], axis=0)


def project_kernel(core, e_ref, own_ref, other_ref, p_ref):
    c = core[0]
    sides = [
        (split(jnp.concatenate([rows_of(e_ref, first + k) for k in range(4)], axis=1)), v_ref)
        for v_ref, first in ((own_ref, 4 * c), (other_ref, 4 - 4 * c))
    ]
    for n in range(4):
        total = sum(dot3(left, split(v_ref[:, n * WIDE : (n + 1) * WIDE])) for left, v_ref in sides)
        for h in range(2):
            for r in range(4):
                p_ref[pl.ds((2 * n + h) * 4 + r, 64, stride=32), :] = total[
                    r * 64 : (r + 1) * 64, h * 128 : (h + 1) * 128
                ]


def project(core, e, own, other):
    return pl.pallas_call(
        project_kernel,
        out_shape=jax.ShapeDtypeStruct((2048, 128), F32),
        in_specs=[smem(), vmem(), vmem(), vmem()],
        out_specs=vmem(),
        compiler_params=params(),
        cost_estimate=pl.CostEstimate(flops=2 * 10**9, bytes_accessed=6 << 20, transcendentals=0),
        name="project",
    )(core, e, own, other)


def solve_kernel(p_ref, th_ref, tl_ref, sh_ref, sl_ref, w_ref):
    sums = [p_ref[k] for k in range(4)]
    for s in range(4, p_ref.shape[0]):
        sums[s % 4] = sums[s % 4] + p_ref[s]
    total = (sums[0] + sums[1]) + (sums[2] + sums[3])
    rest = [
        jnp.concatenate([total[8 * p : 8 * p + 4], total[8 * p + 4 : 8 * p + 8]], axis=1)
        for p in range(4)
    ]

    def times(a, bh, bl):
        high = a.astype(BF16).astype(F32)
        both = jnp.concatenate([high, a - high], axis=0).astype(BF16)
        product = dg(both, bh) + dg(both, bl)
        return product[:4] + product[4:]

    pieces = [None] * 4
    for q in range(3, -1, -1):
        solved = times(rest[q], th_ref[q], tl_ref[q])
        pieces[q] = jnp.concatenate([solved[:, :128], solved[:, 128:]], axis=0)
        for p in range(q):
            at = UPPER.index((p, q))
            rest[p] = rest[p] - times(solved, sh_ref[at], sl_ref[at])
    result = jnp.concatenate(pieces, axis=0)
    w_ref[...] = jnp.broadcast_to(result[None], w_ref.shape)


def solve(p, factors):
    return pl.pallas_call(
        solve_kernel,
        out_shape=jax.ShapeDtypeStruct(p.shape, F32),
        in_specs=[vmem()] * 5,
        out_specs=vmem(),
        compiler_params=params(),
        cost_estimate=pl.CostEstimate(flops=10**9, bytes_accessed=4 << 20, transcendentals=0),
        name="solve",
    )(p, *factors)


def update_kernel(core, e_ref, w_ref, own_ref, other_ref, o_ref):
    c = core[0]
    left = split(jnp.concatenate([rows_of(w_ref, n) for n in range(8)], axis=1))
    for v_ref, first in ((own_ref, 4 * c), (other_ref, 4 - 4 * c)):
        for k in range(2):
            change = dot3(left, split(v_ref[k * WIDE : (k + 1) * WIDE, :]), NT)
            for h in range(2):
                j = first + 2 * k + h
                for r in range(4):
                    before = e_ref[pl.ds(j * 4 + r, 64, stride=e_ref.shape[0] // 64), :]
                    part = change[r * 64 : (r + 1) * 64, h * 128 : (h + 1) * 128]
                    o_ref[pl.ds(j * 4 + r, 64, stride=32), :] = before - part


def update(core, e, w, own, other):
    return pl.pallas_call(
        update_kernel,
        out_shape=jax.ShapeDtypeStruct((2048, 128), F32),
        in_specs=[smem(), vmem(), vmem(), vmem(), vmem()],
        out_specs=vmem(),
        compiler_params=params(),
        cost_estimate=pl.CostEstimate(flops=2 * 10**9, bytes_accessed=7 << 20, transcendentals=0),
        name="update",
    )(core, e, w, own, other)


def to_chips(a):
    return lax.all_to_all(a, CHIPS, split_axis=0, concat_axis=0, tiled=True)


def swap_cores(a):
    return lax.ppermute(a, "c", [(0, 1), (1, 0)])


def body(eigvecs, reflectors, offsets, lengths, panels):
    core = lax.axis_index("c").astype(jnp.int32).reshape(1)
    other = swap_cores(panels)
    parts = to_chips(gram(core, other, gram(core, panels)).reshape(64, 40, 128))
    factors = invert(reflectors, lengths)
    copies = share(parts)
    copies, factors = lax.optimization_barrier((copies, factors))
    half = to_chips(copies).reshape(2560, 128)
    tiles = eigvecs.reshape(4, 512, 128).transpose(1, 0, 2)
    chased = chase(tiles, reflectors, offsets, lengths, *factors)
    chased, half = lax.optimization_barrier((chased, half))
    mine = to_chips(chased.reshape(64, 32, 128)).reshape(2048, 128)
    solvers = factor(core, half, swap_cores(half))
    mine, solvers = lax.optimization_barrier((mine, solvers))
    projected = to_chips(project(core, mine, panels, other).reshape(64, 32, 128))
    weights = to_chips(solve(projected, solvers)).reshape(2048, 128)
    result = to_chips(update(core, mine, weights, panels, other).reshape(64, 32, 128))
    return result.reshape(64, 8, 4, 128).transpose(2, 0, 1, 3).reshape(4, 65536)


def solution(mesh):
    fine = Mesh(mesh.devices.reshape(2, 4, 2, 4, 2), AXES)
    return jax.shard_map(
        body,
        mesh=fine,
        in_specs=(P(AXES, None), P(), P(), P(), P(AXES, None)),
        out_specs=P(AXES, None),
        check_vma=False,
    )
```

```python
import jax
import jax.numpy as jnp
from jax import lax
from jax.experimental import pallas as pl
from jax.experimental.pallas import tpu as pltpu
from jax.sharding import Mesh, PartitionSpec as P

F32 = jnp.float32
BF16 = jnp.bfloat16
AXES = ("yh", "x", "yl", "z", "c")
CHIPS = ("yh", "x", "yl", "z")
VMEM_LIMIT = 20 * 1024 * 1024

NN = (((1,), (0,)), ((), ()))
NT = (((1,), (1,)), ((), ()))
TN = (((0,), (0,)), ((), ()))


def dg(a, b, dims=NN):
    return lax.dot_general(a, b, dims, preferred_element_type=F32)


def split(a):
    high = a.astype(BF16)
    low = (a - high.astype(F32)).astype(BF16)
    return high, low


def dot3(a, b, dims=NN):
    (ah, al), (bh, bl) = a, b
    return dg(ah, bh, dims) + (dg(ah, bl, dims) + dg(al, bh, dims))


def dot4(a, b):
    n = b[0].shape[1]
    right = jnp.concatenate(b, axis=1)
    both = dg(jnp.concatenate(a, axis=1), jnp.concatenate([right, right], axis=0))
    return both[:, :n] + both[:, n:]


def dot4_nt(a, b):
    n = b[0].shape[0]
    right = jnp.concatenate(b, axis=0)
    both = dg(jnp.concatenate(a, axis=1), jnp.concatenate([right, right], axis=1), NT)
    return both[:, :n] + both[:, n:]


def iotas(n):
    return (
        lax.broadcasted_iota(jnp.int32, (n, n), 0),
        lax.broadcasted_iota(jnp.int32, (n, n), 1),
    )


def inverse_of_half(grams):
    n = grams[0].shape[0]
    row, col = iotas(n)
    eye = (row == col).astype(F32)
    upper = row < col
    inverses, strict, scale = [], [], []
    for gram in grams:
        diagonal = gram * (0.5 * eye)
        by_row = jnp.sum(diagonal, axis=1, keepdims=True)
        by_col = jnp.sum(diagonal, axis=0, keepdims=True)
        nil = jnp.where(upper, gram / by_row, 0.0)
        strict.append(nil)
        scale.append(1.0 / by_col)
        first = ((row ^ col) == 1) & ((row & 1) == 0)
        inverses.append(eye - jnp.where(first, nil, 0.0))
    size = 2
    while size < n:
        corner = ((row // (2 * size)) == (col // (2 * size))) & ((row & size) == 0) & ((col & size) != 0)
        halves = [split(x) for x in inverses]
        corners = [split(jnp.where(corner, nil, 0.0)) for nil in strict]
        middles = [split(dot4(x, m)) for x, m in zip(halves, corners)]
        inverses = [x - dot4(y, h) for x, y, h in zip(inverses, middles, halves)]
        size *= 2
    return [x * s for x, s in zip(inverses, scale)]


TOGETHER = 8


def masked_block(lengths, m_ref, b):
    row = lax.broadcasted_iota(jnp.int32, m_ref.shape[1:], 0)
    return split(jnp.where(row < lengths[b], m_ref[b], 0.0))


def gram_of(m):
    width = m[0].shape[1]
    both = dg(m[0], jnp.concatenate(m, axis=1), TN)
    return both[:, :width] + both[:, width:] + dg(m[1], m[0], TN)


def chase_kernel(offsets, lengths, e_ref, m_ref, o_ref, kh_ref, kl_ref):
    blocks = m_ref.shape[0]
    tiles, rows = e_ref.shape[0], e_ref.shape[1]
    o_ref[...] = e_ref[...]

    def group_of(group, carry):
        at = [group * TOGETHER + u for u in range(TOGETHER)]
        masked = [masked_block(lengths, m_ref, b) for b in at]
        factors = [split(f) for f in inverse_of_half([gram_of(m) for m in masked])]
        lefts = [split(dot4_nt(m, f)) for m, f in zip(masked, factors)]
        for left, m, b in zip(lefts, masked, at):
            kh_ref[b], kl_ref[b] = split(dot4_nt(left, m))
        return carry

    lax.fori_loop(0, blocks // TOGETHER, group_of, 0)
    lane = lax.broadcasted_iota(jnp.int32, (rows, 128), 1)

    def step(b, carry):
        offset = offsets[b]
        tile = jnp.minimum(offset // 128, tiles - 3)
        shift = offset - tile * 128
        v0, v1, v2 = o_ref[tile], o_ref[tile + 1], o_ref[tile + 2]
        left = (128 - shift) & 127
        r0 = pltpu.roll(v0, left, 1)
        r1 = pltpu.roll(v1, left, 1)
        r2 = pltpu.roll(v2, left, 1)
        inside = lane < 128 - shift
        window = jnp.concatenate([jnp.where(inside, r0, r1), jnp.where(inside, r1, r2)], axis=1)
        high = window.astype(BF16).astype(F32)
        both = jnp.concatenate([high, window - high], axis=0).astype(BF16)
        change = dg(both, kh_ref[b]) + dg(both, kl_ref[b])
        change = change[:rows] + change[rows:]
        right = shift & 127
        q0 = pltpu.roll(change[:, :128], right, 1)
        q1 = pltpu.roll(change[:, 128:], right, 1)
        after = lane >= shift
        o_ref[tile] = v0 - jnp.where(after, q0, 0.0)
        o_ref[tile + 1] = v1 - jnp.where(after, q1, q0)
        o_ref[tile + 2] = v2 - jnp.where(after, 0.0, q1)
        return carry

    lax.fori_loop(0, blocks, step, 0)


def share_kernel(g_ref, o_ref):
    sums = [g_ref[k] for k in range(4)]
    for s in range(4, g_ref.shape[0]):
        sums[s % 4] = sums[s % 4] + g_ref[s]
    total = (sums[0] + sums[1]) + (sums[2] + sums[3])
    o_ref[...] = jnp.broadcast_to(total[None], o_ref.shape)


def vmem():
    return pl.BlockSpec(memory_space=pltpu.VMEM)


def smem():
    return pl.BlockSpec(memory_space=pltpu.SMEM)


def params():
    return pltpu.CompilerParams(vmem_limit_bytes=VMEM_LIMIT)


def hbm():
    return pl.BlockSpec(memory_space=pltpu.HBM)


def chase(tiles, reflectors, offsets, lengths):
    blocks, extent, width = reflectors.shape
    return pl.pallas_call(
        chase_kernel,
        out_shape=jax.ShapeDtypeStruct(tiles.shape, F32),
        in_specs=[smem(), smem()] + [vmem()] * 2,
        out_specs=vmem(),
        scratch_shapes=[pltpu.VMEM((blocks, extent, extent), BF16)] * 2,
        compiler_params=params(),
        cost_estimate=pl.CostEstimate(flops=20 * 10**9, bytes_accessed=7 << 20, transcendentals=0),
        name="chase",
    )(offsets, lengths, tiles, reflectors)


def share(parts):
    return pl.pallas_call(
        share_kernel,
        out_shape=jax.ShapeDtypeStruct((8,) + parts.shape[1:], F32),
        in_specs=[vmem()],
        out_specs=vmem(),
        compiler_params=params(),
        cost_estimate=pl.CostEstimate(flops=10**6, bytes_accessed=3 << 20, transcendentals=0),
        name="share",
    )(parts)


WIDE = 256
ORDER = ((0, 1, 2, 3), (2, 0, 3, 1))
LOCAL = ((0, 1), (1, 2), (2, 3), (1, 1), (2, 2))
MADE = [(ORDER[c][i], ORDER[c][j]) for c in range(2) for (i, j) in LOCAL]


def gram_kernel(core, v_ref, *refs):
    c = core[0]
    g_ref = refs[-1]
    order = (2 * c, 1 - c, 2 + c, 3 - 2 * c)
    halves = [split(v_ref[:, pl.ds(pl.multiple_of(o * WIDE, WIDE), WIDE)]) for o in order]
    for at, (i, j) in enumerate(LOCAL):
        block = dot3(halves[i], halves[j], TN)
        for h in range(2):
            rows = pl.ds((at * 2 + h) * WIDE, WIDE)
            part = block[:, h * 128 : (h + 1) * 128]
            g_ref[rows, :] = part + refs[0][rows, :] if len(refs) == 2 else part


def gram(core, panels, *before):
    return pl.pallas_call(
        gram_kernel,
        out_shape=jax.ShapeDtypeStruct((len(LOCAL) * 2 * WIDE, 128), F32),
        in_specs=[smem(), vmem()] + [vmem()] * len(before),
        out_specs=vmem(),
        compiler_params=params(),
        cost_estimate=pl.CostEstimate(flops=10**9, bytes_accessed=4 << 20, transcendentals=0),
        name="gram",
    )(core, panels, *before)


def rows_between(ref, half, start, stop):
    pieces = []
    while start < stop:
        group, within = divmod(start, 160)
        count = min(160 - within, stop - start)
        pieces.append(ref[pl.ds(group * 320 + half * 160 + within, count), :])
        start += count
    return jnp.concatenate(pieces, axis=0)


def gram_block(ref, at):
    half, local = divmod(at, len(LOCAL))
    return jnp.concatenate(
        [
            rows_between(ref, half, (2 * local + h) * WIDE, (2 * local + h + 1) * WIDE)
            for h in range(2)
        ],
        axis=1,
    )


def solve_kernel(g_ref, p_ref, w_ref):
    diagonals, others = [None] * 4, {}
    for at, (i, j) in enumerate(MADE):
        value = gram_block(g_ref, at)
        if i == j:
            diagonals[i] = value
        else:
            others[min(i, j), max(i, j)] = split(value.T if i < j else value)
    small = []
    for d in diagonals:
        small.extend([d[:128, :128], d[128:, 128:]])
    inverses = inverse_of_half(small)
    transposed = []
    for p, d in enumerate(diagonals):
        a, c = inverses[2 * p], inverses[2 * p + 1]
        corner = -dot4(split(dot4(split(a), split(d[:128, 128:]))), split(c))
        top = jnp.concatenate([a.T, jnp.zeros((128, 128), F32)], axis=1)
        transposed.append(split(jnp.concatenate([top, jnp.concatenate([corner.T, c.T], axis=1)], axis=0)))

    sums = [p_ref[k] for k in range(4)]
    for s in range(4, p_ref.shape[0]):
        sums[s % 4] = sums[s % 4] + p_ref[s]
    total = (sums[0] + sums[1]) + (sums[2] + sums[3])
    rest = [
        jnp.concatenate([total[8 * p : 8 * p + 4], total[8 * p + 4 : 8 * p + 8]], axis=1)
        for p in range(4)
    ]

    def times(a, b):
        high = a.astype(BF16).astype(F32)
        both = jnp.concatenate([high, a - high], axis=0).astype(BF16)
        product = dg(both, b[0]) + dg(both, b[1])
        return product[:4] + product[4:]

    pieces = [None] * 4
    for q in range(3, -1, -1):
        solved = times(rest[q], transposed[q])
        pieces[q] = jnp.concatenate([solved[:, :128], solved[:, 128:]], axis=0)
        for p in range(q):
            rest[p] = rest[p] - times(solved, others[p, q])
    result = jnp.concatenate(pieces, axis=0)
    w_ref[...] = jnp.broadcast_to(result[None], w_ref.shape)


def solve(gathered, p):
    return pl.pallas_call(
        solve_kernel,
        out_shape=jax.ShapeDtypeStruct(p.shape, F32),
        in_specs=[vmem()] * 2,
        out_specs=vmem(),
        compiler_params=params(),
        cost_estimate=pl.CostEstimate(flops=4 * 10**9, bytes_accessed=5 << 20, transcendentals=0),
        name="solve",
    )(gathered, p)


def rows_of(ref, j):
    stride = ref.shape[0] // 64
    return jnp.concatenate([ref[pl.ds(j * 4 + r, 64, stride=stride), :] for r in range(4)], axis=0)


def project_kernel(core, e_ref, own_ref, other_ref, p_ref):
    c = core[0]
    sides = [
        (split(jnp.concatenate([rows_of(e_ref, first + k) for k in range(4)], axis=1)), v_ref)
        for v_ref, first in ((own_ref, 4 * c), (other_ref, 4 - 4 * c))
    ]
    for n in range(4):
        total = sum(dot3(left, split(v_ref[:, n * WIDE : (n + 1) * WIDE])) for left, v_ref in sides)
        for h in range(2):
            for r in range(4):
                p_ref[pl.ds((2 * n + h) * 4 + r, 64, stride=32), :] = total[
                    r * 64 : (r + 1) * 64, h * 128 : (h + 1) * 128
                ]


def project(core, e, own, other):
    return pl.pallas_call(
        project_kernel,
        out_shape=jax.ShapeDtypeStruct((2048, 128), F32),
        in_specs=[smem(), vmem(), vmem(), vmem()],
        out_specs=vmem(),
        compiler_params=params(),
        cost_estimate=pl.CostEstimate(flops=2 * 10**9, bytes_accessed=6 << 20, transcendentals=0),
        name="project",
    )(core, e, own, other)


def update_kernel(core, e_ref, w_ref, own_ref, other_ref, o_ref):
    c = core[0]
    left = split(jnp.concatenate([rows_of(w_ref, n) for n in range(8)], axis=1))
    for v_ref, first in ((own_ref, 4 * c), (other_ref, 4 - 4 * c)):
        for k in range(2):
            change = dot3(left, split(v_ref[k * WIDE : (k + 1) * WIDE, :]), NT)
            for h in range(2):
                j = first + 2 * k + h
                for r in range(4):
                    before = e_ref[pl.ds(j * 4 + r, 64, stride=e_ref.shape[0] // 64), :]
                    part = change[r * 64 : (r + 1) * 64, h * 128 : (h + 1) * 128]
                    o_ref[pl.ds(j * 4 + r, 64, stride=32), :] = before - part


def update(core, e, w, own, other):
    return pl.pallas_call(
        update_kernel,
        out_shape=jax.ShapeDtypeStruct((2048, 128), F32),
        in_specs=[smem(), vmem(), vmem(), vmem(), vmem()],
        out_specs=vmem(),
        compiler_params=params(),
        cost_estimate=pl.CostEstimate(flops=2 * 10**9, bytes_accessed=7 << 20, transcendentals=0),
        name="update",
    )(core, e, w, own, other)


def to_chips(a):
    return lax.all_to_all(a, CHIPS, split_axis=0, concat_axis=0, tiled=True)


def swap_cores(a):
    return lax.ppermute(a, "c", [(0, 1), (1, 0)])


def body(eigvecs, reflectors, offsets, lengths, panels):
    core = lax.axis_index("c").astype(jnp.int32).reshape(1)
    other = swap_cores(panels)
    parts = gram(core, other, gram(core, panels)).reshape(64, 40, 128)
    parts = lax.all_to_all(parts, ("x", "z", "yh", "yl"), split_axis=0, concat_axis=0, tiled=True)
    tiles = eigvecs.reshape(4, 512, 128).transpose(1, 0, 2)
    chased = chase(tiles, reflectors, offsets, lengths)
    parts, chased = lax.optimization_barrier((parts, chased))
    shares = lax.all_to_all(share(parts), ("c", "yh", "yl"), split_axis=0, concat_axis=0, tiled=True)
    shares, chased = lax.optimization_barrier((shares, chased))
    gathered = lax.all_gather(shares.reshape(320, 128), ("x", "z"), axis=0, tiled=True)
    mine = to_chips(chased.reshape(64, 32, 128)).reshape(2048, 128)
    projected = to_chips(project(core, mine, panels, other).reshape(64, 32, 128))
    weights = to_chips(solve(gathered, projected)).reshape(2048, 128)
    result = to_chips(update(core, mine, weights, panels, other).reshape(64, 32, 128))
    return result.reshape(64, 8, 4, 128).transpose(2, 0, 1, 3).reshape(4, 65536)


def solution(mesh):
    fine = Mesh(mesh.devices.reshape(2, 4, 2, 4, 2), AXES)
    return jax.shard_map(
        body,
        mesh=fine,
        in_specs=(P(AXES, None), P(), P(), P(), P(AXES, None)),
        out_specs=P(AXES, None),
        check_vma=False,
    )
```

```python
import jax
import jax.numpy as jnp
from jax import lax
from jax.experimental import pallas as pl
from jax.experimental.pallas import tpu as pltpu
from jax.sharding import Mesh, PartitionSpec as P

F32 = jnp.float32
BF16 = jnp.bfloat16
AXES = ("yh", "x", "yl", "z", "c")
CHIPS = ("yh", "x", "yl", "z")
VMEM_LIMIT = 20 * 1024 * 1024

NN = (((1,), (0,)), ((), ()))
NT = (((1,), (1,)), ((), ()))
TN = (((0,), (0,)), ((), ()))


def dg(a, b, dims=NN):
    return lax.dot_general(a, b, dims, preferred_element_type=F32)


def split(a):
    high = a.astype(BF16)
    low = (a - high.astype(F32)).astype(BF16)
    return high, low


def dot3(a, b, dims=NN):
    (ah, al), (bh, bl) = a, b
    return dg(ah, bh, dims) + (dg(ah, bl, dims) + dg(al, bh, dims))


def dot4(a, b):
    n = b[0].shape[1]
    right = jnp.concatenate(b, axis=1)
    both = dg(jnp.concatenate(a, axis=1), jnp.concatenate([right, right], axis=0))
    return both[:, :n] + both[:, n:]


def dot4_nt(a, b):
    n = b[0].shape[0]
    right = jnp.concatenate(b, axis=0)
    both = dg(jnp.concatenate(a, axis=1), jnp.concatenate([right, right], axis=1), NT)
    return both[:, :n] + both[:, n:]


def iotas(n):
    return (
        lax.broadcasted_iota(jnp.int32, (n, n), 0),
        lax.broadcasted_iota(jnp.int32, (n, n), 1),
    )


def inverse_of_half(grams):
    n = grams[0].shape[0]
    row, col = iotas(n)
    eye = (row == col).astype(F32)
    upper = row < col
    inverses, strict, scale = [], [], []
    for gram in grams:
        diagonal = gram * (0.5 * eye)
        by_row = jnp.sum(diagonal, axis=1, keepdims=True)
        by_col = jnp.sum(diagonal, axis=0, keepdims=True)
        nil = jnp.where(upper, gram / by_row, 0.0)
        strict.append(nil)
        scale.append(1.0 / by_col)
        first = ((row ^ col) == 1) & ((row & 1) == 0)
        inverses.append(eye - jnp.where(first, nil, 0.0))
    size = 2
    while size < n:
        corner = ((row // (2 * size)) == (col // (2 * size))) & ((row & size) == 0) & ((col & size) != 0)
        halves = [split(x) for x in inverses]
        corners = [split(jnp.where(corner, nil, 0.0)) for nil in strict]
        middles = [split(dot4(x, m)) for x, m in zip(halves, corners)]
        inverses = [x - dot4(y, h) for x, y, h in zip(inverses, middles, halves)]
        size *= 2
    return [x * s for x, s in zip(inverses, scale)]


TOGETHER = 8


def masked_block(lengths, m_ref, b):
    row = lax.broadcasted_iota(jnp.int32, m_ref.shape[1:], 0)
    return split(jnp.where(row < lengths[b], m_ref[b], 0.0))


def gram_of(m):
    width = m[0].shape[1]
    both = dg(m[0], jnp.concatenate(m, axis=1), TN)
    return both[:, :width] + both[:, width:] + dg(m[1], m[0], TN)


def chase_kernel(offsets, lengths, e_ref, m_ref, o_ref, kh_ref, kl_ref):
    blocks = m_ref.shape[0]
    tiles, rows = e_ref.shape[0], e_ref.shape[1]
    o_ref[...] = e_ref[...]

    def group_of(group, carry):
        at = [group * TOGETHER + u for u in range(TOGETHER)]
        masked = [masked_block(lengths, m_ref, b) for b in at]
        factors = [split(f) for f in inverse_of_half([gram_of(m) for m in masked])]
        lefts = [split(dot4_nt(m, f)) for m, f in zip(masked, factors)]
        for left, m, b in zip(lefts, masked, at):
            kh_ref[b], kl_ref[b] = split(dot4_nt(left, m))
        return carry

    lax.fori_loop(0, blocks // TOGETHER, group_of, 0)
    lane = lax.broadcasted_iota(jnp.int32, (rows, 128), 1)

    def step(b, carry):
        offset = offsets[b]
        tile = jnp.minimum(offset // 128, tiles - 3)
        shift = offset - tile * 128
        v0, v1, v2 = o_ref[tile], o_ref[tile + 1], o_ref[tile + 2]
        left = (128 - shift) & 127
        r0 = pltpu.roll(v0, left, 1)
        r1 = pltpu.roll(v1, left, 1)
        r2 = pltpu.roll(v2, left, 1)
        inside = lane < 128 - shift
        window = jnp.concatenate([jnp.where(inside, r0, r1), jnp.where(inside, r1, r2)], axis=1)
        high = window.astype(BF16).astype(F32)
        both = jnp.concatenate([high, window - high], axis=0).astype(BF16)
        change = dg(both, kh_ref[b]) + dg(both, kl_ref[b])
        change = change[:rows] + change[rows:]
        right = shift & 127
        q0 = pltpu.roll(change[:, :128], right, 1)
        q1 = pltpu.roll(change[:, 128:], right, 1)
        after = lane >= shift
        o_ref[tile] = v0 - jnp.where(after, q0, 0.0)
        o_ref[tile + 1] = v1 - jnp.where(after, q1, q0)
        o_ref[tile + 2] = v2 - jnp.where(after, 0.0, q1)
        return carry

    lax.fori_loop(0, blocks, step, 0)


def share_kernel(e_ref, g_ref, o_ref):
    sums = [g_ref[k] for k in range(4)]
    for s in range(4, g_ref.shape[0]):
        sums[s % 4] = sums[s % 4] + g_ref[s]
    total = (sums[0] + sums[1]) + (sums[2] + sums[3])
    for s in range(g_ref.shape[0]):
        o_ref[s, :32, :] = e_ref[s]
        o_ref[s, 32:, :] = total


def vmem():
    return pl.BlockSpec(memory_space=pltpu.VMEM)


def smem():
    return pl.BlockSpec(memory_space=pltpu.SMEM)


def params():
    return pltpu.CompilerParams(vmem_limit_bytes=VMEM_LIMIT)


def hbm():
    return pl.BlockSpec(memory_space=pltpu.HBM)


def chase(tiles, reflectors, offsets, lengths):
    blocks, extent, width = reflectors.shape
    return pl.pallas_call(
        chase_kernel,
        out_shape=jax.ShapeDtypeStruct(tiles.shape, F32),
        in_specs=[smem(), smem()] + [vmem()] * 2,
        out_specs=vmem(),
        scratch_shapes=[pltpu.VMEM((blocks, extent, extent), BF16)] * 2,
        compiler_params=params(),
        cost_estimate=pl.CostEstimate(flops=20 * 10**9, bytes_accessed=7 << 20, transcendentals=0),
        name="chase",
    )(offsets, lengths, tiles, reflectors)


def share(chased, parts):
    return pl.pallas_call(
        share_kernel,
        out_shape=jax.ShapeDtypeStruct((64, 72, 128), F32),
        in_specs=[vmem()] * 2,
        out_specs=vmem(),
        compiler_params=params(),
        cost_estimate=pl.CostEstimate(flops=10**6, bytes_accessed=5 << 20, transcendentals=0),
        name="share",
    )(chased, parts)


WIDE = 256
ORDER = ((0, 1, 2, 3), (2, 0, 3, 1))
LOCAL = ((0, 1), (1, 2), (2, 3), (1, 1), (2, 2))
MADE = [(ORDER[c][i], ORDER[c][j]) for c in range(2) for (i, j) in LOCAL]


def gram_kernel(core, v_ref, *refs):
    c = core[0]
    g_ref = refs[-1]
    order = (2 * c, 1 - c, 2 + c, 3 - 2 * c)
    halves = [split(v_ref[:, pl.ds(pl.multiple_of(o * WIDE, WIDE), WIDE)]) for o in order]
    for at, (i, j) in enumerate(LOCAL):
        block = dot3(halves[i], halves[j], TN)
        for h in range(2):
            rows = pl.ds((at * 2 + h) * WIDE, WIDE)
            part = block[:, h * 128 : (h + 1) * 128]
            g_ref[rows, :] = part + refs[0][rows, :] if len(refs) == 2 else part


def gram(core, panels, *before):
    return pl.pallas_call(
        gram_kernel,
        out_shape=jax.ShapeDtypeStruct((len(LOCAL) * 2 * WIDE, 128), F32),
        in_specs=[smem(), vmem()] + [vmem()] * len(before),
        out_specs=vmem(),
        compiler_params=params(),
        cost_estimate=pl.CostEstimate(flops=10**9, bytes_accessed=4 << 20, transcendentals=0),
        name="gram",
    )(core, panels, *before)


def gram_rows(ref, start, stop):
    pieces = []
    while start < stop:
        chip, within = divmod(start, 40)
        count = min(40 - within, stop - start)
        pieces.append(ref[pl.ds(chip * 72 + 32 + within, count), :])
        start += count
    return jnp.concatenate(pieces, axis=0)


def gram_block(ref, local):
    return jnp.concatenate(
        [gram_rows(ref, (2 * local + h) * WIDE, (2 * local + h + 1) * WIDE) for h in range(2)], axis=1
    )


def solve_kernel(core, own_ref, other_ref, p_ref, w_ref):
    diagonals, others = [None] * 4, {}
    first = core[0] == 0
    pairs = [(gram_block(own_ref, k), gram_block(other_ref, k)) for k in range(len(LOCAL))]
    values = [jnp.where(first, a, b) for a, b in pairs] + [jnp.where(first, b, a) for a, b in pairs]
    for value, (i, j) in zip(values, MADE):
        if i == j:
            diagonals[i] = value
        else:
            others[min(i, j), max(i, j)] = split(value.T if i < j else value)
    small = []
    for d in diagonals:
        small.extend([d[:128, :128], d[128:, 128:]])
    inverses = inverse_of_half(small)
    transposed = []
    for p, d in enumerate(diagonals):
        a, c = inverses[2 * p], inverses[2 * p + 1]
        corner = -dot4(split(dot4(split(a), split(d[:128, 128:]))), split(c))
        top = jnp.concatenate([a.T, jnp.zeros((128, 128), F32)], axis=1)
        transposed.append(split(jnp.concatenate([top, jnp.concatenate([corner.T, c.T], axis=1)], axis=0)))

    sums = [p_ref[k] for k in range(4)]
    for s in range(4, p_ref.shape[0]):
        sums[s % 4] = sums[s % 4] + p_ref[s]
    total = (sums[0] + sums[1]) + (sums[2] + sums[3])
    rest = [
        jnp.concatenate([total[8 * p : 8 * p + 4], total[8 * p + 4 : 8 * p + 8]], axis=1)
        for p in range(4)
    ]

    def times(a, b):
        high = a.astype(BF16).astype(F32)
        both = jnp.concatenate([high, a - high], axis=0).astype(BF16)
        product = dg(both, b[0]) + dg(both, b[1])
        return product[:4] + product[4:]

    pieces = [None] * 4
    for q in range(3, -1, -1):
        solved = times(rest[q], transposed[q])
        pieces[q] = jnp.concatenate([solved[:, :128], solved[:, 128:]], axis=0)
        for p in range(q):
            rest[p] = rest[p] - times(solved, others[p, q])
    result = jnp.concatenate(pieces, axis=0)
    w_ref[...] = jnp.broadcast_to(result[None], w_ref.shape)


def solve(core, own, other, p):
    return pl.pallas_call(
        solve_kernel,
        out_shape=jax.ShapeDtypeStruct(p.shape, F32),
        in_specs=[smem()] + [vmem()] * 3,
        out_specs=vmem(),
        compiler_params=params(),
        cost_estimate=pl.CostEstimate(flops=4 * 10**9, bytes_accessed=5 << 20, transcendentals=0),
        name="solve",
    )(core, own, other, p)


def rows_of(ref, j):
    stride = ref.shape[0] // 64
    return jnp.concatenate([ref[pl.ds(j * 4 + r, 64, stride=stride), :] for r in range(4)], axis=0)


def project_kernel(core, e_ref, own_ref, other_ref, p_ref):
    c = core[0]
    sides = [
        (split(jnp.concatenate([rows_of(e_ref, first + k) for k in range(4)], axis=1)), v_ref)
        for v_ref, first in ((own_ref, 4 * c), (other_ref, 4 - 4 * c))
    ]
    for n in range(4):
        total = sum(dot3(left, split(v_ref[:, n * WIDE : (n + 1) * WIDE])) for left, v_ref in sides)
        for h in range(2):
            for r in range(4):
                p_ref[pl.ds((2 * n + h) * 4 + r, 64, stride=32), :] = total[
                    r * 64 : (r + 1) * 64, h * 128 : (h + 1) * 128
                ]


def project(core, e, own, other):
    return pl.pallas_call(
        project_kernel,
        out_shape=jax.ShapeDtypeStruct((2048, 128), F32),
        in_specs=[smem(), vmem(), vmem(), vmem()],
        out_specs=vmem(),
        compiler_params=params(),
        cost_estimate=pl.CostEstimate(flops=2 * 10**9, bytes_accessed=6 << 20, transcendentals=0),
        name="project",
    )(core, e, own, other)


def update_kernel(core, e_ref, w_ref, own_ref, other_ref, o_ref):
    c = core[0]
    left = split(jnp.concatenate([rows_of(w_ref, n) for n in range(8)], axis=1))
    for v_ref, first in ((own_ref, 4 * c), (other_ref, 4 - 4 * c)):
        for k in range(2):
            change = dot3(left, split(v_ref[k * WIDE : (k + 1) * WIDE, :]), NT)
            for h in range(2):
                j = first + 2 * k + h
                for r in range(4):
                    before = e_ref[pl.ds(j * 4 + r, 64, stride=e_ref.shape[0] // 64), :]
                    part = change[r * 64 : (r + 1) * 64, h * 128 : (h + 1) * 128]
                    o_ref[pl.ds(j * 4 + r, 64, stride=32), :] = before - part


def update(core, e, w, own, other):
    return pl.pallas_call(
        update_kernel,
        out_shape=jax.ShapeDtypeStruct((2048, 128), F32),
        in_specs=[smem(), vmem(), vmem(), vmem(), vmem()],
        out_specs=vmem(),
        compiler_params=params(),
        cost_estimate=pl.CostEstimate(flops=2 * 10**9, bytes_accessed=7 << 20, transcendentals=0),
        name="update",
    )(core, e, w, own, other)


def to_chips(a):
    return lax.all_to_all(a, CHIPS, split_axis=0, concat_axis=0, tiled=True)


def swap_cores(a):
    return lax.ppermute(a, "c", [(0, 1), (1, 0)])


def body(eigvecs, reflectors, offsets, lengths, panels):
    core = lax.axis_index("c").astype(jnp.int32).reshape(1)
    other = swap_cores(panels)
    parts = to_chips(gram(core, other, gram(core, panels)).reshape(64, 40, 128))
    tiles = eigvecs.reshape(4, 512, 128).transpose(1, 0, 2)
    chased = chase(tiles, reflectors, offsets, lengths)
    mine = to_chips(share(chased.reshape(64, 32, 128), parts)).reshape(4608, 128)
    theirs = swap_cores(mine)
    projected = to_chips(project(core, mine, panels, other).reshape(64, 32, 128))
    weights = to_chips(solve(core, mine, theirs, projected)).reshape(2048, 128)
    result = to_chips(update(core, mine, weights, panels, other).reshape(64, 32, 128))
    return result.reshape(64, 8, 4, 128).transpose(2, 0, 1, 3).reshape(4, 65536)


def solution(mesh):
    fine = Mesh(mesh.devices.reshape(2, 4, 2, 4, 2), AXES)
    return jax.shard_map(
        body,
        mesh=fine,
        in_specs=(P(AXES, None), P(), P(), P(), P(AXES, None)),
        out_specs=P(AXES, None),
        check_vma=False,
    )
```

```python
import jax
import jax.numpy as jnp
from jax import lax
from jax.experimental import pallas as pl
from jax.experimental.pallas import tpu as pltpu
from jax.sharding import Mesh, PartitionSpec as P

F32 = jnp.float32
BF16 = jnp.bfloat16
AXES = ("yh", "x", "yl", "z", "c")
CHIPS = ("yh", "x", "yl", "z")
VMEM_LIMIT = 20 * 1024 * 1024
LARGE = 58 * 1024 * 1024

NN = (((1,), (0,)), ((), ()))
NT = (((1,), (1,)), ((), ()))
TN = (((0,), (0,)), ((), ()))


def dg(a, b, dims=NN):
    return lax.dot_general(a, b, dims, preferred_element_type=F32)


def split(a):
    high = a.astype(BF16)
    low = (a - high.astype(F32)).astype(BF16)
    return high, low


def dot3(a, b, dims=NN):
    (ah, al), (bh, bl) = a, b
    return dg(ah, bh, dims) + (dg(ah, bl, dims) + dg(al, bh, dims))


def dot4(a, b):
    n = b[0].shape[1]
    right = jnp.concatenate(b, axis=1)
    both = dg(jnp.concatenate(a, axis=1), jnp.concatenate([right, right], axis=0))
    return both[:, :n] + both[:, n:]


def dot4_nt(a, b):
    n = b[0].shape[0]
    right = jnp.concatenate(b, axis=0)
    both = dg(jnp.concatenate(a, axis=1), jnp.concatenate([right, right], axis=1), NT)
    return both[:, :n] + both[:, n:]


def iotas(n):
    return (
        lax.broadcasted_iota(jnp.int32, (n, n), 0),
        lax.broadcasted_iota(jnp.int32, (n, n), 1),
    )


def inverse_of_half(grams):
    stages = inverse_stages(grams)
    while True:
        try:
            next(stages)
        except StopIteration as end:
            return end.value


def inverse_stages(grams):
    n = grams[0].shape[0]
    row, col = iotas(n)
    eye = (row == col).astype(F32)
    upper = row < col
    inverses, strict, scale = [], [], []
    for gram in grams:
        diagonal = gram * (0.5 * eye)
        by_row = jnp.sum(diagonal, axis=1, keepdims=True)
        by_col = jnp.sum(diagonal, axis=0, keepdims=True)
        nil = jnp.where(upper, gram / by_row, 0.0)
        strict.append(nil)
        scale.append(1.0 / by_col)
        first = ((row ^ col) == 1) & ((row & 1) == 0)
        inverses.append(eye - jnp.where(first, nil, 0.0))
    size = 2
    while size < n:
        corner = ((row // (2 * size)) == (col // (2 * size))) & ((row & size) == 0) & ((col & size) != 0)
        halves = [split(x) for x in inverses]
        corners = [split(jnp.where(corner, nil, 0.0)) for nil in strict]
        middles = [split(dot4(x, m)) for x, m in zip(halves, corners)]
        yield
        inverses = [x - dot4(y, h) for x, y, h in zip(inverses, middles, halves)]
        size *= 2
        yield
    return [x * s for x, s in zip(inverses, scale)]


TOGETHER = 8
EVERY = 2


def gram_of(m):
    width = m[0].shape[1]
    both = dg(m[0], jnp.concatenate(m, axis=1), TN)
    return both[:, :width] + both[:, width:] + dg(m[1], m[0], TN)


def chase_kernel(offsets, lengths, e_hbm, m_hbm, o_hbm, e_ref, m_ref, kh_ref, kl_ref, sems):
    blocks, extent, width = m_ref.shape
    tiles, rows = e_ref.shape[0], e_ref.shape[1]
    groups = blocks // TOGETHER
    loads = [
        pltpu.make_async_copy(
            m_hbm.at[pl.ds(g * TOGETHER, TOGETHER)], m_ref.at[pl.ds(g * TOGETHER, TOGETHER)], sems.at[g]
        )
        for g in range(groups)
    ]
    load_e = pltpu.make_async_copy(e_hbm, e_ref, sems.at[groups])
    loads[0].start()
    load_e.start()
    for load in loads[1:]:
        load.start()
    row = lax.broadcasted_iota(jnp.int32, (extent, width), 0)
    lane = lax.broadcasted_iota(jnp.int32, (rows, 128), 1)

    def prepare(group):
        at = [group * TOGETHER + u for u in range(TOGETHER)]
        masked = [split(jnp.where(row < lengths[b], m_ref[b], 0.0)) for b in at]
        grams = [gram_of(m) for m in masked]
        yield
        inverses = yield from inverse_stages(grams)
        lefts = [split(dot4_nt(m, split(f))) for m, f in zip(masked, inverses)]
        yield
        for left, m, b in zip(lefts, masked, at):
            kh_ref[b], kl_ref[b] = split(dot4_nt(left, m))

    def step(b):
        offset = offsets[b]
        tile = jnp.minimum(offset // 128, tiles - 3)
        shift = offset - tile * 128
        v0, v1, v2 = e_ref[tile], e_ref[tile + 1], e_ref[tile + 2]
        left = (128 - shift) & 127
        r0 = pltpu.roll(v0, left, 1)
        r1 = pltpu.roll(v1, left, 1)
        r2 = pltpu.roll(v2, left, 1)
        inside = lane < 128 - shift
        window = jnp.concatenate([jnp.where(inside, r0, r1), jnp.where(inside, r1, r2)], axis=1)
        high = window.astype(BF16).astype(F32)
        both = jnp.concatenate([high, window - high], axis=0).astype(BF16)
        change = dg(both, kh_ref[b]) + dg(both, kl_ref[b])
        change = change[:rows] + change[rows:]
        right = shift & 127
        q0 = pltpu.roll(change[:, :128], right, 1)
        q1 = pltpu.roll(change[:, 128:], right, 1)
        after = lane >= shift
        e_ref[tile] = v0 - jnp.where(after, q0, 0.0)
        e_ref[tile + 1] = v1 - jnp.where(after, q1, q0)
        e_ref[tile + 2] = v2 - jnp.where(after, 0.0, q1)

    loads[0].wait()
    for stage in prepare(0):
        pass
    load_e.wait()
    for load in loads[1:]:
        load.wait()
    for group in range(1, groups):
        waiting = list(range((group - 1) * TOGETHER, group * TOGETHER))
        for at, stage in enumerate(prepare(group)):
            if waiting and at % EVERY == 0:
                step(waiting.pop(0))
        for b in waiting:
            step(b)
    for u in range(TOGETHER):
        step((groups - 1) * TOGETHER + u)
    store = pltpu.make_async_copy(e_ref, o_hbm, sems.at[groups + 1])
    store.start()
    store.wait()


def share_kernel(e_hbm, g_ref, o_ref, sem):
    copy = pltpu.make_async_copy(e_hbm, o_ref.at[:, pl.ds(0, 32), :], sem)
    copy.start()
    sums = [g_ref[k] for k in range(4)]
    for s in range(4, g_ref.shape[0]):
        sums[s % 4] = sums[s % 4] + g_ref[s]
    total = (sums[0] + sums[1]) + (sums[2] + sums[3])
    for s in range(g_ref.shape[0]):
        o_ref[s, 32:, :] = total
    copy.wait()


def vmem():
    return pl.BlockSpec(memory_space=pltpu.VMEM)


def smem():
    return pl.BlockSpec(memory_space=pltpu.SMEM)


def params():
    return pltpu.CompilerParams(vmem_limit_bytes=VMEM_LIMIT)


def hbm():
    return pl.BlockSpec(memory_space=pltpu.HBM)


def chase(tiles, reflectors, offsets, lengths):
    blocks, extent, width = reflectors.shape
    return pl.pallas_call(
        chase_kernel,
        out_shape=jax.ShapeDtypeStruct(tiles.shape, F32),
        in_specs=[smem(), smem()] + [hbm()] * 2,
        out_specs=hbm(),
        scratch_shapes=[pltpu.VMEM(tiles.shape, F32), pltpu.VMEM(reflectors.shape, F32)]
        + [pltpu.VMEM((blocks, extent, extent), BF16)] * 2
        + [pltpu.SemaphoreType.DMA((blocks // TOGETHER + 2,))],
        compiler_params=pltpu.CompilerParams(vmem_limit_bytes=LARGE),
        cost_estimate=pl.CostEstimate(flops=20 * 10**9, bytes_accessed=7 << 20, transcendentals=0),
        name="chase",
    )(offsets, lengths, tiles, reflectors)


def share(chased, parts):
    return pl.pallas_call(
        share_kernel,
        out_shape=jax.ShapeDtypeStruct((64, 72, 128), F32),
        in_specs=[hbm(), vmem()],
        out_specs=vmem(),
        scratch_shapes=[pltpu.SemaphoreType.DMA],
        compiler_params=params(),
        cost_estimate=pl.CostEstimate(flops=10**6, bytes_accessed=5 << 20, transcendentals=0),
        name="share",
    )(chased, parts)


WIDE = 256
ORDER = ((0, 1, 2, 3), (2, 0, 3, 1))
LOCAL = ((0, 1), (1, 2), (2, 3), (1, 1), (2, 2))
MADE = [(ORDER[c][i], ORDER[c][j]) for c in range(2) for (i, j) in LOCAL]


def gram_kernel(core, v_ref, *refs):
    c = core[0]
    g_ref = refs[-1]
    order = (2 * c, 1 - c, 2 + c, 3 - 2 * c)
    halves = [split(v_ref[:, pl.ds(pl.multiple_of(o * WIDE, WIDE), WIDE)]) for o in order]
    for at, (i, j) in enumerate(LOCAL):
        block = dot3(halves[i], halves[j], TN)
        for h in range(2):
            rows = pl.ds((at * 2 + h) * WIDE, WIDE)
            part = block[:, h * 128 : (h + 1) * 128]
            g_ref[rows, :] = part + refs[0][rows, :] if len(refs) == 2 else part


def gram(core, panels, *before):
    return pl.pallas_call(
        gram_kernel,
        out_shape=jax.ShapeDtypeStruct((len(LOCAL) * 2 * WIDE, 128), F32),
        in_specs=[smem(), vmem()] + [vmem()] * len(before),
        out_specs=vmem(),
        compiler_params=params(),
        cost_estimate=pl.CostEstimate(flops=10**9, bytes_accessed=4 << 20, transcendentals=0),
        name="gram",
    )(core, panels, *before)


def gram_block(ref, local):
    first = 2 * local * WIDE
    return jnp.concatenate([ref[pl.ds(first + h * WIDE, WIDE), :] for h in range(2)], axis=1)


def solve_kernel(core, own_ref, other_ref, p_ref, w_ref):
    diagonals, others = [None] * 4, {}
    first = core[0] == 0
    pairs = [(gram_block(own_ref, k), gram_block(other_ref, k)) for k in range(len(LOCAL))]
    values = [jnp.where(first, a, b) for a, b in pairs] + [jnp.where(first, b, a) for a, b in pairs]
    for value, (i, j) in zip(values, MADE):
        if i == j:
            diagonals[i] = value
        else:
            others[min(i, j), max(i, j)] = split(value.T if i < j else value)
    small = []
    for d in diagonals:
        small.extend([d[:128, :128], d[128:, 128:]])
    inverses = inverse_of_half(small)
    transposed = []
    for p, d in enumerate(diagonals):
        a, c = inverses[2 * p], inverses[2 * p + 1]
        corner = -dot4(split(dot4(split(a), split(d[:128, 128:]))), split(c))
        top = jnp.concatenate([a.T, jnp.zeros((128, 128), F32)], axis=1)
        transposed.append(split(jnp.concatenate([top, jnp.concatenate([corner.T, c.T], axis=1)], axis=0)))

    sums = [p_ref[k] for k in range(4)]
    for s in range(4, p_ref.shape[0]):
        sums[s % 4] = sums[s % 4] + p_ref[s]
    total = (sums[0] + sums[1]) + (sums[2] + sums[3])
    rest = [
        jnp.concatenate([total[8 * p : 8 * p + 4], total[8 * p + 4 : 8 * p + 8]], axis=1)
        for p in range(4)
    ]

    def times(a, b):
        high = a.astype(BF16).astype(F32)
        both = jnp.concatenate([high, a - high], axis=0).astype(BF16)
        product = dg(both, b[0]) + dg(both, b[1])
        return product[:4] + product[4:]

    pieces = [None] * 4
    for q in range(3, -1, -1):
        solved = times(rest[q], transposed[q])
        pieces[q] = jnp.concatenate([solved[:, :128], solved[:, 128:]], axis=0)
        for p in range(q):
            rest[p] = rest[p] - times(solved, others[p, q])
    result = jnp.concatenate(pieces, axis=0)
    w_ref[...] = jnp.broadcast_to(result[None], w_ref.shape)


def solve(core, own, other, p):
    return pl.pallas_call(
        solve_kernel,
        out_shape=jax.ShapeDtypeStruct(p.shape, F32),
        in_specs=[smem()] + [vmem()] * 3,
        out_specs=vmem(),
        compiler_params=params(),
        cost_estimate=pl.CostEstimate(flops=4 * 10**9, bytes_accessed=5 << 20, transcendentals=0),
        name="solve",
    )(core, own, other, p)


def rows_of(ref, j):
    stride = ref.shape[0] // 64
    return jnp.concatenate([ref[pl.ds(j * 4 + r, 64, stride=stride), :] for r in range(4)], axis=0)


def project_kernel(core, e_ref, own_ref, other_ref, p_ref, half_ref):
    for s in range(64):
        half_ref[s * 40 : (s + 1) * 40, :] = e_ref[s * 72 + 32 : (s + 1) * 72, :]
    c = core[0]
    sides = [
        (split(jnp.concatenate([rows_of(e_ref, first + k) for k in range(4)], axis=1)), v_ref)
        for v_ref, first in ((own_ref, 4 * c), (other_ref, 4 - 4 * c))
    ]
    for n in range(4):
        total = sum(dot3(left, split(v_ref[:, n * WIDE : (n + 1) * WIDE])) for left, v_ref in sides)
        for h in range(2):
            for r in range(4):
                p_ref[pl.ds((2 * n + h) * 4 + r, 64, stride=32), :] = total[
                    r * 64 : (r + 1) * 64, h * 128 : (h + 1) * 128
                ]


def project(core, e, own, other):
    return pl.pallas_call(
        project_kernel,
        out_shape=[jax.ShapeDtypeStruct((rows, 128), F32) for rows in (2048, 2560)],
        in_specs=[smem(), vmem(), vmem(), vmem()],
        out_specs=[vmem()] * 2,
        compiler_params=params(),
        cost_estimate=pl.CostEstimate(flops=2 * 10**9, bytes_accessed=6 << 20, transcendentals=0),
        name="project",
    )(core, e, own, other)


def update_kernel(core, e_ref, w_ref, own_ref, other_ref, o_ref):
    c = core[0]
    left = split(jnp.concatenate([rows_of(w_ref, n) for n in range(8)], axis=1))
    for v_ref, first in ((own_ref, 4 * c), (other_ref, 4 - 4 * c)):
        for k in range(2):
            change = dot3(left, split(v_ref[k * WIDE : (k + 1) * WIDE, :]), NT)
            for h in range(2):
                j = first + 2 * k + h
                for r in range(4):
                    before = e_ref[pl.ds(j * 4 + r, 64, stride=e_ref.shape[0] // 64), :]
                    part = change[r * 64 : (r + 1) * 64, h * 128 : (h + 1) * 128]
                    o_ref[pl.ds(j * 4 + r, 64, stride=32), :] = before - part


def update(core, e, w, own, other):
    return pl.pallas_call(
        update_kernel,
        out_shape=jax.ShapeDtypeStruct((2048, 128), F32),
        in_specs=[smem(), vmem(), vmem(), vmem(), vmem()],
        out_specs=vmem(),
        compiler_params=params(),
        cost_estimate=pl.CostEstimate(flops=2 * 10**9, bytes_accessed=7 << 20, transcendentals=0),
        name="update",
    )(core, e, w, own, other)


def finish_kernel(t_ref, o_ref):
    count = o_ref.shape[1] // 128
    first = pl.program_id(0) * count
    for t in range(count):
        o_ref[:, t * 128 : (t + 1) * 128] = t_ref[first + t]


def to_chips(a):
    return lax.all_to_all(a, CHIPS, split_axis=0, concat_axis=0, tiled=True)


def swap_cores(a):
    return lax.ppermute(a, "c", [(0, 1), (1, 0)])


def body(eigvecs, reflectors, offsets, lengths, panels):
    core = lax.axis_index("c").astype(jnp.int32).reshape(1)
    other = swap_cores(panels)
    parts = to_chips(gram(core, other, gram(core, panels)).reshape(64, 40, 128))
    tiles = eigvecs.reshape(4, 512, 128).transpose(1, 0, 2)
    chased = chase(tiles, reflectors, offsets, lengths)
    mine = to_chips(share(chased.reshape(64, 32, 128), parts)).reshape(4608, 128)
    projected, half = project(core, mine, panels, other)
    projected = to_chips(projected.reshape(64, 32, 128))
    weights = to_chips(solve(core, half, swap_cores(half), projected)).reshape(2048, 128)
    result = to_chips(update(core, mine, weights, panels, other).reshape(64, 32, 128))
    return pl.pallas_call(
        finish_kernel,
        out_shape=jax.ShapeDtypeStruct((4, 65536), F32),
        grid=(4,),
        in_specs=[vmem()],
        out_specs=pl.BlockSpec((4, 16384), lambda i: (0, i)),
        compiler_params=params(),
        cost_estimate=pl.CostEstimate(flops=0, bytes_accessed=2 << 20, transcendentals=0),
        name="finish",
    )(result.reshape(512, 4, 128))


def solution(mesh):
    fine = Mesh(mesh.devices.reshape(2, 4, 2, 4, 2), AXES)
    return jax.shard_map(
        body,
        mesh=fine,
        in_specs=(P(AXES, None), P(), P(), P(), P(AXES, None)),
        out_specs=P(AXES, None),
        check_vma=False,
    )
```

```python
import jax
import jax.numpy as jnp
from jax import lax
from jax.experimental import pallas as pl
from jax.experimental.pallas import tpu as pltpu
from jax.sharding import Mesh, PartitionSpec as P

F32 = jnp.float32
BF16 = jnp.bfloat16
AXES = ("yh", "x", "yl", "z", "c")
CHIPS = ("yh", "x", "yl", "z")
VMEM_LIMIT = 20 * 1024 * 1024
LARGE = 58 * 1024 * 1024

NN = (((1,), (0,)), ((), ()))
NT = (((1,), (1,)), ((), ()))
TN = (((0,), (0,)), ((), ()))


def dg(a, b, dims=NN):
    return lax.dot_general(a, b, dims, preferred_element_type=F32)


def split(a):
    high = a.astype(BF16)
    low = (a - high.astype(F32)).astype(BF16)
    return high, low


def dot3(a, b, dims=NN):
    (ah, al), (bh, bl) = a, b
    return dg(ah, bh, dims) + (dg(ah, bl, dims) + dg(al, bh, dims))


def dot4(a, b):
    n = b[0].shape[1]
    right = jnp.concatenate(b, axis=1)
    both = dg(jnp.concatenate(a, axis=1), jnp.concatenate([right, right], axis=0))
    return both[:, :n] + both[:, n:]


def dot4_nt(a, b):
    n = b[0].shape[0]
    right = jnp.concatenate(b, axis=0)
    both = dg(jnp.concatenate(a, axis=1), jnp.concatenate([right, right], axis=1), NT)
    return both[:, :n] + both[:, n:]


def iotas(n):
    return (
        lax.broadcasted_iota(jnp.int32, (n, n), 0),
        lax.broadcasted_iota(jnp.int32, (n, n), 1),
    )


def inverse_of_half(grams):
    stages = inverse_stages(grams)
    while True:
        try:
            next(stages)
        except StopIteration as end:
            return end.value


def inverse_stages(grams):
    n = grams[0].shape[0]
    row, col = iotas(n)
    eye = (row == col).astype(F32)
    upper = row < col
    inverses, strict, scale = [], [], []
    for gram in grams:
        diagonal = gram * (0.5 * eye)
        by_row = jnp.sum(diagonal, axis=1, keepdims=True)
        by_col = jnp.sum(diagonal, axis=0, keepdims=True)
        nil = jnp.where(upper, gram / by_row, 0.0)
        strict.append(nil)
        scale.append(1.0 / by_col)
        first = ((row ^ col) == 1) & ((row & 1) == 0)
        inverses.append(eye - jnp.where(first, nil, 0.0))
    size = 2
    while size < n:
        corner = ((row // (2 * size)) == (col // (2 * size))) & ((row & size) == 0) & ((col & size) != 0)
        halves = [split(x) for x in inverses]
        corners = [split(jnp.where(corner, nil, 0.0)) for nil in strict]
        middles = [split(dot4(x, m)) for x, m in zip(halves, corners)]
        yield
        inverses = [x - dot4(y, h) for x, y, h in zip(inverses, middles, halves)]
        size *= 2
        yield
    return [x * s for x, s in zip(inverses, scale)]


TOGETHER = 8
EVERY = 2


def gram_of(m):
    width = m[0].shape[1]
    both = dg(m[0], jnp.concatenate(m, axis=1), TN)
    return both[:, :width] + both[:, width:] + dg(m[1], m[0], TN)


def chase_kernel(offsets, lengths, e_hbm, m_hbm, o_hbm, e_ref, m_ref, kh_ref, kl_ref, sems):
    blocks, extent, width = m_ref.shape
    tiles, rows = e_ref.shape[0], e_ref.shape[1]
    groups = blocks // TOGETHER
    loads = [
        pltpu.make_async_copy(
            m_hbm.at[pl.ds(g * TOGETHER, TOGETHER)], m_ref.at[pl.ds(g * TOGETHER, TOGETHER)], sems.at[g]
        )
        for g in range(groups)
    ]
    load_e = pltpu.make_async_copy(e_hbm, e_ref, sems.at[groups])
    loads[0].start()
    load_e.start()
    for load in loads[1:]:
        load.start()
    row = lax.broadcasted_iota(jnp.int32, (extent, width), 0)
    lane = lax.broadcasted_iota(jnp.int32, (rows, 128), 1)

    def prepare(group):
        at = [group * TOGETHER + u for u in range(TOGETHER)]
        masked = [split(jnp.where(row < lengths[b], m_ref[b], 0.0)) for b in at]
        grams = [gram_of(m) for m in masked]
        yield
        inverses = yield from inverse_stages(grams)
        lefts = [split(dot4_nt(m, split(f))) for m, f in zip(masked, inverses)]
        yield
        for left, m, b in zip(lefts, masked, at):
            kh_ref[b], kl_ref[b] = split(dot4_nt(left, m))

    def step(b):
        offset = offsets[b]
        tile = jnp.minimum(offset // 128, tiles - 3)
        shift = offset - tile * 128
        v0, v1, v2 = e_ref[tile], e_ref[tile + 1], e_ref[tile + 2]
        left = (128 - shift) & 127
        r0 = pltpu.roll(v0, left, 1)
        r1 = pltpu.roll(v1, left, 1)
        r2 = pltpu.roll(v2, left, 1)
        inside = lane < 128 - shift
        window = jnp.concatenate([jnp.where(inside, r0, r1), jnp.where(inside, r1, r2)], axis=1)
        high = window.astype(BF16).astype(F32)
        both = jnp.concatenate([high, window - high], axis=0).astype(BF16)
        change = dg(both, kh_ref[b]) + dg(both, kl_ref[b])
        change = change[:rows] + change[rows:]
        right = shift & 127
        q0 = pltpu.roll(change[:, :128], right, 1)
        q1 = pltpu.roll(change[:, 128:], right, 1)
        after = lane >= shift
        e_ref[tile] = v0 - jnp.where(after, q0, 0.0)
        e_ref[tile + 1] = v1 - jnp.where(after, q1, q0)
        e_ref[tile + 2] = v2 - jnp.where(after, 0.0, q1)

    loads[0].wait()
    for stage in prepare(0):
        pass
    load_e.wait()
    for load in loads[1:]:
        load.wait()
    for group in range(1, groups):
        waiting = list(range((group - 1) * TOGETHER, group * TOGETHER))
        for at, stage in enumerate(prepare(group)):
            if waiting and at % EVERY == 0:
                step(waiting.pop(0))
        for b in waiting:
            step(b)
    for u in range(TOGETHER):
        step((groups - 1) * TOGETHER + u)
    store = pltpu.make_async_copy(e_ref, o_hbm, sems.at[groups + 1])
    store.start()
    store.wait()


def share_kernel(e_hbm, g_ref, o_ref, sem):
    copy = pltpu.make_async_copy(e_hbm, o_ref.at[:, pl.ds(0, 8)], sem)
    copy.start()
    chips, count = g_ref.shape[0], g_ref.shape[1]
    sums = [g_ref[k] for k in range(4)]
    for s in range(4, chips):
        sums[s % 4] = sums[s % 4] + g_ref[s]
    total = (sums[0] + sums[1]) + (sums[2] + sums[3])
    for s in range(chips):
        o_ref[s, 8:] = total
    copy.wait()


def vmem():
    return pl.BlockSpec(memory_space=pltpu.VMEM)


def smem():
    return pl.BlockSpec(memory_space=pltpu.SMEM)


def params():
    return pltpu.CompilerParams(vmem_limit_bytes=VMEM_LIMIT)


def hbm():
    return pl.BlockSpec(memory_space=pltpu.HBM)


def chase(tiles, reflectors, offsets, lengths):
    blocks, extent, width = reflectors.shape
    return pl.pallas_call(
        chase_kernel,
        out_shape=jax.ShapeDtypeStruct(tiles.shape, F32),
        in_specs=[smem(), smem()] + [hbm()] * 2,
        out_specs=hbm(),
        scratch_shapes=[pltpu.VMEM(tiles.shape, F32), pltpu.VMEM(reflectors.shape, F32)]
        + [pltpu.VMEM((blocks, extent, extent), BF16)] * 2
        + [pltpu.SemaphoreType.DMA((blocks // TOGETHER + 2,))],
        compiler_params=pltpu.CompilerParams(vmem_limit_bytes=LARGE),
        cost_estimate=pl.CostEstimate(flops=20 * 10**9, bytes_accessed=7 << 20, transcendentals=0),
        name="chase",
    )(offsets, lengths, tiles, reflectors)


def share(chased, parts):
    return pl.pallas_call(
        share_kernel,
        out_shape=jax.ShapeDtypeStruct((64, 8 + SHARE // 4, 4, 128), F32),
        in_specs=[hbm(), vmem()],
        out_specs=vmem(),
        scratch_shapes=[pltpu.SemaphoreType.DMA],
        compiler_params=params(),
        cost_estimate=pl.CostEstimate(flops=10**6, bytes_accessed=5 << 20, transcendentals=0),
        name="share",
    )(chased, parts)


WIDE = 256
ORDER = ((0, 1, 2, 3), (2, 0, 3, 1))
LOCAL = ((0, 1), (1, 2), (2, 3), (1, 1), (2, 2))
MADE = [(ORDER[c][i], ORDER[c][j]) for c in range(2) for (i, j) in LOCAL]
SENT = [(WIDE // 2 if i == j else WIDE, WIDE) for (i, j) in LOCAL]
STARTS = [sum(map(sum, SENT[:at])) for at in range(len(LOCAL) + 1)]
SHARE = STARTS[-1] // 64


def gram_kernel(core, v_ref, *refs):
    c = core[0]
    g_ref = refs[-1]
    order = (2 * c, 1 - c, 2 + c, 3 - 2 * c)
    halves = [split(v_ref[:, pl.ds(pl.multiple_of(o * WIDE, WIDE), WIDE)]) for o in order]
    for at, (i, j) in enumerate(LOCAL):
        block = dot3(halves[i], halves[j], TN)
        start = STARTS[at]
        for h, count in enumerate(SENT[at]):
            rows = pl.ds(start, count)
            part = block[:count, h * 128 : (h + 1) * 128]
            g_ref[rows, :] = part + refs[0][rows, :] if len(refs) == 2 else part
            start += count


def gram(core, panels, *before):
    return pl.pallas_call(
        gram_kernel,
        out_shape=jax.ShapeDtypeStruct((STARTS[-1], 128), F32),
        in_specs=[smem(), vmem()] + [vmem()] * len(before),
        out_specs=vmem(),
        compiler_params=params(),
        cost_estimate=pl.CostEstimate(flops=10**9, bytes_accessed=4 << 20, transcendentals=0),
        name="gram",
    )(core, panels, *before)


def gram_block(ref, local):
    left, right = SENT[local]
    start = STARTS[local]
    first = ref[pl.ds(start, left), :]
    if left < right:
        first = jnp.concatenate([first, jnp.zeros((right - left, 128), F32)], axis=0)
    return jnp.concatenate([first, ref[pl.ds(start + left, right), :]], axis=1)


def solve_kernel(core, own_ref, other_ref, p_ref, w_ref):
    diagonals, others = [None] * 4, {}
    first = core[0] == 0
    pairs = [(gram_block(own_ref, k), gram_block(other_ref, k)) for k in range(len(LOCAL))]
    values = [jnp.where(first, a, b) for a, b in pairs] + [jnp.where(first, b, a) for a, b in pairs]
    for value, (i, j) in zip(values, MADE):
        if i == j:
            diagonals[i] = value
        else:
            others[min(i, j), max(i, j)] = split(value.T if i < j else value)
    small = []
    for d in diagonals:
        small.extend([d[:128, :128], d[128:, 128:]])
    inverses = inverse_of_half(small)
    transposed = []
    for p, d in enumerate(diagonals):
        a, c = inverses[2 * p], inverses[2 * p + 1]
        corner = -dot4(split(dot4(split(a), split(d[:128, 128:]))), split(c))
        top = jnp.concatenate([a.T, jnp.zeros((128, 128), F32)], axis=1)
        transposed.append(split(jnp.concatenate([top, jnp.concatenate([corner.T, c.T], axis=1)], axis=0)))

    sums = [p_ref[k] for k in range(4)]
    for s in range(4, p_ref.shape[0]):
        sums[s % 4] = sums[s % 4] + p_ref[s]
    total = (sums[0] + sums[1]) + (sums[2] + sums[3])
    rest = [
        jnp.concatenate([total[8 * p : 8 * p + 4], total[8 * p + 4 : 8 * p + 8]], axis=1)
        for p in range(4)
    ]

    def times(a, b):
        high = a.astype(BF16).astype(F32)
        both = jnp.concatenate([high, a - high], axis=0).astype(BF16)
        product = dg(both, b[0]) + dg(both, b[1])
        return product[:4] + product[4:]

    pieces = [None] * 4
    for q in range(3, -1, -1):
        solved = times(rest[q], transposed[q])
        pieces[q] = jnp.concatenate([solved[:, :128], solved[:, 128:]], axis=0)
        for p in range(q):
            rest[p] = rest[p] - times(solved, others[p, q])
    result = jnp.concatenate(pieces, axis=0)
    w_ref[...] = jnp.broadcast_to(result[None], w_ref.shape)


def solve(core, own, other, p):
    return pl.pallas_call(
        solve_kernel,
        out_shape=jax.ShapeDtypeStruct(p.shape, F32),
        in_specs=[smem()] + [vmem()] * 3,
        out_specs=vmem(),
        compiler_params=params(),
        cost_estimate=pl.CostEstimate(flops=4 * 10**9, bytes_accessed=5 << 20, transcendentals=0),
        name="solve",
    )(core, own, other, p)


def rows_of(ref, j):
    stride = ref.shape[0] // 64
    return jnp.concatenate([ref[pl.ds(j * 4 + r, 64, stride=stride), :] for r in range(4)], axis=0)


def project_kernel(core, e_ref, own_ref, other_ref, p_ref, half_ref):
    stride = 32 + SHARE
    for s in range(64):
        half_ref[s * SHARE : (s + 1) * SHARE, :] = e_ref[s * stride + 32 : (s + 1) * stride, :]
    c = core[0]
    sides = [
        (split(jnp.concatenate([rows_of(e_ref, first + k) for k in range(4)], axis=1)), v_ref)
        for v_ref, first in ((own_ref, 4 * c), (other_ref, 4 - 4 * c))
    ]
    for n in range(4):
        total = sum(dot3(left, split(v_ref[:, n * WIDE : (n + 1) * WIDE])) for left, v_ref in sides)
        for h in range(2):
            for r in range(4):
                p_ref[pl.ds((2 * n + h) * 4 + r, 64, stride=32), :] = total[
                    r * 64 : (r + 1) * 64, h * 128 : (h + 1) * 128
                ]


def project(core, e, own, other):
    return pl.pallas_call(
        project_kernel,
        out_shape=[jax.ShapeDtypeStruct((rows, 128), F32) for rows in (2048, STARTS[-1])],
        in_specs=[smem(), vmem(), vmem(), vmem()],
        out_specs=[vmem()] * 2,
        compiler_params=params(),
        cost_estimate=pl.CostEstimate(flops=2 * 10**9, bytes_accessed=6 << 20, transcendentals=0),
        name="project",
    )(core, e, own, other)


def update_kernel(core, e_ref, w_ref, own_ref, other_ref, o_ref):
    c = core[0]
    left = split(jnp.concatenate([rows_of(w_ref, n) for n in range(8)], axis=1))
    for v_ref, first in ((own_ref, 4 * c), (other_ref, 4 - 4 * c)):
        for k in range(2):
            change = dot3(left, split(v_ref[k * WIDE : (k + 1) * WIDE, :]), NT)
            for h in range(2):
                j = first + 2 * k + h
                for r in range(4):
                    before = e_ref[pl.ds(j * 4 + r, 64, stride=e_ref.shape[0] // 64), :]
                    part = change[r * 64 : (r + 1) * 64, h * 128 : (h + 1) * 128]
                    o_ref[pl.ds(j * 4 + r, 64, stride=32), :] = before - part


def update(core, e, w, own, other):
    return pl.pallas_call(
        update_kernel,
        out_shape=jax.ShapeDtypeStruct((2048, 128), F32),
        in_specs=[smem(), vmem(), vmem(), vmem(), vmem()],
        out_specs=vmem(),
        compiler_params=params(),
        cost_estimate=pl.CostEstimate(flops=2 * 10**9, bytes_accessed=7 << 20, transcendentals=0),
        name="update",
    )(core, e, w, own, other)


def finish_kernel(t_ref, o_ref):
    count = o_ref.shape[1] // 128
    first = pl.program_id(0) * count
    for t in range(count):
        o_ref[:, t * 128 : (t + 1) * 128] = t_ref[first + t]


def to_chips(a):
    return lax.all_to_all(a, CHIPS, split_axis=0, concat_axis=0, tiled=True)


def swap_cores(a):
    return lax.ppermute(a, "c", [(0, 1), (1, 0)])


def body(eigvecs, reflectors, offsets, lengths, panels):
    core = lax.axis_index("c").astype(jnp.int32).reshape(1)
    other = swap_cores(panels)
    parts = to_chips(gram(core, other, gram(core, panels)).reshape(64, SHARE // 4, 4, 128))
    tiles = eigvecs.reshape(4, 512, 128).transpose(1, 0, 2)
    chased = chase(tiles, reflectors, offsets, lengths)
    mine = to_chips(share(chased.reshape(64, 8, 4, 128), parts)).reshape(64 * (32 + SHARE), 128)
    projected, half = project(core, mine, panels, other)
    projected = to_chips(projected.reshape(64, 32, 128))
    weights = to_chips(solve(core, half, swap_cores(half), projected)).reshape(2048, 128)
    result = to_chips(update(core, mine, weights, panels, other).reshape(64, 32, 128))
    return pl.pallas_call(
        finish_kernel,
        out_shape=jax.ShapeDtypeStruct((4, 65536), F32),
        grid=(4,),
        in_specs=[vmem()],
        out_specs=pl.BlockSpec((4, 16384), lambda i: (0, i)),
        compiler_params=params(),
        cost_estimate=pl.CostEstimate(flops=0, bytes_accessed=2 << 20, transcendentals=0),
        name="finish",
    )(result.reshape(512, 4, 128))


def solution(mesh):
    fine = Mesh(mesh.devices.reshape(2, 4, 2, 4, 2), AXES)
    return jax.shard_map(
        body,
        mesh=fine,
        in_specs=(P(AXES, None), P(), P(), P(), P(AXES, None)),
        out_specs=P(AXES, None),
        check_vma=False,
    )
```

```python
import jax
import jax.numpy as jnp
from jax import lax
from jax.experimental import pallas as pl
from jax.experimental.pallas import tpu as pltpu
from jax.sharding import Mesh, PartitionSpec as P

F32 = jnp.float32
BF16 = jnp.bfloat16
AXES = ("yh", "x", "yl", "z", "c")
CHIPS = ("yh", "x", "yl", "z")
VMEM_LIMIT = 20 * 1024 * 1024
LARGE = 58 * 1024 * 1024

NN = (((1,), (0,)), ((), ()))
NT = (((1,), (1,)), ((), ()))
TN = (((0,), (0,)), ((), ()))


def dg(a, b, dims=NN):
    return lax.dot_general(a, b, dims, preferred_element_type=F32)


def split(a):
    high = a.astype(BF16)
    low = (a - high.astype(F32)).astype(BF16)
    return high, low


def dot3(a, b, dims=NN):
    (ah, al), (bh, bl) = a, b
    return dg(ah, bh, dims) + (dg(ah, bl, dims) + dg(al, bh, dims))


def dot4(a, b):
    n = b[0].shape[1]
    right = jnp.concatenate(b, axis=1)
    both = dg(jnp.concatenate(a, axis=1), jnp.concatenate([right, right], axis=0))
    return both[:, :n] + both[:, n:]


def dot4_nt(a, b):
    n = b[0].shape[0]
    right = jnp.concatenate(b, axis=0)
    both = dg(jnp.concatenate(a, axis=1), jnp.concatenate([right, right], axis=1), NT)
    return both[:, :n] + both[:, n:]


def iotas(n):
    return (
        lax.broadcasted_iota(jnp.int32, (n, n), 0),
        lax.broadcasted_iota(jnp.int32, (n, n), 1),
    )


def inverse_of_half(grams):
    stages = inverse_stages(grams)
    while True:
        try:
            next(stages)
        except StopIteration as end:
            return end.value


def inverse_stages(grams):
    n = grams[0].shape[0]
    row, col = iotas(n)
    eye = (row == col).astype(F32)
    upper = row < col
    inverses, strict, scale = [], [], []
    for gram in grams:
        diagonal = gram * (0.5 * eye)
        by_row = jnp.sum(diagonal, axis=1, keepdims=True)
        by_col = jnp.sum(diagonal, axis=0, keepdims=True)
        nil = jnp.where(upper, gram / by_row, 0.0)
        strict.append(nil)
        scale.append(1.0 / by_col)
        first = ((row ^ col) == 1) & ((row & 1) == 0)
        inverses.append(eye - jnp.where(first, nil, 0.0))
    size = 2
    while size < n:
        corner = ((row // (2 * size)) == (col // (2 * size))) & ((row & size) == 0) & ((col & size) != 0)
        halves = [split(x) for x in inverses]
        corners = [split(jnp.where(corner, nil, 0.0)) for nil in strict]
        middles = [split(dot4(x, m)) for x, m in zip(halves, corners)]
        yield
        inverses = [x - dot4(y, h) for x, y, h in zip(inverses, middles, halves)]
        size *= 2
        yield
    return [x * s for x, s in zip(inverses, scale)]


TOGETHER = 8
EVERY = 2


def gram_of(m):
    width = m[0].shape[1]
    both = dg(m[0], jnp.concatenate(m, axis=1), TN)
    return both[:, :width] + both[:, width:] + dg(m[1], m[0], TN)


def chase_kernel(offsets, lengths, e_hbm, m_hbm, o_hbm, e_ref, m_ref, kh_ref, kl_ref, sems):
    blocks, extent, width = m_ref.shape
    tiles, rows = e_ref.shape[0], e_ref.shape[1]
    groups = blocks // TOGETHER
    loads = [
        pltpu.make_async_copy(
            m_hbm.at[pl.ds(g * TOGETHER, TOGETHER)], m_ref.at[pl.ds(g * TOGETHER, TOGETHER)], sems.at[g]
        )
        for g in range(groups)
    ]
    load_e = pltpu.make_async_copy(e_hbm, e_ref, sems.at[groups])
    loads[0].start()
    load_e.start()
    for load in loads[1:]:
        load.start()
    row = lax.broadcasted_iota(jnp.int32, (extent, width), 0)
    lane = lax.broadcasted_iota(jnp.int32, (rows, 128), 1)

    def prepare(group):
        at = [group * TOGETHER + u for u in range(TOGETHER)]
        masked = [split(jnp.where(row < lengths[b], m_ref[b], 0.0)) for b in at]
        grams = [gram_of(m) for m in masked]
        yield
        inverses = yield from inverse_stages(grams)
        lefts = [split(dot4_nt(m, split(f))) for m, f in zip(masked, inverses)]
        yield
        for left, m, b in zip(lefts, masked, at):
            kh_ref[b], kl_ref[b] = split(dot4_nt(left, m))

    def step(b):
        offset = offsets[b]
        tile = jnp.minimum(offset // 128, tiles - 3)
        shift = offset - tile * 128
        v0, v1, v2 = e_ref[tile], e_ref[tile + 1], e_ref[tile + 2]
        left = (128 - shift) & 127
        r0 = pltpu.roll(v0, left, 1)
        r1 = pltpu.roll(v1, left, 1)
        r2 = pltpu.roll(v2, left, 1)
        inside = lane < 128 - shift
        window = jnp.concatenate([jnp.where(inside, r0, r1), jnp.where(inside, r1, r2)], axis=1)
        high = window.astype(BF16).astype(F32)
        both = jnp.concatenate([high, window - high], axis=0).astype(BF16)
        change = dg(both, kh_ref[b]) + dg(both, kl_ref[b])
        change = change[:rows] + change[rows:]
        right = shift & 127
        q0 = pltpu.roll(change[:, :128], right, 1)
        q1 = pltpu.roll(change[:, 128:], right, 1)
        after = lane >= shift
        e_ref[tile] = v0 - jnp.where(after, q0, 0.0)
        e_ref[tile + 1] = v1 - jnp.where(after, q1, q0)
        e_ref[tile + 2] = v2 - jnp.where(after, 0.0, q1)

    loads[0].wait()
    for stage in prepare(0):
        pass
    load_e.wait()
    for load in loads[1:]:
        load.wait()
    for group in range(1, groups):
        waiting = list(range((group - 1) * TOGETHER, group * TOGETHER))
        for at, stage in enumerate(prepare(group)):
            if waiting and at % EVERY == 0:
                step(waiting.pop(0))
        for b in waiting:
            step(b)
    for u in range(TOGETHER):
        step((groups - 1) * TOGETHER + u)
    store = pltpu.make_async_copy(e_ref, o_hbm, sems.at[groups + 1])
    store.start()
    store.wait()


def share_kernel(e_hbm, g_ref, o_ref, sem):
    copy = pltpu.make_async_copy(e_hbm, o_ref.at[:, pl.ds(0, 8)], sem)
    copy.start()
    chips, count = g_ref.shape[0], g_ref.shape[1]
    sums = [g_ref[k] for k in range(4)]
    for s in range(4, chips):
        sums[s % 4] = sums[s % 4] + g_ref[s]
    total = (sums[0] + sums[1]) + (sums[2] + sums[3])
    for s in range(chips):
        o_ref[s, 8:] = total
    copy.wait()


def vmem():
    return pl.BlockSpec(memory_space=pltpu.VMEM)


def smem():
    return pl.BlockSpec(memory_space=pltpu.SMEM)


def params():
    return pltpu.CompilerParams(vmem_limit_bytes=VMEM_LIMIT)


def hbm():
    return pl.BlockSpec(memory_space=pltpu.HBM)


def chase(tiles, reflectors, offsets, lengths):
    blocks, extent, width = reflectors.shape
    return pl.pallas_call(
        chase_kernel,
        out_shape=jax.ShapeDtypeStruct(tiles.shape, F32),
        in_specs=[smem(), smem()] + [hbm()] * 2,
        out_specs=hbm(),
        scratch_shapes=[pltpu.VMEM(tiles.shape, F32), pltpu.VMEM(reflectors.shape, F32)]
        + [pltpu.VMEM((blocks, extent, extent), BF16)] * 2
        + [pltpu.SemaphoreType.DMA((blocks // TOGETHER + 2,))],
        compiler_params=pltpu.CompilerParams(vmem_limit_bytes=LARGE),
        cost_estimate=pl.CostEstimate(flops=20 * 10**9, bytes_accessed=7 << 20, transcendentals=0),
        name="chase",
    )(offsets, lengths, tiles, reflectors)


def share(chased, parts):
    return pl.pallas_call(
        share_kernel,
        out_shape=jax.ShapeDtypeStruct((64, 8 + SHARE // 4, 4, 128), F32),
        in_specs=[hbm(), vmem()],
        out_specs=vmem(),
        scratch_shapes=[pltpu.SemaphoreType.DMA],
        compiler_params=pltpu.CompilerParams(vmem_limit_bytes=20 * 1024 * 1024),
        cost_estimate=pl.CostEstimate(flops=10**6, bytes_accessed=5 << 20, transcendentals=0),
        name="share",
    )(chased, parts)


WIDE = 256
ORDER = ((0, 1, 2, 3), (2, 0, 3, 1))
LOCAL = ((0, 1), (1, 2), (2, 3), (1, 1), (2, 2))
MADE = [(ORDER[c][i], ORDER[c][j]) for c in range(2) for (i, j) in LOCAL]
SENT = [(WIDE // 2 if i == j else WIDE, WIDE) for (i, j) in LOCAL]
STARTS = [sum(map(sum, SENT[:at])) for at in range(len(LOCAL) + 1)]
SHARE = STARTS[-1] // 64


def gram_blocks(core, v_ref):
    c = core[0]
    order = (2 * c, 1 - c, 2 + c, 3 - 2 * c)
    halves = [split(v_ref[:, pl.ds(pl.multiple_of(o * WIDE, WIDE), WIDE)]) for o in order]
    for at, (i, j) in enumerate(LOCAL):
        block = dot3(halves[i], halves[j], TN)
        start = STARTS[at]
        for h, count in enumerate(SENT[at]):
            yield pl.ds(start, count), block[:count, h * 128 : (h + 1) * 128]
            start += count


def gram_kernel(core, v_ref, g_ref):
    for rows, part in gram_blocks(core, v_ref):
        g_ref[rows, :] = part


def gram_more_kernel(core, v_ref, before_ref, g_hbm, g_ref, sems):
    copies = []
    for rows, part in gram_blocks(core, v_ref):
        g_ref[rows, :] = before_ref[rows, :] + part
        copies.append(pltpu.make_async_copy(g_ref.at[rows], g_hbm.at[rows], sems.at[len(copies)]))
        copies[-1].start()
    for copy in copies:
        copy.wait()


def gram(core, panels):
    return pl.pallas_call(
        gram_kernel,
        out_shape=jax.ShapeDtypeStruct((STARTS[-1], 128), F32),
        in_specs=[smem(), vmem()],
        out_specs=vmem(),
        compiler_params=params(),
        cost_estimate=pl.CostEstimate(flops=10**9, bytes_accessed=3 << 20, transcendentals=0),
        name="gram",
    )(core, panels)


def gram_more(core, panels, before):
    return pl.pallas_call(
        gram_more_kernel,
        out_shape=jax.ShapeDtypeStruct((STARTS[-1], 128), F32),
        in_specs=[smem(), vmem(), vmem()],
        out_specs=hbm(),
        scratch_shapes=[
            pltpu.VMEM((STARTS[-1], 128), F32),
            pltpu.SemaphoreType.DMA((2 * len(LOCAL),)),
        ],
        compiler_params=params(),
        cost_estimate=pl.CostEstimate(flops=10**9, bytes_accessed=4 << 20, transcendentals=0),
        name="gram_more",
    )(core, panels, before)


def gram_block(ref, local):
    left, right = SENT[local]
    start = STARTS[local]
    first = ref[pl.ds(start, left), :]
    if left < right:
        first = jnp.concatenate([first, jnp.zeros((right - left, 128), F32)], axis=0)
    return jnp.concatenate([first, ref[pl.ds(start + left, right), :]], axis=1)


def solve_kernel(core, own_ref, other_ref, p_ref, w_ref):
    diagonals, others = [None] * 4, {}
    first = core[0] == 0
    pairs = [(gram_block(own_ref, k), gram_block(other_ref, k)) for k in range(len(LOCAL))]
    values = [jnp.where(first, a, b) for a, b in pairs] + [jnp.where(first, b, a) for a, b in pairs]
    for value, (i, j) in zip(values, MADE):
        if i == j:
            diagonals[i] = value
        else:
            others[min(i, j), max(i, j)] = split(value.T if i < j else value)
    small = []
    for d in diagonals:
        small.extend([d[:128, :128], d[128:, 128:]])
    inverses = inverse_of_half(small)
    transposed = []
    for p, d in enumerate(diagonals):
        a, c = inverses[2 * p], inverses[2 * p + 1]
        corner = -dot4(split(dot4(split(a), split(d[:128, 128:]))), split(c))
        top = jnp.concatenate([a.T, jnp.zeros((128, 128), F32)], axis=1)
        transposed.append(split(jnp.concatenate([top, jnp.concatenate([corner.T, c.T], axis=1)], axis=0)))

    sums = [p_ref[k] for k in range(4)]
    for s in range(4, p_ref.shape[0]):
        sums[s % 4] = sums[s % 4] + p_ref[s]
    total = (sums[0] + sums[1]) + (sums[2] + sums[3])
    rest = [
        jnp.concatenate([total[8 * p : 8 * p + 4], total[8 * p + 4 : 8 * p + 8]], axis=1)
        for p in range(4)
    ]

    def times(a, b):
        high = a.astype(BF16).astype(F32)
        both = jnp.concatenate([high, a - high], axis=0).astype(BF16)
        product = dg(both, b[0]) + dg(both, b[1])
        return product[:4] + product[4:]

    pieces = [None] * 4
    for q in range(3, -1, -1):
        solved = times(rest[q], transposed[q])
        pieces[q] = jnp.concatenate([solved[:, :128], solved[:, 128:]], axis=0)
        for p in range(q):
            rest[p] = rest[p] - times(solved, others[p, q])
    result = jnp.concatenate(pieces, axis=0)
    w_ref[...] = jnp.broadcast_to(result[None], w_ref.shape)


def solve(core, own, other, p):
    return pl.pallas_call(
        solve_kernel,
        out_shape=jax.ShapeDtypeStruct(p.shape, F32),
        in_specs=[smem()] + [vmem()] * 3,
        out_specs=vmem(),
        compiler_params=params(),
        cost_estimate=pl.CostEstimate(flops=4 * 10**9, bytes_accessed=5 << 20, transcendentals=0),
        name="solve",
    )(core, own, other, p)


def rows_of(ref, j):
    stride = ref.shape[0] // 64
    return jnp.concatenate([ref[pl.ds(j * 4 + r, 64, stride=stride), :] for r in range(4)], axis=0)


def compact_kernel(e_ref, half_ref):
    stride = 32 + SHARE
    for s in range(64):
        half_ref[s * SHARE : (s + 1) * SHARE, :] = e_ref[s * stride + 32 : (s + 1) * stride, :]


def compact(e):
    return pl.pallas_call(
        compact_kernel,
        out_shape=jax.ShapeDtypeStruct((STARTS[-1], 128), F32),
        in_specs=[vmem()],
        out_specs=vmem(),
        compiler_params=params(),
        cost_estimate=pl.CostEstimate(flops=0, bytes_accessed=2 << 20, transcendentals=0),
        name="compact",
    )(e)


def project_kernel(core, e_ref, own_ref, other_ref, p_ref):
    c = core[0]
    sides = [
        (split(jnp.concatenate([rows_of(e_ref, first + k) for k in range(4)], axis=1)), v_ref)
        for v_ref, first in ((own_ref, 4 * c), (other_ref, 4 - 4 * c))
    ]
    for n in range(4):
        total = sum(dot3(left, split(v_ref[:, n * WIDE : (n + 1) * WIDE])) for left, v_ref in sides)
        for h in range(2):
            for r in range(4):
                p_ref[pl.ds((2 * n + h) * 4 + r, 64, stride=32), :] = total[
                    r * 64 : (r + 1) * 64, h * 128 : (h + 1) * 128
                ]


def project(core, e, own, other):
    return pl.pallas_call(
        project_kernel,
        out_shape=jax.ShapeDtypeStruct((2048, 128), F32),
        in_specs=[smem(), vmem(), vmem(), vmem()],
        out_specs=vmem(),
        compiler_params=params(),
        cost_estimate=pl.CostEstimate(flops=2 * 10**9, bytes_accessed=6 << 20, transcendentals=0),
        name="project",
    )(core, e, own, other)


def update_kernel(core, e_ref, w_ref, own_ref, other_ref, o_ref):
    c = core[0]
    left = split(jnp.concatenate([rows_of(w_ref, n) for n in range(8)], axis=1))
    for v_ref, first in ((own_ref, 4 * c), (other_ref, 4 - 4 * c)):
        for k in range(2):
            change = dot3(left, split(v_ref[k * WIDE : (k + 1) * WIDE, :]), NT)
            for h in range(2):
                j = first + 2 * k + h
                for r in range(4):
                    before = e_ref[pl.ds(j * 4 + r, 64, stride=e_ref.shape[0] // 64), :]
                    part = change[r * 64 : (r + 1) * 64, h * 128 : (h + 1) * 128]
                    o_ref[pl.ds(j * 4 + r, 64, stride=32), :] = before - part


def update(core, e, w, own, other):
    return pl.pallas_call(
        update_kernel,
        out_shape=jax.ShapeDtypeStruct((2048, 128), F32),
        in_specs=[smem(), vmem(), vmem(), vmem(), vmem()],
        out_specs=vmem(),
        compiler_params=params(),
        cost_estimate=pl.CostEstimate(flops=2 * 10**9, bytes_accessed=7 << 20, transcendentals=0),
        name="update",
    )(core, e, w, own, other)


def finish_kernel(t_ref, o_ref):
    count = o_ref.shape[1] // 128
    first = pl.program_id(0) * count
    for t in range(count):
        o_ref[:, t * 128 : (t + 1) * 128] = t_ref[first + t]


def to_chips(a):
    return lax.all_to_all(a, CHIPS, split_axis=0, concat_axis=0, tiled=True)


def swap_cores(a):
    return lax.ppermute(a, "c", [(0, 1), (1, 0)])


def body(eigvecs, reflectors, offsets, lengths, panels):
    core = lax.axis_index("c").astype(jnp.int32).reshape(1)
    other = swap_cores(panels)
    parts = to_chips(gram_more(core, other, gram(core, panels)).reshape(64, SHARE // 4, 4, 128))
    tiles = eigvecs.reshape(4, 512, 128).transpose(1, 0, 2)
    chased = chase(tiles, reflectors, offsets, lengths)
    mine = to_chips(share(chased.reshape(64, 8, 4, 128), parts)).reshape(64 * (32 + SHARE), 128)
    half = compact(mine)
    theirs = swap_cores(half)
    projected = to_chips(project(core, mine, panels, other).reshape(64, 32, 128))
    weights = to_chips(solve(core, half, theirs, projected)).reshape(2048, 128)
    result = to_chips(update(core, mine, weights, panels, other).reshape(64, 32, 128))
    return pl.pallas_call(
        finish_kernel,
        out_shape=jax.ShapeDtypeStruct((4, 65536), F32),
        grid=(2,),
        in_specs=[vmem()],
        out_specs=pl.BlockSpec((4, 32768), lambda i: (0, i)),
        compiler_params=params(),
        cost_estimate=pl.CostEstimate(flops=0, bytes_accessed=2 << 20, transcendentals=0),
        name="finish",
    )(result.reshape(512, 4, 128))


def solution(mesh):
    fine = Mesh(mesh.devices.reshape(2, 4, 2, 4, 2), AXES)
    return jax.shard_map(
        body,
        mesh=fine,
        in_specs=(P(AXES, None), P(), P(), P(), P(AXES, None)),
        out_specs=P(AXES, None),
        check_vma=False,
    )
```

```python
import jax
import jax.numpy as jnp
from jax import lax
from jax.experimental import pallas as pl
from jax.experimental.pallas import tpu as pltpu
from jax.sharding import Mesh, PartitionSpec as P

F32 = jnp.float32
BF16 = jnp.bfloat16
AXES = ("yh", "x", "yl", "z", "c")
CHIPS = ("yh", "x", "yl", "z")
VMEM_LIMIT = 20 * 1024 * 1024
LARGE = 58 * 1024 * 1024

NN = (((1,), (0,)), ((), ()))
NT = (((1,), (1,)), ((), ()))
TN = (((0,), (0,)), ((), ()))


def dg(a, b, dims=NN):
    return lax.dot_general(a, b, dims, preferred_element_type=F32)


def split(a):
    high = a.astype(BF16)
    low = (a - high.astype(F32)).astype(BF16)
    return high, low


def dot3(a, b, dims=NN):
    (ah, al), (bh, bl) = a, b
    return dg(ah, bh, dims) + (dg(ah, bl, dims) + dg(al, bh, dims))


def dot4(a, b):
    n = b[0].shape[1]
    right = jnp.concatenate(b, axis=1)
    both = dg(jnp.concatenate(a, axis=1), jnp.concatenate([right, right], axis=0))
    return both[:, :n] + both[:, n:]


def dot4_nt(a, b):
    n = b[0].shape[0]
    right = jnp.concatenate(b, axis=0)
    both = dg(jnp.concatenate(a, axis=1), jnp.concatenate([right, right], axis=1), NT)
    return both[:, :n] + both[:, n:]


def iotas(n):
    return (
        lax.broadcasted_iota(jnp.int32, (n, n), 0),
        lax.broadcasted_iota(jnp.int32, (n, n), 1),
    )


def inverse_of_half(grams):
    stages = inverse_stages(grams)
    while True:
        try:
            next(stages)
        except StopIteration as end:
            return end.value


def inverse_stages(grams):
    n = grams[0].shape[0]
    row, col = iotas(n)
    eye = (row == col).astype(F32)
    upper = row < col
    inverses, strict, scale = [], [], []
    for gram in grams:
        diagonal = gram * (0.5 * eye)
        by_row = jnp.sum(diagonal, axis=1, keepdims=True)
        by_col = jnp.sum(diagonal, axis=0, keepdims=True)
        nil = jnp.where(upper, gram / by_row, 0.0)
        strict.append(nil)
        scale.append(1.0 / by_col)
        first = ((row ^ col) == 1) & ((row & 1) == 0)
        inverses.append(eye - jnp.where(first, nil, 0.0))
    size = 2
    while size < n:
        corner = ((row // (2 * size)) == (col // (2 * size))) & ((row & size) == 0) & ((col & size) != 0)
        halves = [split(x) for x in inverses]
        corners = [split(jnp.where(corner, nil, 0.0)) for nil in strict]
        middles = [split(dot4(x, m)) for x, m in zip(halves, corners)]
        yield
        inverses = [x - dot4(y, h) for x, y, h in zip(inverses, middles, halves)]
        size *= 2
        yield
    return [x * s for x, s in zip(inverses, scale)]


TOGETHER = 8
EVERY = 2


def gram_of(m):
    width = m[0].shape[1]
    both = dg(m[0], jnp.concatenate(m, axis=1), TN)
    return both[:, :width] + both[:, width:] + dg(m[1], m[0], TN)


def chase_kernel(offsets, lengths, e_hbm, m_hbm, o_hbm, e_ref, m_ref, kh_ref, kl_ref, sems):
    blocks, extent, width = m_ref.shape
    tiles, rows = e_ref.shape[0], e_ref.shape[1]
    groups = blocks // TOGETHER
    loads = [
        pltpu.make_async_copy(
            m_hbm.at[pl.ds(g * TOGETHER, TOGETHER)], m_ref.at[pl.ds(g * TOGETHER, TOGETHER)], sems.at[g]
        )
        for g in range(groups)
    ]
    load_e = pltpu.make_async_copy(e_hbm, e_ref, sems.at[groups])
    loads[0].start()
    load_e.start()
    for load in loads[1:]:
        load.start()
    row = lax.broadcasted_iota(jnp.int32, (extent, width), 0)
    lane = lax.broadcasted_iota(jnp.int32, (rows, 128), 1)

    def prepare(group):
        at = [group * TOGETHER + u for u in range(TOGETHER)]
        masked = [split(jnp.where(row < lengths[b], m_ref[b], 0.0)) for b in at]
        grams = [gram_of(m) for m in masked]
        yield
        inverses = yield from inverse_stages(grams)
        lefts = [split(dot4_nt(m, split(f))) for m, f in zip(masked, inverses)]
        yield
        for left, m, b in zip(lefts, masked, at):
            kh_ref[b], kl_ref[b] = split(dot4_nt(left, m))

    def step(b):
        offset = offsets[b]
        tile = jnp.minimum(offset // 128, tiles - 3)
        shift = offset - tile * 128
        v0, v1, v2 = e_ref[tile], e_ref[tile + 1], e_ref[tile + 2]
        left = (128 - shift) & 127
        r0 = pltpu.roll(v0, left, 1)
        r1 = pltpu.roll(v1, left, 1)
        r2 = pltpu.roll(v2, left, 1)
        inside = lane < 128 - shift
        window = jnp.concatenate([jnp.where(inside, r0, r1), jnp.where(inside, r1, r2)], axis=1)
        high = window.astype(BF16).astype(F32)
        both = jnp.concatenate([high, window - high], axis=0).astype(BF16)
        change = dg(both, kh_ref[b]) + dg(both, kl_ref[b])
        change = change[:rows] + change[rows:]
        right = shift & 127
        q0 = pltpu.roll(change[:, :128], right, 1)
        q1 = pltpu.roll(change[:, 128:], right, 1)
        after = lane >= shift
        e_ref[tile] = v0 - jnp.where(after, q0, 0.0)
        e_ref[tile + 1] = v1 - jnp.where(after, q1, q0)
        e_ref[tile + 2] = v2 - jnp.where(after, 0.0, q1)

    loads[0].wait()
    for stage in prepare(0):
        pass
    load_e.wait()
    for load in loads[1:]:
        load.wait()
    for group in range(1, groups):
        waiting = list(range((group - 1) * TOGETHER, group * TOGETHER))
        for at, stage in enumerate(prepare(group)):
            if waiting and at % EVERY == 0:
                step(waiting.pop(0))
        for b in waiting:
            step(b)
    for u in range(TOGETHER):
        step((groups - 1) * TOGETHER + u)
    store = pltpu.make_async_copy(e_ref, o_hbm, sems.at[groups + 1])
    store.start()
    store.wait()


def share_kernel(e_hbm, g_ref, o_ref, sem):
    copy = pltpu.make_async_copy(e_hbm, o_ref.at[:, pl.ds(0, 8)], sem)
    copy.start()
    chips, count = g_ref.shape[0], g_ref.shape[1]
    sums = [g_ref[k] for k in range(4)]
    for s in range(4, chips):
        sums[s % 4] = sums[s % 4] + g_ref[s]
    total = (sums[0] + sums[1]) + (sums[2] + sums[3])
    for s in range(chips):
        o_ref[s, 8:] = total
    copy.wait()


def vmem():
    return pl.BlockSpec(memory_space=pltpu.VMEM)


def smem():
    return pl.BlockSpec(memory_space=pltpu.SMEM)


def params():
    return pltpu.CompilerParams(vmem_limit_bytes=VMEM_LIMIT)


def hbm():
    return pl.BlockSpec(memory_space=pltpu.HBM)


def chase(tiles, reflectors, offsets, lengths):
    blocks, extent, width = reflectors.shape
    return pl.pallas_call(
        chase_kernel,
        out_shape=jax.ShapeDtypeStruct(tiles.shape, F32),
        in_specs=[smem(), smem()] + [hbm()] * 2,
        out_specs=hbm(),
        scratch_shapes=[pltpu.VMEM(tiles.shape, F32), pltpu.VMEM(reflectors.shape, F32)]
        + [pltpu.VMEM((blocks, extent, extent), BF16)] * 2
        + [pltpu.SemaphoreType.DMA((blocks // TOGETHER + 2,))],
        compiler_params=pltpu.CompilerParams(vmem_limit_bytes=LARGE),
        cost_estimate=pl.CostEstimate(flops=20 * 10**9, bytes_accessed=7 << 20, transcendentals=0),
        name="chase",
    )(offsets, lengths, tiles, reflectors)


def share(chased, parts):
    return pl.pallas_call(
        share_kernel,
        out_shape=jax.ShapeDtypeStruct((64, 8 + SHARE // 4, 4, 128), F32),
        in_specs=[hbm(), vmem()],
        out_specs=vmem(),
        scratch_shapes=[pltpu.SemaphoreType.DMA],
        compiler_params=pltpu.CompilerParams(vmem_limit_bytes=20 * 1024 * 1024),
        cost_estimate=pl.CostEstimate(flops=10**6, bytes_accessed=5 << 20, transcendentals=0),
        name="share",
    )(chased, parts)


WIDE = 256
ORDER = ((0, 1, 2, 3), (2, 0, 3, 1))
LOCAL = ((0, 1), (1, 2), (2, 3), (1, 1), (2, 2))
MADE = [(ORDER[c][i], ORDER[c][j]) for c in range(2) for (i, j) in LOCAL]
SENT = [(WIDE // 2 if i == j else WIDE, WIDE) for (i, j) in LOCAL]
STARTS = [sum(map(sum, SENT[:at])) for at in range(len(LOCAL) + 1)]
SHARE = STARTS[-1] // 64


def gram_blocks(core, v_ref):
    c = core[0]
    order = (2 * c, 1 - c, 2 + c, 3 - 2 * c)
    halves = [split(v_ref[:, pl.ds(pl.multiple_of(o * WIDE, WIDE), WIDE)]) for o in order]
    for at, (i, j) in enumerate(LOCAL):
        block = dot3(halves[i], halves[j], TN)
        start = STARTS[at]
        for h, count in enumerate(SENT[at]):
            yield pl.ds(start, count), block[:count, h * 128 : (h + 1) * 128]
            start += count


def gram_kernel(core, v_ref, g_ref):
    for rows, part in gram_blocks(core, v_ref):
        g_ref[rows, :] = part


def gram_more_kernel(core, v_ref, before_ref, g_hbm, g_ref, sems):
    copies = []
    for rows, part in gram_blocks(core, v_ref):
        g_ref[rows, :] = before_ref[rows, :] + part
        copies.append(pltpu.make_async_copy(g_ref.at[rows], g_hbm.at[rows], sems.at[len(copies)]))
        copies[-1].start()
    for copy in copies:
        copy.wait()


def gram(core, panels):
    return pl.pallas_call(
        gram_kernel,
        out_shape=jax.ShapeDtypeStruct((STARTS[-1], 128), F32),
        in_specs=[smem(), vmem()],
        out_specs=vmem(),
        compiler_params=params(),
        cost_estimate=pl.CostEstimate(flops=10**9, bytes_accessed=3 << 20, transcendentals=0),
        name="gram",
    )(core, panels)


def gram_more(core, panels, before):
    return pl.pallas_call(
        gram_more_kernel,
        out_shape=jax.ShapeDtypeStruct((STARTS[-1], 128), F32),
        in_specs=[smem(), vmem(), vmem()],
        out_specs=hbm(),
        scratch_shapes=[
            pltpu.VMEM((STARTS[-1], 128), F32),
            pltpu.SemaphoreType.DMA((2 * len(LOCAL),)),
        ],
        compiler_params=params(),
        cost_estimate=pl.CostEstimate(flops=10**9, bytes_accessed=4 << 20, transcendentals=0),
        name="gram_more",
    )(core, panels, before)


def gram_block(ref, local):
    left, right = SENT[local]
    start = STARTS[local]
    first = ref[pl.ds(start, left), :]
    if left < right:
        first = jnp.concatenate([first, jnp.zeros((right - left, 128), F32)], axis=0)
    return jnp.concatenate([first, ref[pl.ds(start + left, right), :]], axis=1)


def solve_kernel(core, own_ref, other_ref, p_ref, w_ref):
    diagonals, others = [None] * 4, {}
    first = core[0] == 0
    pairs = [(gram_block(own_ref, k), gram_block(other_ref, k)) for k in range(len(LOCAL))]
    values = [jnp.where(first, a, b) for a, b in pairs] + [jnp.where(first, b, a) for a, b in pairs]
    for value, (i, j) in zip(values, MADE):
        if i == j:
            diagonals[i] = value
        else:
            others[min(i, j), max(i, j)] = split(value.T if i < j else value)
    small = []
    for d in diagonals:
        small.extend([d[:128, :128], d[128:, 128:]])
    inverses = inverse_of_half(small)
    transposed = []
    for p, d in enumerate(diagonals):
        a, c = inverses[2 * p], inverses[2 * p + 1]
        corner = -dot4(split(dot4(split(a), split(d[:128, 128:]))), split(c))
        top = jnp.concatenate([a.T, jnp.zeros((128, 128), F32)], axis=1)
        transposed.append(split(jnp.concatenate([top, jnp.concatenate([corner.T, c.T], axis=1)], axis=0)))

    sums = [p_ref[k] for k in range(4)]
    for s in range(4, p_ref.shape[0]):
        sums[s % 4] = sums[s % 4] + p_ref[s]
    total = (sums[0] + sums[1]) + (sums[2] + sums[3])
    rest = [
        jnp.concatenate([total[8 * p : 8 * p + 4], total[8 * p + 4 : 8 * p + 8]], axis=1)
        for p in range(4)
    ]

    def times(a, b):
        high = a.astype(BF16).astype(F32)
        both = jnp.concatenate([high, a - high], axis=0).astype(BF16)
        product = dg(both, b[0]) + dg(both, b[1])
        return product[:4] + product[4:]

    pieces = [None] * 4
    for q in range(3, -1, -1):
        solved = times(rest[q], transposed[q])
        pieces[q] = jnp.concatenate([solved[:, :128], solved[:, 128:]], axis=0)
        for p in range(q):
            rest[p] = rest[p] - times(solved, others[p, q])
    result = jnp.concatenate(pieces, axis=0)
    w_ref[...] = jnp.broadcast_to(result[None], w_ref.shape)


def solve(core, own, other, p):
    return pl.pallas_call(
        solve_kernel,
        out_shape=jax.ShapeDtypeStruct(p.shape, F32),
        in_specs=[smem()] + [vmem()] * 3,
        out_specs=vmem(),
        compiler_params=params(),
        cost_estimate=pl.CostEstimate(flops=4 * 10**9, bytes_accessed=5 << 20, transcendentals=0),
        name="solve",
    )(core, own, other, p)


def rows_of(ref, j):
    stride = ref.shape[0] // 64
    return jnp.concatenate([ref[pl.ds(j * 4 + r, 64, stride=stride), :] for r in range(4)], axis=0)


def compact_kernel(e_ref, own_ref, half_ref):
    stride = 32 + SHARE
    for s in range(64):
        half_ref[s * SHARE : (s + 1) * SHARE, :] = e_ref[s * stride + 32 : (s + 1) * stride, :]


def compact(e, own):
    return pl.pallas_call(
        compact_kernel,
        out_shape=jax.ShapeDtypeStruct((STARTS[-1], 128), F32),
        in_specs=[vmem()] * 2,
        out_specs=vmem(),
        compiler_params=params(),
        cost_estimate=pl.CostEstimate(flops=0, bytes_accessed=6 << 20, transcendentals=0),
        name="compact",
    )(e, own)


def project_kernel(core, e_ref, own_ref, other_ref, p_ref):
    c = core[0]
    sides = [
        (split(jnp.concatenate([rows_of(e_ref, first + k) for k in range(4)], axis=1)), v_ref)
        for v_ref, first in ((own_ref, 4 * c), (other_ref, 4 - 4 * c))
    ]
    for n in range(4):
        total = sum(dot3(left, split(v_ref[:, n * WIDE : (n + 1) * WIDE])) for left, v_ref in sides)
        for h in range(2):
            for r in range(4):
                p_ref[pl.ds((2 * n + h) * 4 + r, 64, stride=32), :] = total[
                    r * 64 : (r + 1) * 64, h * 128 : (h + 1) * 128
                ]


def project(core, e, own, other):
    return pl.pallas_call(
        project_kernel,
        out_shape=jax.ShapeDtypeStruct((2048, 128), F32),
        in_specs=[smem(), vmem(), vmem(), vmem()],
        out_specs=vmem(),
        compiler_params=params(),
        cost_estimate=pl.CostEstimate(flops=2 * 10**9, bytes_accessed=6 << 20, transcendentals=0),
        name="project",
    )(core, e, own, other)


def update_kernel(core, e_ref, w_ref, own_ref, other_ref, o_ref):
    c = core[0]
    left = split(jnp.concatenate([rows_of(w_ref, n) for n in range(8)], axis=1))
    for v_ref, first in ((own_ref, 4 * c), (other_ref, 4 - 4 * c)):
        for k in range(2):
            change = dot3(left, split(v_ref[k * WIDE : (k + 1) * WIDE, :]), NT)
            for h in range(2):
                j = first + 2 * k + h
                for r in range(4):
                    before = e_ref[pl.ds(j * 4 + r, 64, stride=e_ref.shape[0] // 64), :]
                    part = change[r * 64 : (r + 1) * 64, h * 128 : (h + 1) * 128]
                    o_ref[pl.ds(j * 4 + r, 64, stride=32), :] = before - part


def update(core, e, w, own, other):
    return pl.pallas_call(
        update_kernel,
        out_shape=jax.ShapeDtypeStruct((2048, 128), F32),
        in_specs=[smem(), vmem(), vmem(), vmem(), vmem()],
        out_specs=vmem(),
        compiler_params=params(),
        cost_estimate=pl.CostEstimate(flops=2 * 10**9, bytes_accessed=7 << 20, transcendentals=0),
        name="update",
    )(core, e, w, own, other)


def finish_kernel(t_ref, o_ref):
    count = o_ref.shape[1] // 128
    first = pl.program_id(0) * count
    for t in range(count):
        o_ref[:, t * 128 : (t + 1) * 128] = t_ref[first + t]


def to_chips(a):
    return lax.all_to_all(a, CHIPS, split_axis=0, concat_axis=0, tiled=True)


def swap_cores(a):
    return lax.ppermute(a, "c", [(0, 1), (1, 0)])


def body(eigvecs, reflectors, offsets, lengths, panels):
    core = lax.axis_index("c").astype(jnp.int32).reshape(1)
    other = swap_cores(panels)
    parts = to_chips(gram_more(core, other, gram(core, panels)).reshape(64, SHARE // 4, 4, 128))
    tiles = eigvecs.reshape(4, 512, 128).transpose(1, 0, 2)
    chased = chase(tiles, reflectors, offsets, lengths)
    mine = to_chips(share(chased.reshape(64, 8, 4, 128), parts)).reshape(64 * (32 + SHARE), 128)
    half = compact(mine, panels)
    theirs = swap_cores(half)
    projected = to_chips(project(core, mine, panels, other).reshape(64, 32, 128))
    weights = to_chips(solve(core, half, theirs, projected)).reshape(2048, 128)
    result = to_chips(update(core, mine, weights, panels, other).reshape(64, 32, 128))
    return pl.pallas_call(
        finish_kernel,
        out_shape=jax.ShapeDtypeStruct((4, 65536), F32),
        grid=(2,),
        in_specs=[vmem()],
        out_specs=pl.BlockSpec((4, 32768), lambda i: (0, i)),
        compiler_params=params(),
        cost_estimate=pl.CostEstimate(flops=0, bytes_accessed=2 << 20, transcendentals=0),
        name="finish",
    )(result.reshape(512, 4, 128))


def solution(mesh):
    fine = Mesh(mesh.devices.reshape(2, 4, 2, 4, 2), AXES)
    return jax.shard_map(
        body,
        mesh=fine,
        in_specs=(P(AXES, None), P(), P(), P(), P(AXES, None)),
        out_specs=P(AXES, None),
        check_vma=False,
    )
```

```python
import jax
import jax.numpy as jnp
from jax import lax
from jax.experimental import pallas as pl
from jax.experimental.pallas import tpu as pltpu
from jax.sharding import Mesh, PartitionSpec as P

F32 = jnp.float32
BF16 = jnp.bfloat16
AXES = ("yh", "x", "yl", "z", "c")
CHIPS = ("yh", "x", "yl", "z")
VMEM_LIMIT = 20 * 1024 * 1024
LARGE = 58 * 1024 * 1024

NN = (((1,), (0,)), ((), ()))
NT = (((1,), (1,)), ((), ()))
TN = (((0,), (0,)), ((), ()))


def dg(a, b, dims=NN):
    return lax.dot_general(a, b, dims, preferred_element_type=F32)


def split(a):
    high = a.astype(BF16)
    low = (a - high.astype(F32)).astype(BF16)
    return high, low


def dot3(a, b, dims=NN):
    (ah, al), (bh, bl) = a, b
    return dg(ah, bh, dims) + (dg(ah, bl, dims) + dg(al, bh, dims))


def dot4(a, b):
    n = b[0].shape[1]
    right = jnp.concatenate(b, axis=1)
    both = dg(jnp.concatenate(a, axis=1), jnp.concatenate([right, right], axis=0))
    return both[:, :n] + both[:, n:]


def dot4_nt(a, b):
    n = b[0].shape[0]
    right = jnp.concatenate(b, axis=0)
    both = dg(jnp.concatenate(a, axis=1), jnp.concatenate([right, right], axis=1), NT)
    return both[:, :n] + both[:, n:]


def iotas(n):
    return (
        lax.broadcasted_iota(jnp.int32, (n, n), 0),
        lax.broadcasted_iota(jnp.int32, (n, n), 1),
    )


def inverse_of_half(grams):
    stages = inverse_stages(grams)
    while True:
        try:
            next(stages)
        except StopIteration as end:
            return end.value


def inverse_stages(grams):
    n = grams[0].shape[0]
    row, col = iotas(n)
    eye = (row == col).astype(F32)
    upper = row < col
    inverses, strict, scale = [], [], []
    for gram in grams:
        diagonal = gram * (0.5 * eye)
        by_row = jnp.sum(diagonal, axis=1, keepdims=True)
        by_col = jnp.sum(diagonal, axis=0, keepdims=True)
        nil = jnp.where(upper, gram / by_row, 0.0)
        strict.append(nil)
        scale.append(1.0 / by_col)
        first = ((row ^ col) == 1) & ((row & 1) == 0)
        inverses.append(eye - jnp.where(first, nil, 0.0))
    size = 2
    while size < n:
        corner = ((row // (2 * size)) == (col // (2 * size))) & ((row & size) == 0) & ((col & size) != 0)
        halves = [split(x) for x in inverses]
        corners = [split(jnp.where(corner, nil, 0.0)) for nil in strict]
        middles = [split(dot4(x, m)) for x, m in zip(halves, corners)]
        yield
        inverses = [x - dot4(y, h) for x, y, h in zip(inverses, middles, halves)]
        size *= 2
        yield
    return [x * s for x, s in zip(inverses, scale)]


TOGETHER = 8
EVERY = 2


def gram_of(m):
    width = m[0].shape[1]
    both = dg(m[0], jnp.concatenate(m, axis=1), TN)
    return both[:, :width] + both[:, width:] + dg(m[1], m[0], TN)


def chase_kernel(offsets, lengths, e_hbm, m_hbm, o_hbm, e_ref, m_ref, kh_ref, kl_ref, sems):
    blocks, extent, width = m_ref.shape
    tiles, rows = e_ref.shape[0], e_ref.shape[1]
    groups = blocks // TOGETHER
    loads = [
        pltpu.make_async_copy(
            m_hbm.at[pl.ds(g * TOGETHER, TOGETHER)], m_ref.at[pl.ds(g * TOGETHER, TOGETHER)], sems.at[g]
        )
        for g in range(groups)
    ]
    load_e = pltpu.make_async_copy(e_hbm, e_ref, sems.at[groups])
    loads[0].start()
    load_e.start()
    for load in loads[1:]:
        load.start()
    row = lax.broadcasted_iota(jnp.int32, (extent, width), 0)
    lane = lax.broadcasted_iota(jnp.int32, (rows, 128), 1)

    def prepare(group):
        at = [group * TOGETHER + u for u in range(TOGETHER)]
        masked = [split(jnp.where(row < lengths[b], m_ref[b], 0.0)) for b in at]
        grams = [gram_of(m) for m in masked]
        yield
        inverses = yield from inverse_stages(grams)
        lefts = [split(dot4_nt(m, split(f))) for m, f in zip(masked, inverses)]
        yield
        for left, m, b in zip(lefts, masked, at):
            kh_ref[b], kl_ref[b] = split(dot4_nt(left, m))

    def step(b):
        offset = offsets[b]
        tile = jnp.minimum(offset // 128, tiles - 3)
        shift = offset - tile * 128
        v0, v1, v2 = e_ref[tile], e_ref[tile + 1], e_ref[tile + 2]
        left = (128 - shift) & 127
        r0 = pltpu.roll(v0, left, 1)
        r1 = pltpu.roll(v1, left, 1)
        r2 = pltpu.roll(v2, left, 1)
        inside = lane < 128 - shift
        window = jnp.concatenate([jnp.where(inside, r0, r1), jnp.where(inside, r1, r2)], axis=1)
        high = window.astype(BF16).astype(F32)
        both = jnp.concatenate([high, window - high], axis=0).astype(BF16)
        change = dg(both, kh_ref[b]) + dg(both, kl_ref[b])
        change = change[:rows] + change[rows:]
        right = shift & 127
        q0 = pltpu.roll(change[:, :128], right, 1)
        q1 = pltpu.roll(change[:, 128:], right, 1)
        after = lane >= shift
        e_ref[tile] = v0 - jnp.where(after, q0, 0.0)
        e_ref[tile + 1] = v1 - jnp.where(after, q1, q0)
        e_ref[tile + 2] = v2 - jnp.where(after, 0.0, q1)

    loads[0].wait()
    for stage in prepare(0):
        pass
    load_e.wait()
    for load in loads[1:]:
        load.wait()
    for group in range(1, groups):
        waiting = list(range((group - 1) * TOGETHER, group * TOGETHER))
        for at, stage in enumerate(prepare(group)):
            if waiting and at % EVERY == 0:
                step(waiting.pop(0))
        for b in waiting:
            step(b)
    for u in range(TOGETHER):
        step((groups - 1) * TOGETHER + u)
    store = pltpu.make_async_copy(e_ref, o_hbm, sems.at[groups + 1])
    store.start()
    store.wait()


def share_kernel(e_hbm, g_ref, o_ref, sem):
    copy = pltpu.make_async_copy(e_hbm, o_ref.at[:, pl.ds(0, 8)], sem)
    copy.start()
    chips, count = g_ref.shape[0], g_ref.shape[1]
    sums = [g_ref[k] for k in range(4)]
    for s in range(4, chips):
        sums[s % 4] = sums[s % 4] + g_ref[s]
    total = (sums[0] + sums[1]) + (sums[2] + sums[3])
    for s in range(chips):
        o_ref[s, 8:] = total
    copy.wait()


def vmem():
    return pl.BlockSpec(memory_space=pltpu.VMEM)


def smem():
    return pl.BlockSpec(memory_space=pltpu.SMEM)


def params():
    return pltpu.CompilerParams(vmem_limit_bytes=VMEM_LIMIT)


def hbm():
    return pl.BlockSpec(memory_space=pltpu.HBM)


def chase(tiles, reflectors, offsets, lengths):
    blocks, extent, width = reflectors.shape
    return pl.pallas_call(
        chase_kernel,
        out_shape=jax.ShapeDtypeStruct(tiles.shape, F32),
        in_specs=[smem(), smem()] + [hbm()] * 2,
        out_specs=hbm(),
        scratch_shapes=[pltpu.VMEM(tiles.shape, F32), pltpu.VMEM(reflectors.shape, F32)]
        + [pltpu.VMEM((blocks, extent, extent), BF16)] * 2
        + [pltpu.SemaphoreType.DMA((blocks // TOGETHER + 2,))],
        compiler_params=pltpu.CompilerParams(vmem_limit_bytes=LARGE),
        cost_estimate=pl.CostEstimate(flops=20 * 10**9, bytes_accessed=7 << 20, transcendentals=0),
        name="chase",
    )(offsets, lengths, tiles, reflectors)


def share(chased, parts):
    return pl.pallas_call(
        share_kernel,
        out_shape=jax.ShapeDtypeStruct((64, 8 + SHARE // 4, 4, 128), F32),
        in_specs=[hbm(), vmem()],
        out_specs=vmem(),
        scratch_shapes=[pltpu.SemaphoreType.DMA],
        compiler_params=pltpu.CompilerParams(vmem_limit_bytes=20 * 1024 * 1024),
        cost_estimate=pl.CostEstimate(flops=10**6, bytes_accessed=5 << 20, transcendentals=0),
        name="share",
    )(chased, parts)


WIDE = 256
ORDER = ((0, 1, 2, 3), (2, 0, 3, 1))
LOCAL = ((0, 1), (1, 2), (2, 3), (1, 1), (2, 2))
MADE = [(ORDER[c][i], ORDER[c][j]) for c in range(2) for (i, j) in LOCAL]
SENT = [(WIDE // 2 if i == j else WIDE, WIDE) for (i, j) in LOCAL]
STARTS = [sum(map(sum, SENT[:at])) for at in range(len(LOCAL) + 1)]
SHARE = STARTS[-1] // 64


def gram_blocks(core, v_ref):
    c = core[0]
    order = (2 * c, 1 - c, 2 + c, 3 - 2 * c)
    halves = [split(v_ref[:, pl.ds(pl.multiple_of(o * WIDE, WIDE), WIDE)]) for o in order]
    for at, (i, j) in enumerate(LOCAL):
        block = dot3(halves[i], halves[j], TN)
        start = STARTS[at]
        for h, count in enumerate(SENT[at]):
            yield pl.ds(start, count), block[:count, h * 128 : (h + 1) * 128]
            start += count


def gram_kernel(core, v_ref, g_ref):
    for rows, part in gram_blocks(core, v_ref):
        g_ref[rows, :] = part


def gram_more_kernel(core, v_ref, before_ref, g_hbm, g_ref, sems):
    copies = []
    for rows, part in gram_blocks(core, v_ref):
        g_ref[rows, :] = before_ref[rows, :] + part
        copies.append(pltpu.make_async_copy(g_ref.at[rows], g_hbm.at[rows], sems.at[len(copies)]))
        copies[-1].start()
    for copy in copies:
        copy.wait()


def gram(core, panels):
    return pl.pallas_call(
        gram_kernel,
        out_shape=jax.ShapeDtypeStruct((STARTS[-1], 128), F32),
        in_specs=[smem(), vmem()],
        out_specs=vmem(),
        compiler_params=params(),
        cost_estimate=pl.CostEstimate(flops=10**9, bytes_accessed=3 << 20, transcendentals=0),
        name="gram",
    )(core, panels)


def gram_more(core, panels, before):
    return pl.pallas_call(
        gram_more_kernel,
        out_shape=jax.ShapeDtypeStruct((STARTS[-1], 128), F32),
        in_specs=[smem(), vmem(), vmem()],
        out_specs=hbm(),
        scratch_shapes=[
            pltpu.VMEM((STARTS[-1], 128), F32),
            pltpu.SemaphoreType.DMA((2 * len(LOCAL),)),
        ],
        compiler_params=params(),
        cost_estimate=pl.CostEstimate(flops=10**9, bytes_accessed=4 << 20, transcendentals=0),
        name="gram_more",
    )(core, panels, before)


def gram_block(ref, local):
    left, right = SENT[local]
    start = STARTS[local]
    first = ref[pl.ds(start, left), :]
    if left < right:
        first = jnp.concatenate([first, jnp.zeros((right - left, 128), F32)], axis=0)
    return jnp.concatenate([first, ref[pl.ds(start + left, right), :]], axis=1)


def solve_kernel(core, own_ref, other_ref, p_ref, w_ref):
    diagonals, others = [None] * 4, {}
    first = core[0] == 0
    pairs = [(gram_block(own_ref, k), gram_block(other_ref, k)) for k in range(len(LOCAL))]
    values = [jnp.where(first, a, b) for a, b in pairs] + [jnp.where(first, b, a) for a, b in pairs]
    for value, (i, j) in zip(values, MADE):
        if i == j:
            diagonals[i] = value
        else:
            others[min(i, j), max(i, j)] = split(value.T if i < j else value)
    small = []
    for d in diagonals:
        small.extend([d[:128, :128], d[128:, 128:]])
    inverses = inverse_of_half(small)
    transposed = []
    for p, d in enumerate(diagonals):
        a, c = inverses[2 * p], inverses[2 * p + 1]
        corner = -dot4(split(dot4(split(a), split(d[:128, 128:]))), split(c))
        top = jnp.concatenate([a.T, jnp.zeros((128, 128), F32)], axis=1)
        transposed.append(split(jnp.concatenate([top, jnp.concatenate([corner.T, c.T], axis=1)], axis=0)))

    sums = [p_ref[k] for k in range(4)]
    for s in range(4, p_ref.shape[0]):
        sums[s % 4] = sums[s % 4] + p_ref[s]
    total = (sums[0] + sums[1]) + (sums[2] + sums[3])
    rest = [
        jnp.concatenate([total[8 * p : 8 * p + 4], total[8 * p + 4 : 8 * p + 8]], axis=1)
        for p in range(4)
    ]

    def times(a, b):
        high = a.astype(BF16).astype(F32)
        both = jnp.concatenate([high, a - high], axis=0).astype(BF16)
        product = dg(both, b[0]) + dg(both, b[1])
        return product[:4] + product[4:]

    pieces = [None] * 4
    for q in range(3, -1, -1):
        solved = times(rest[q], transposed[q])
        pieces[q] = jnp.concatenate([solved[:, :128], solved[:, 128:]], axis=0)
        for p in range(q):
            rest[p] = rest[p] - times(solved, others[p, q])
    result = jnp.concatenate(pieces, axis=0)
    w_ref[...] = jnp.broadcast_to(result[None], w_ref.shape)


def solve(core, own, other, p):
    return pl.pallas_call(
        solve_kernel,
        out_shape=jax.ShapeDtypeStruct(p.shape, F32),
        in_specs=[smem()] + [vmem()] * 3,
        out_specs=vmem(),
        compiler_params=params(),
        cost_estimate=pl.CostEstimate(flops=4 * 10**9, bytes_accessed=5 << 20, transcendentals=0),
        name="solve",
    )(core, own, other, p)


def rows_of(ref, j):
    stride = ref.shape[0] // 64
    return jnp.concatenate([ref[pl.ds(j * 4 + r, 64, stride=stride), :] for r in range(4)], axis=0)


def compact_kernel(e_ref, own_ref, half_ref):
    stride = 32 + SHARE
    for s in range(64):
        half_ref[s * SHARE : (s + 1) * SHARE, :] = e_ref[s * stride + 32 : (s + 1) * stride, :]


def compact(e, own):
    return pl.pallas_call(
        compact_kernel,
        out_shape=jax.ShapeDtypeStruct((STARTS[-1], 128), F32),
        in_specs=[vmem()] * 2,
        out_specs=vmem(),
        compiler_params=params(),
        cost_estimate=pl.CostEstimate(flops=0, bytes_accessed=6 << 20, transcendentals=0),
        name="compact",
    )(e, own)


def project_kernel(core, e_ref, own_ref, other_ref, p_ref):
    c = core[0]
    sides = [
        (split(jnp.concatenate([rows_of(e_ref, first + k) for k in range(4)], axis=1)), v_ref)
        for v_ref, first in ((own_ref, 4 * c), (other_ref, 4 - 4 * c))
    ]
    for n in range(4):
        total = sum(dot3(left, split(v_ref[:, n * WIDE : (n + 1) * WIDE])) for left, v_ref in sides)
        for h in range(2):
            for r in range(4):
                p_ref[pl.ds((2 * n + h) * 4 + r, 64, stride=32), :] = total[
                    r * 64 : (r + 1) * 64, h * 128 : (h + 1) * 128
                ]


def project(core, e, own, other):
    return pl.pallas_call(
        project_kernel,
        out_shape=jax.ShapeDtypeStruct((2048, 128), F32),
        in_specs=[smem(), vmem(), vmem(), vmem()],
        out_specs=vmem(),
        compiler_params=params(),
        cost_estimate=pl.CostEstimate(flops=2 * 10**9, bytes_accessed=6 << 20, transcendentals=0),
        name="project",
    )(core, e, own, other)


def update_kernel(core, e_ref, w_ref, own_ref, other_ref, o_ref):
    c = core[0]
    left = split(jnp.concatenate([rows_of(w_ref, n) for n in range(8)], axis=1))
    for v_ref, first in ((own_ref, 4 * c), (other_ref, 4 - 4 * c)):
        for k in range(2):
            change = dot3(left, split(v_ref[k * WIDE : (k + 1) * WIDE, :]), NT)
            for h in range(2):
                j = first + 2 * k + h
                for r in range(4):
                    before = e_ref[pl.ds(j * 4 + r, 64, stride=e_ref.shape[0] // 64), :]
                    part = change[r * 64 : (r + 1) * 64, h * 128 : (h + 1) * 128]
                    o_ref[pl.ds(j * 4 + r, 64, stride=32), :] = before - part


def update(core, e, w, own, other):
    return pl.pallas_call(
        update_kernel,
        out_shape=jax.ShapeDtypeStruct((2048, 128), F32),
        in_specs=[smem(), vmem(), vmem(), vmem(), vmem()],
        out_specs=vmem(),
        compiler_params=params(),
        cost_estimate=pl.CostEstimate(flops=2 * 10**9, bytes_accessed=7 << 20, transcendentals=0),
        name="update",
    )(core, e, w, own, other)


def finish_kernel(t_ref, o_ref):
    count = o_ref.shape[1] // 128
    first = pl.program_id(0) * count
    for t in range(count):
        o_ref[:, t * 128 : (t + 1) * 128] = t_ref[first + t]


def to_chips(a):
    return lax.all_to_all(a, CHIPS, split_axis=0, concat_axis=0, tiled=True)


def swap_cores(a):
    return lax.ppermute(a, "c", [(0, 1), (1, 0)])


def body(eigvecs, reflectors, offsets, lengths, panels):
    core = lax.axis_index("c").astype(jnp.int32).reshape(1)
    other = swap_cores(panels)
    parts = to_chips(gram_more(core, other, gram(core, panels)).reshape(64, SHARE // 4, 4, 128))
    tiles = eigvecs.reshape(4, 512, 128).transpose(1, 0, 2)
    chased = chase(tiles, reflectors, offsets, lengths)
    mine = to_chips(share(chased.reshape(64, 8, 4, 128), parts)).reshape(64 * (32 + SHARE), 128)
    half = compact(mine, panels)
    theirs = swap_cores(half)
    projected, theirs = lax.optimization_barrier((project(core, mine, panels, other), theirs))
    projected = to_chips(projected.reshape(64, 32, 128))
    weights = to_chips(solve(core, half, theirs, projected)).reshape(2048, 128)
    result = to_chips(update(core, mine, weights, panels, other).reshape(64, 32, 128))
    return pl.pallas_call(
        finish_kernel,
        out_shape=jax.ShapeDtypeStruct((4, 65536), F32),
        grid=(2,),
        in_specs=[vmem()],
        out_specs=pl.BlockSpec((4, 32768), lambda i: (0, i)),
        compiler_params=params(),
        cost_estimate=pl.CostEstimate(flops=0, bytes_accessed=2 << 20, transcendentals=0),
        name="finish",
    )(result.reshape(512, 4, 128))


def solution(mesh):
    fine = Mesh(mesh.devices.reshape(2, 4, 2, 4, 2), AXES)
    return jax.shard_map(
        body,
        mesh=fine,
        in_specs=(P(AXES, None), P(), P(), P(), P(AXES, None)),
        out_specs=P(AXES, None),
        check_vma=False,
    )
```

```python
import jax
import jax.numpy as jnp
from jax import lax
from jax.experimental import pallas as pl
from jax.experimental.pallas import tpu as pltpu
from jax.sharding import Mesh, PartitionSpec as P

F32 = jnp.float32
BF16 = jnp.bfloat16
AXES = ("yh", "x", "yl", "z", "c")
CHIPS = ("yh", "x", "yl", "z")
STEPS = ("x", "yh", "yl", "z")
CHIP_AT = [yh * 32 + x * 8 + low for x in range(4) for yh in range(2) for low in range(8)]
VMEM_LIMIT = 20 * 1024 * 1024
LARGE = 58 * 1024 * 1024

NN = (((1,), (0,)), ((), ()))
NT = (((1,), (1,)), ((), ()))
TN = (((0,), (0,)), ((), ()))


def dg(a, b, dims=NN):
    return lax.dot_general(a, b, dims, preferred_element_type=F32)


def split(a):
    high = a.astype(BF16)
    low = (a - high.astype(F32)).astype(BF16)
    return high, low


def dot3(a, b, dims=NN):
    (ah, al), (bh, bl) = a, b
    return dg(ah, bh, dims) + (dg(ah, bl, dims) + dg(al, bh, dims))


def dot4(a, b):
    n = b[0].shape[1]
    right = jnp.concatenate(b, axis=1)
    both = dg(jnp.concatenate(a, axis=1), jnp.concatenate([right, right], axis=0))
    return both[:, :n] + both[:, n:]


def dot4_nt(a, b):
    n = b[0].shape[0]
    right = jnp.concatenate(b, axis=0)
    both = dg(jnp.concatenate(a, axis=1), jnp.concatenate([right, right], axis=1), NT)
    return both[:, :n] + both[:, n:]


def iotas(n):
    return (
        lax.broadcasted_iota(jnp.int32, (n, n), 0),
        lax.broadcasted_iota(jnp.int32, (n, n), 1),
    )


def inverse_of_half(grams):
    stages = inverse_stages(grams)
    while True:
        try:
            next(stages)
        except StopIteration as end:
            return end.value


def inverse_stages(grams):
    n = grams[0].shape[0]
    row, col = iotas(n)
    eye = (row == col).astype(F32)
    upper = row < col
    inverses, strict, scale = [], [], []
    for gram in grams:
        diagonal = gram * (0.5 * eye)
        by_row = jnp.sum(diagonal, axis=1, keepdims=True)
        by_col = jnp.sum(diagonal, axis=0, keepdims=True)
        nil = jnp.where(upper, gram / by_row, 0.0)
        strict.append(nil)
        scale.append(1.0 / by_col)
        first = ((row ^ col) == 1) & ((row & 1) == 0)
        inverses.append(eye - jnp.where(first, nil, 0.0))
    size = 2
    while size < n:
        corner = ((row // (2 * size)) == (col // (2 * size))) & ((row & size) == 0) & ((col & size) != 0)
        halves = [split(x) for x in inverses]
        corners = [split(jnp.where(corner, nil, 0.0)) for nil in strict]
        middles = [split(dot4(x, m)) for x, m in zip(halves, corners)]
        yield
        inverses = [x - dot4(y, h) for x, y, h in zip(inverses, middles, halves)]
        size *= 2
        yield
    return [x * s for x, s in zip(inverses, scale)]


TOGETHER = 8
EVERY = 2


def gram_of(m):
    width = m[0].shape[1]
    both = dg(m[0], jnp.concatenate(m, axis=1), TN)
    return both[:, :width] + both[:, width:] + dg(m[1], m[0], TN)


def chase_kernel(offsets, lengths, e_hbm, m_hbm, o_hbm, e_ref, m_ref, kh_ref, kl_ref, sems):
    blocks, extent, width = m_ref.shape
    tiles, rows = e_ref.shape[0], e_ref.shape[1]
    groups = blocks // TOGETHER
    loads = [
        pltpu.make_async_copy(
            m_hbm.at[pl.ds(g * TOGETHER, TOGETHER)], m_ref.at[pl.ds(g * TOGETHER, TOGETHER)], sems.at[g]
        )
        for g in range(groups)
    ]
    load_e = pltpu.make_async_copy(e_hbm, e_ref, sems.at[groups])
    loads[0].start()
    load_e.start()
    for load in loads[1:]:
        load.start()
    row = lax.broadcasted_iota(jnp.int32, (extent, width), 0)
    lane = lax.broadcasted_iota(jnp.int32, (rows, 128), 1)

    def prepare(group):
        at = [group * TOGETHER + u for u in range(TOGETHER)]
        masked = [split(jnp.where(row < lengths[b], m_ref[b], 0.0)) for b in at]
        grams = [gram_of(m) for m in masked]
        yield
        inverses = yield from inverse_stages(grams)
        lefts = [split(dot4_nt(m, split(f))) for m, f in zip(masked, inverses)]
        yield
        for left, m, b in zip(lefts, masked, at):
            kh_ref[b], kl_ref[b] = split(dot4_nt(left, m))

    def step(b):
        offset = offsets[b]
        tile = jnp.minimum(offset // 128, tiles - 3)
        shift = offset - tile * 128
        v0, v1, v2 = e_ref[tile], e_ref[tile + 1], e_ref[tile + 2]
        left = (128 - shift) & 127
        r0 = pltpu.roll(v0, left, 1)
        r1 = pltpu.roll(v1, left, 1)
        r2 = pltpu.roll(v2, left, 1)
        inside = lane < 128 - shift
        window = jnp.concatenate([jnp.where(inside, r0, r1), jnp.where(inside, r1, r2)], axis=1)
        high = window.astype(BF16).astype(F32)
        both = jnp.concatenate([high, window - high], axis=0).astype(BF16)
        change = dg(both, kh_ref[b]) + dg(both, kl_ref[b])
        change = change[:rows] + change[rows:]
        right = shift & 127
        q0 = pltpu.roll(change[:, :128], right, 1)
        q1 = pltpu.roll(change[:, 128:], right, 1)
        after = lane >= shift
        e_ref[tile] = v0 - jnp.where(after, q0, 0.0)
        e_ref[tile + 1] = v1 - jnp.where(after, q1, q0)
        e_ref[tile + 2] = v2 - jnp.where(after, 0.0, q1)

    loads[0].wait()
    for stage in prepare(0):
        pass
    load_e.wait()
    for load in loads[1:]:
        load.wait()
    for group in range(1, groups):
        waiting = list(range((group - 1) * TOGETHER, group * TOGETHER))
        for at, stage in enumerate(prepare(group)):
            if waiting and at % EVERY == 0:
                step(waiting.pop(0))
        for b in waiting:
            step(b)
    for u in range(TOGETHER):
        step((groups - 1) * TOGETHER + u)
    store = pltpu.make_async_copy(e_ref, o_hbm, sems.at[groups + 1])
    store.start()
    store.wait()


def share_kernel(e_hbm, g_ref, o_ref, sems):
    copies = [
        pltpu.make_async_copy(
            e_hbm.at[pl.ds(CHIP_AT[k], 8)], o_ref.at[pl.ds(k, 8), pl.ds(0, 8)], sems.at[k // 8]
        )
        for k in range(0, 64, 8)
    ]
    for copy in copies:
        copy.start()
    chips, count = g_ref.shape[0], g_ref.shape[1]
    sums = [g_ref[k] for k in range(4)]
    for s in range(4, chips):
        sums[s % 4] = sums[s % 4] + g_ref[s]
    total = (sums[0] + sums[1]) + (sums[2] + sums[3])
    for s in range(chips):
        o_ref[s, 8:] = total
    for copy in copies:
        copy.wait()


def vmem():
    return pl.BlockSpec(memory_space=pltpu.VMEM)


def smem():
    return pl.BlockSpec(memory_space=pltpu.SMEM)


def params():
    return pltpu.CompilerParams(vmem_limit_bytes=VMEM_LIMIT)


def hbm():
    return pl.BlockSpec(memory_space=pltpu.HBM)


def chase(tiles, reflectors, offsets, lengths):
    blocks, extent, width = reflectors.shape
    return pl.pallas_call(
        chase_kernel,
        out_shape=jax.ShapeDtypeStruct(tiles.shape, F32),
        in_specs=[smem(), smem()] + [hbm()] * 2,
        out_specs=hbm(),
        scratch_shapes=[pltpu.VMEM(tiles.shape, F32), pltpu.VMEM(reflectors.shape, F32)]
        + [pltpu.VMEM((blocks, extent, extent), BF16)] * 2
        + [pltpu.SemaphoreType.DMA((blocks // TOGETHER + 2,))],
        compiler_params=pltpu.CompilerParams(vmem_limit_bytes=LARGE),
        cost_estimate=pl.CostEstimate(flops=20 * 10**9, bytes_accessed=7 << 20, transcendentals=0),
        name="chase",
    )(offsets, lengths, tiles, reflectors)


def share(chased, parts):
    return pl.pallas_call(
        share_kernel,
        out_shape=jax.ShapeDtypeStruct((64, 8 + SHARE // 4, 4, 128), F32),
        in_specs=[hbm(), vmem()],
        out_specs=vmem(),
        scratch_shapes=[pltpu.SemaphoreType.DMA((8,))],
        compiler_params=pltpu.CompilerParams(vmem_limit_bytes=20 * 1024 * 1024),
        cost_estimate=pl.CostEstimate(flops=10**6, bytes_accessed=5 << 20, transcendentals=0),
        name="share",
    )(chased, parts)


WIDE = 256
ORDER = ((0, 1, 2, 3), (2, 0, 3, 1))
LOCAL = ((0, 1), (1, 2), (2, 3), (1, 1), (2, 2))
MADE = [(ORDER[c][i], ORDER[c][j]) for c in range(2) for (i, j) in LOCAL]
SENT = [(WIDE // 2 if i == j else WIDE, WIDE) for (i, j) in LOCAL]
STARTS = [sum(map(sum, SENT[:at])) for at in range(len(LOCAL) + 1)]
SHARE = STARTS[-1] // 64


def gram_blocks(core, v_ref):
    c = core[0]
    order = (2 * c, 1 - c, 2 + c, 3 - 2 * c)
    halves = [split(v_ref[:, pl.ds(pl.multiple_of(o * WIDE, WIDE), WIDE)]) for o in order]
    for at, (i, j) in enumerate(LOCAL):
        block = dot3(halves[i], halves[j], TN)
        start = STARTS[at]
        for h, count in enumerate(SENT[at]):
            yield pl.ds(start, count), block[:count, h * 128 : (h + 1) * 128]
            start += count


def gram_kernel(core, v_ref, g_ref):
    for rows, part in gram_blocks(core, v_ref):
        g_ref[rows, :] = part


def gram_more_kernel(core, v_ref, before_ref, g_hbm, g_ref, sems):
    copies = []
    for rows, part in gram_blocks(core, v_ref):
        g_ref[rows, :] = before_ref[rows, :] + part
        copies.append(pltpu.make_async_copy(g_ref.at[rows], g_hbm.at[rows], sems.at[len(copies)]))
        copies[-1].start()
    for copy in copies:
        copy.wait()


def gram(core, panels):
    return pl.pallas_call(
        gram_kernel,
        out_shape=jax.ShapeDtypeStruct((STARTS[-1], 128), F32),
        in_specs=[smem(), vmem()],
        out_specs=vmem(),
        compiler_params=params(),
        cost_estimate=pl.CostEstimate(flops=10**9, bytes_accessed=3 << 20, transcendentals=0),
        name="gram",
    )(core, panels)


def gram_more(core, panels, before):
    return pl.pallas_call(
        gram_more_kernel,
        out_shape=jax.ShapeDtypeStruct((STARTS[-1], 128), F32),
        in_specs=[smem(), vmem(), vmem()],
        out_specs=hbm(),
        scratch_shapes=[
            pltpu.VMEM((STARTS[-1], 128), F32),
            pltpu.SemaphoreType.DMA((2 * len(LOCAL),)),
        ],
        compiler_params=params(),
        cost_estimate=pl.CostEstimate(flops=10**9, bytes_accessed=4 << 20, transcendentals=0),
        name="gram_more",
    )(core, panels, before)


def gram_block(ref, local):
    left, right = SENT[local]
    start = STARTS[local]
    first = ref[pl.ds(start, left), :]
    if left < right:
        first = jnp.concatenate([first, jnp.zeros((right - left, 128), F32)], axis=0)
    return jnp.concatenate([first, ref[pl.ds(start + left, right), :]], axis=1)


def solve_kernel(core, own_ref, other_ref, p_ref, w_ref):
    diagonals, others = [None] * 4, {}
    first = core[0] == 0
    pairs = [(gram_block(own_ref, k), gram_block(other_ref, k)) for k in range(len(LOCAL))]
    values = [jnp.where(first, a, b) for a, b in pairs] + [jnp.where(first, b, a) for a, b in pairs]
    for value, (i, j) in zip(values, MADE):
        if i == j:
            diagonals[i] = value
        else:
            others[min(i, j), max(i, j)] = split(value.T if i < j else value)
    small = []
    for d in diagonals:
        small.extend([d[:128, :128], d[128:, 128:]])
    inverses = inverse_of_half(small)
    transposed = []
    for p, d in enumerate(diagonals):
        a, c = inverses[2 * p], inverses[2 * p + 1]
        corner = -dot4(split(dot4(split(a), split(d[:128, 128:]))), split(c))
        top = jnp.concatenate([a.T, jnp.zeros((128, 128), F32)], axis=1)
        transposed.append(split(jnp.concatenate([top, jnp.concatenate([corner.T, c.T], axis=1)], axis=0)))

    sums = [p_ref[k] for k in range(4)]
    for s in range(4, p_ref.shape[0]):
        sums[s % 4] = sums[s % 4] + p_ref[s]
    total = (sums[0] + sums[1]) + (sums[2] + sums[3])
    rest = [
        jnp.concatenate([total[8 * p : 8 * p + 4], total[8 * p + 4 : 8 * p + 8]], axis=1)
        for p in range(4)
    ]

    def times(a, b):
        high = a.astype(BF16).astype(F32)
        both = jnp.concatenate([high, a - high], axis=0).astype(BF16)
        product = dg(both, b[0]) + dg(both, b[1])
        return product[:4] + product[4:]

    pieces = [None] * 4
    for q in range(3, -1, -1):
        solved = times(rest[q], transposed[q])
        pieces[q] = jnp.concatenate([solved[:, :128], solved[:, 128:]], axis=0)
        for p in range(q):
            rest[p] = rest[p] - times(solved, others[p, q])
    result = jnp.concatenate(pieces, axis=0)
    w_ref[...] = jnp.broadcast_to(result[None], w_ref.shape)


def solve(core, own, other, p):
    return pl.pallas_call(
        solve_kernel,
        out_shape=jax.ShapeDtypeStruct(p.shape, F32),
        in_specs=[smem()] + [vmem()] * 3,
        out_specs=vmem(),
        compiler_params=params(),
        cost_estimate=pl.CostEstimate(flops=4 * 10**9, bytes_accessed=5 << 20, transcendentals=0),
        name="solve",
    )(core, own, other, p)


def rows_of(ref, j):
    stride = ref.shape[0] // 64
    return jnp.concatenate([ref[pl.ds(j * 4 + r, 64, stride=stride), :] for r in range(4)], axis=0)


def compact_kernel(e_ref, half_ref):
    stride = 32 + SHARE
    for s in range(64):
        chip = CHIP_AT[s]
        half_ref[chip * SHARE : (chip + 1) * SHARE, :] = e_ref[s * stride + 32 : (s + 1) * stride, :]


def compact(e):
    return pl.pallas_call(
        compact_kernel,
        out_shape=jax.ShapeDtypeStruct((STARTS[-1], 128), F32),
        in_specs=[vmem()],
        out_specs=vmem(),
        compiler_params=params(),
        cost_estimate=pl.CostEstimate(flops=0, bytes_accessed=2 << 20, transcendentals=0),
        name="compact",
    )(e)


def project_kernel(core, e_ref, own_ref, other_ref, p_ref):
    c = core[0]
    sides = [
        (split(jnp.concatenate([rows_of(e_ref, first + k) for k in range(4)], axis=1)), v_ref)
        for v_ref, first in ((own_ref, 4 * c), (other_ref, 4 - 4 * c))
    ]
    for n in range(4):
        total = sum(dot3(left, split(v_ref[:, n * WIDE : (n + 1) * WIDE])) for left, v_ref in sides)
        for h in range(2):
            for r in range(4):
                p_ref[pl.ds((2 * n + h) * 4 + r, 64, stride=32), :] = total[
                    r * 64 : (r + 1) * 64, h * 128 : (h + 1) * 128
                ]


def project(core, e, own, other):
    return pl.pallas_call(
        project_kernel,
        out_shape=jax.ShapeDtypeStruct((2048, 128), F32),
        in_specs=[smem(), vmem(), vmem(), vmem()],
        out_specs=vmem(),
        compiler_params=params(),
        cost_estimate=pl.CostEstimate(flops=2 * 10**9, bytes_accessed=6 << 20, transcendentals=0),
        name="project",
    )(core, e, own, other)


def update_kernel(core, e_ref, w_ref, own_ref, other_ref, o_ref):
    c = core[0]
    left = split(jnp.concatenate([rows_of(w_ref, n) for n in range(8)], axis=1))
    for v_ref, first in ((own_ref, 4 * c), (other_ref, 4 - 4 * c)):
        for k in range(2):
            change = dot3(left, split(v_ref[k * WIDE : (k + 1) * WIDE, :]), NT)
            for h in range(2):
                j = first + 2 * k + h
                for r in range(4):
                    before = e_ref[pl.ds(j * 4 + r, 64, stride=e_ref.shape[0] // 64), :]
                    part = change[r * 64 : (r + 1) * 64, h * 128 : (h + 1) * 128]
                    o_ref[pl.ds(j * 4 + r, 64, stride=32), :] = before - part


def update(core, e, w, own, other):
    return pl.pallas_call(
        update_kernel,
        out_shape=jax.ShapeDtypeStruct((2048, 128), F32),
        in_specs=[smem(), vmem(), vmem(), vmem(), vmem()],
        out_specs=vmem(),
        compiler_params=params(),
        cost_estimate=pl.CostEstimate(flops=2 * 10**9, bytes_accessed=7 << 20, transcendentals=0),
        name="update",
    )(core, e, w, own, other)


def finish_kernel(t_ref, o_ref):
    count = o_ref.shape[1] // 128
    first = pl.program_id(0) * 64
    for t in range(count):
        o_ref[:, t * 128 : (t + 1) * 128] = t_ref[first + (t // 64) * 128 + t % 64]


def to_steps(a):
    return lax.all_to_all(a, STEPS, split_axis=0, concat_axis=0, tiled=True)


def to_chips(a):
    return lax.all_to_all(a, CHIPS, split_axis=0, concat_axis=0, tiled=True)


def swap_cores(a):
    return lax.ppermute(a, "c", [(0, 1), (1, 0)])


def body(eigvecs, reflectors, offsets, lengths, panels):
    core = lax.axis_index("c").astype(jnp.int32).reshape(1)
    other = swap_cores(panels)
    parts = to_chips(gram_more(core, other, gram(core, panels)).reshape(64, SHARE // 4, 4, 128))
    tiles = eigvecs.reshape(4, 512, 128).transpose(1, 0, 2)
    chased = chase(tiles, reflectors, offsets, lengths)
    mine = to_steps(share(chased.reshape(64, 8, 4, 128), parts)).reshape(64 * (32 + SHARE), 128)
    half = compact(mine)
    theirs = swap_cores(half)
    projected = to_steps(project(core, mine, panels, other).reshape(64, 32, 128))
    weights = to_steps(solve(core, half, theirs, projected)).reshape(2048, 128)
    result = to_steps(update(core, mine, weights, panels, other).reshape(64, 32, 128))
    return pl.pallas_call(
        finish_kernel,
        out_shape=jax.ShapeDtypeStruct((4, 65536), F32),
        grid=(2,),
        in_specs=[vmem()],
        out_specs=pl.BlockSpec((4, 32768), lambda i: (0, i)),
        compiler_params=params(),
        cost_estimate=pl.CostEstimate(flops=0, bytes_accessed=2 << 20, transcendentals=0),
        name="finish",
    )(result.reshape(512, 4, 128))


def solution(mesh):
    fine = Mesh(mesh.devices.reshape(2, 4, 2, 4, 2), AXES)
    return jax.shard_map(
        body,
        mesh=fine,
        in_specs=(P(AXES, None), P(), P(), P(), P(AXES, None)),
        out_specs=P(AXES, None),
        check_vma=False,
    )
```

```python
import jax
import jax.numpy as jnp
from jax import lax
from jax.experimental import pallas as pl
from jax.experimental.pallas import tpu as pltpu
from jax.sharding import Mesh, PartitionSpec as P

F32 = jnp.float32
BF16 = jnp.bfloat16
AXES = ("yh", "x", "yl", "z", "c")
CHIPS = ("yh", "x", "yl", "z")
STEPS = ("x", "yh", "yl", "z")
CHIP_AT = [yh * 32 + x * 8 + low for x in range(4) for yh in range(2) for low in range(8)]
VMEM_LIMIT = 20 * 1024 * 1024
LARGE = 58 * 1024 * 1024

NN = (((1,), (0,)), ((), ()))
NT = (((1,), (1,)), ((), ()))
TN = (((0,), (0,)), ((), ()))


def dg(a, b, dims=NN):
    return lax.dot_general(a, b, dims, preferred_element_type=F32)


def split(a):
    high = a.astype(BF16)
    low = (a - high.astype(F32)).astype(BF16)
    return high, low


def dot3(a, b, dims=NN):
    (ah, al), (bh, bl) = a, b
    return dg(ah, bh, dims) + (dg(ah, bl, dims) + dg(al, bh, dims))


def dot4(a, b):
    n = b[0].shape[1]
    right = jnp.concatenate(b, axis=1)
    both = dg(jnp.concatenate(a, axis=1), jnp.concatenate([right, right], axis=0))
    return both[:, :n] + both[:, n:]


def dot4_nt(a, b):
    n = b[0].shape[0]
    right = jnp.concatenate(b, axis=0)
    both = dg(jnp.concatenate(a, axis=1), jnp.concatenate([right, right], axis=1), NT)
    return both[:, :n] + both[:, n:]


def iotas(n):
    return (
        lax.broadcasted_iota(jnp.int32, (n, n), 0),
        lax.broadcasted_iota(jnp.int32, (n, n), 1),
    )


def inverse_of_half(grams):
    stages = inverse_stages(grams)
    while True:
        try:
            next(stages)
        except StopIteration as end:
            return end.value


def inverse_stages(grams):
    n = grams[0].shape[0]
    row, col = iotas(n)
    eye = (row == col).astype(F32)
    upper = row < col
    inverses, strict, scale = [], [], []
    for gram in grams:
        diagonal = gram * (0.5 * eye)
        by_row = jnp.sum(diagonal, axis=1, keepdims=True)
        by_col = jnp.sum(diagonal, axis=0, keepdims=True)
        nil = jnp.where(upper, gram / by_row, 0.0)
        strict.append(nil)
        scale.append(1.0 / by_col)
        first = ((row ^ col) == 1) & ((row & 1) == 0)
        inverses.append(eye - jnp.where(first, nil, 0.0))
    size = 2
    while size < n:
        corner = ((row // (2 * size)) == (col // (2 * size))) & ((row & size) == 0) & ((col & size) != 0)
        halves = [split(x) for x in inverses]
        corners = [split(jnp.where(corner, nil, 0.0)) for nil in strict]
        middles = [split(dot4(x, m)) for x, m in zip(halves, corners)]
        yield
        inverses = [x - dot4(y, h) for x, y, h in zip(inverses, middles, halves)]
        size *= 2
        yield
    return [x * s for x, s in zip(inverses, scale)]


TOGETHER = 8
EVERY = 2


def gram_of(m):
    width = m[0].shape[1]
    both = dg(m[0], jnp.concatenate(m, axis=1), TN)
    return both[:, :width] + both[:, width:] + dg(m[1], m[0], TN)


def chase_kernel(offsets, lengths, e_hbm, m_hbm, o_hbm, e_ref, m_ref, kh_ref, kl_ref, sems):
    blocks, extent, width = m_ref.shape
    tiles, rows = e_ref.shape[0], e_ref.shape[1]
    groups = blocks // TOGETHER
    loads = [
        pltpu.make_async_copy(
            m_hbm.at[pl.ds(g * TOGETHER, TOGETHER)], m_ref.at[pl.ds(g * TOGETHER, TOGETHER)], sems.at[g]
        )
        for g in range(groups)
    ]
    load_e = pltpu.make_async_copy(e_hbm, e_ref, sems.at[groups])
    loads[0].start()
    load_e.start()
    for load in loads[1:]:
        load.start()
    row = lax.broadcasted_iota(jnp.int32, (extent, width), 0)
    lane = lax.broadcasted_iota(jnp.int32, (rows, 128), 1)

    def prepare(group):
        at = [group * TOGETHER + u for u in range(TOGETHER)]
        masked = [split(jnp.where(row < lengths[b], m_ref[b], 0.0)) for b in at]
        grams = [gram_of(m) for m in masked]
        yield
        inverses = yield from inverse_stages(grams)
        lefts = [split(dot4_nt(m, split(f))) for m, f in zip(masked, inverses)]
        yield
        for left, m, b in zip(lefts, masked, at):
            kh_ref[b], kl_ref[b] = split(dot4_nt(left, m))

    def step(b):
        offset = offsets[b]
        tile = jnp.minimum(offset // 128, tiles - 3)
        shift = offset - tile * 128
        v0, v1, v2 = e_ref[tile], e_ref[tile + 1], e_ref[tile + 2]
        left = (128 - shift) & 127
        r0 = pltpu.roll(v0, left, 1)
        r1 = pltpu.roll(v1, left, 1)
        r2 = pltpu.roll(v2, left, 1)
        inside = lane < 128 - shift
        window = jnp.concatenate([jnp.where(inside, r0, r1), jnp.where(inside, r1, r2)], axis=1)
        high = window.astype(BF16).astype(F32)
        both = jnp.concatenate([high, window - high], axis=0).astype(BF16)
        change = dg(both, kh_ref[b]) + dg(both, kl_ref[b])
        change = change[:rows] + change[rows:]
        right = shift & 127
        q0 = pltpu.roll(change[:, :128], right, 1)
        q1 = pltpu.roll(change[:, 128:], right, 1)
        after = lane >= shift
        e_ref[tile] = v0 - jnp.where(after, q0, 0.0)
        e_ref[tile + 1] = v1 - jnp.where(after, q1, q0)
        e_ref[tile + 2] = v2 - jnp.where(after, 0.0, q1)

    loads[0].wait()
    for stage in prepare(0):
        pass
    load_e.wait()
    for load in loads[1:]:
        load.wait()
    for group in range(1, groups):
        waiting = list(range((group - 1) * TOGETHER, group * TOGETHER))
        for at, stage in enumerate(prepare(group)):
            if waiting and at % EVERY == 0:
                step(waiting.pop(0))
        for b in waiting:
            step(b)
    for u in range(TOGETHER):
        step((groups - 1) * TOGETHER + u)
    store = pltpu.make_async_copy(e_ref, o_hbm, sems.at[groups + 1])
    store.start()
    store.wait()


def share_kernel(e_hbm, g_ref, o_ref, sems):
    copies = [
        pltpu.make_async_copy(
            e_hbm.at[pl.ds(CHIP_AT[k], 8)], o_ref.at[pl.ds(k, 8), pl.ds(0, 8)], sems.at[k // 8]
        )
        for k in range(0, 64, 8)
    ]
    for copy in copies:
        copy.start()
    chips, count = g_ref.shape[0], g_ref.shape[1]
    sums = [g_ref[k] for k in range(4)]
    for s in range(4, chips):
        sums[s % 4] = sums[s % 4] + g_ref[s]
    total = (sums[0] + sums[1]) + (sums[2] + sums[3])
    for s in range(chips):
        o_ref[s, 8:] = total
    for copy in copies:
        copy.wait()


def vmem():
    return pl.BlockSpec(memory_space=pltpu.VMEM)


def smem():
    return pl.BlockSpec(memory_space=pltpu.SMEM)


def params():
    return pltpu.CompilerParams(vmem_limit_bytes=VMEM_LIMIT)


def hbm():
    return pl.BlockSpec(memory_space=pltpu.HBM)


def chase(tiles, reflectors, offsets, lengths):
    blocks, extent, width = reflectors.shape
    return pl.pallas_call(
        chase_kernel,
        out_shape=jax.ShapeDtypeStruct(tiles.shape, F32),
        in_specs=[smem(), smem()] + [hbm()] * 2,
        out_specs=hbm(),
        scratch_shapes=[pltpu.VMEM(tiles.shape, F32), pltpu.VMEM(reflectors.shape, F32)]
        + [pltpu.VMEM((blocks, extent, extent), BF16)] * 2
        + [pltpu.SemaphoreType.DMA((blocks // TOGETHER + 2,))],
        compiler_params=pltpu.CompilerParams(vmem_limit_bytes=LARGE),
        cost_estimate=pl.CostEstimate(flops=20 * 10**9, bytes_accessed=7 << 20, transcendentals=0),
        name="chase",
    )(offsets, lengths, tiles, reflectors)


def share(chased, parts):
    return pl.pallas_call(
        share_kernel,
        out_shape=jax.ShapeDtypeStruct((64, 8 + SHARE // 4, 4, 128), F32),
        in_specs=[hbm(), vmem()],
        out_specs=vmem(),
        scratch_shapes=[pltpu.SemaphoreType.DMA((8,))],
        compiler_params=pltpu.CompilerParams(vmem_limit_bytes=20 * 1024 * 1024),
        cost_estimate=pl.CostEstimate(flops=10**6, bytes_accessed=5 << 20, transcendentals=0),
        name="share",
    )(chased, parts)


WIDE = 256
ORDER = ((0, 1, 2, 3), (2, 0, 3, 1))
LOCAL = ((0, 1), (1, 2), (2, 3), (1, 1), (2, 2))
MADE = [(ORDER[c][i], ORDER[c][j]) for c in range(2) for (i, j) in LOCAL]
SENT = [(WIDE // 2 if i == j else WIDE, WIDE) for (i, j) in LOCAL]
STARTS = [sum(map(sum, SENT[:at])) for at in range(len(LOCAL) + 1)]
SHARE = STARTS[-1] // 64


def gram_blocks(core, v_ref):
    c = core[0]
    order = (2 * c, 1 - c, 2 + c, 3 - 2 * c)
    halves = [split(v_ref[:, pl.ds(pl.multiple_of(o * WIDE, WIDE), WIDE)]) for o in order]
    for at, (i, j) in enumerate(LOCAL):
        block = dot3(halves[i], halves[j], TN)
        start = STARTS[at]
        for h, count in enumerate(SENT[at]):
            yield pl.ds(start, count), block[:count, h * 128 : (h + 1) * 128]
            start += count


def gram_kernel(core, v_ref, g_ref):
    for rows, part in gram_blocks(core, v_ref):
        g_ref[rows, :] = part


def gram_more_kernel(core, v_ref, before_ref, g_hbm, g_ref, sems):
    copies = []
    for rows, part in gram_blocks(core, v_ref):
        g_ref[rows, :] = before_ref[rows, :] + part
        copies.append(pltpu.make_async_copy(g_ref.at[rows], g_hbm.at[rows], sems.at[len(copies)]))
        copies[-1].start()
    for copy in copies:
        copy.wait()


def gram(core, panels):
    return pl.pallas_call(
        gram_kernel,
        out_shape=jax.ShapeDtypeStruct((STARTS[-1], 128), F32),
        in_specs=[smem(), vmem()],
        out_specs=vmem(),
        compiler_params=params(),
        cost_estimate=pl.CostEstimate(flops=10**9, bytes_accessed=3 << 20, transcendentals=0),
        name="gram",
    )(core, panels)


def gram_more(core, panels, before):
    return pl.pallas_call(
        gram_more_kernel,
        out_shape=jax.ShapeDtypeStruct((STARTS[-1], 128), F32),
        in_specs=[smem(), vmem(), vmem()],
        out_specs=hbm(),
        scratch_shapes=[
            pltpu.VMEM((STARTS[-1], 128), F32),
            pltpu.SemaphoreType.DMA((2 * len(LOCAL),)),
        ],
        compiler_params=params(),
        cost_estimate=pl.CostEstimate(flops=10**9, bytes_accessed=4 << 20, transcendentals=0),
        name="gram_more",
    )(core, panels, before)


def gram_block(ref, local):
    left, right = SENT[local]
    start = STARTS[local]
    first = ref[pl.ds(start, left), :]
    if left < right:
        first = jnp.concatenate([first, jnp.zeros((right - left, 128), F32)], axis=0)
    return jnp.concatenate([first, ref[pl.ds(start + left, right), :]], axis=1)


def solve_kernel(core, own_ref, other_ref, p_ref, w_ref):
    diagonals, others = [None] * 4, {}
    first = core[0] == 0
    pairs = [(gram_block(own_ref, k), gram_block(other_ref, k)) for k in range(len(LOCAL))]
    values = [jnp.where(first, a, b) for a, b in pairs] + [jnp.where(first, b, a) for a, b in pairs]
    for value, (i, j) in zip(values, MADE):
        if i == j:
            diagonals[i] = value
        else:
            others[min(i, j), max(i, j)] = split(value.T if i < j else value)
    small = []
    for d in diagonals:
        small.extend([d[:128, :128], d[128:, 128:]])
    inverses = inverse_of_half(small)
    transposed = []
    for p, d in enumerate(diagonals):
        a, c = inverses[2 * p], inverses[2 * p + 1]
        corner = -dot4(split(dot4(split(a), split(d[:128, 128:]))), split(c))
        top = jnp.concatenate([a.T, jnp.zeros((128, 128), F32)], axis=1)
        transposed.append(split(jnp.concatenate([top, jnp.concatenate([corner.T, c.T], axis=1)], axis=0)))

    sums = [p_ref[k] for k in range(4)]
    for s in range(4, p_ref.shape[0]):
        sums[s % 4] = sums[s % 4] + p_ref[s]
    total = (sums[0] + sums[1]) + (sums[2] + sums[3])
    rest = [
        jnp.concatenate([total[8 * p : 8 * p + 4], total[8 * p + 4 : 8 * p + 8]], axis=1)
        for p in range(4)
    ]

    def times(a, b):
        high = a.astype(BF16).astype(F32)
        both = jnp.concatenate([high, a - high], axis=0).astype(BF16)
        product = dg(both, b[0]) + dg(both, b[1])
        return product[:4] + product[4:]

    pieces = [None] * 4
    for q in range(3, -1, -1):
        solved = times(rest[q], transposed[q])
        pieces[q] = jnp.concatenate([solved[:, :128], solved[:, 128:]], axis=0)
        for p in range(q):
            rest[p] = rest[p] - times(solved, others[p, q])
    result = jnp.concatenate(pieces, axis=0)
    w_ref[...] = jnp.broadcast_to(result[None], w_ref.shape)


def solve(core, own, other, p):
    return pl.pallas_call(
        solve_kernel,
        out_shape=jax.ShapeDtypeStruct(p.shape, F32),
        in_specs=[smem()] + [vmem()] * 3,
        out_specs=vmem(),
        compiler_params=params(),
        cost_estimate=pl.CostEstimate(flops=4 * 10**9, bytes_accessed=5 << 20, transcendentals=0),
        name="solve",
    )(core, own, other, p)


def rows_of(ref, j):
    stride = ref.shape[0] // 64
    return jnp.concatenate([ref[pl.ds(j * 4 + r, 64, stride=stride), :] for r in range(4)], axis=0)


def compact_kernel(e_ref, own_ref, half_ref):
    stride = 32 + SHARE
    for s in range(64):
        chip = CHIP_AT[s]
        half_ref[chip * SHARE : (chip + 1) * SHARE, :] = e_ref[s * stride + 32 : (s + 1) * stride, :]


def compact(e, own):
    return pl.pallas_call(
        compact_kernel,
        out_shape=jax.ShapeDtypeStruct((STARTS[-1], 128), F32),
        in_specs=[vmem()] * 2,
        out_specs=vmem(),
        compiler_params=params(),
        cost_estimate=pl.CostEstimate(flops=0, bytes_accessed=6 << 20, transcendentals=0),
        name="compact",
    )(e, own)


def project_kernel(core, e_ref, own_ref, other_ref, p_ref):
    c = core[0]
    sides = [
        (split(jnp.concatenate([rows_of(e_ref, first + k) for k in range(4)], axis=1)), v_ref)
        for v_ref, first in ((own_ref, 4 * c), (other_ref, 4 - 4 * c))
    ]
    for n in range(4):
        total = sum(dot3(left, split(v_ref[:, n * WIDE : (n + 1) * WIDE])) for left, v_ref in sides)
        for h in range(2):
            for r in range(4):
                p_ref[pl.ds((2 * n + h) * 4 + r, 64, stride=32), :] = total[
                    r * 64 : (r + 1) * 64, h * 128 : (h + 1) * 128
                ]


def project(core, e, own, other):
    return pl.pallas_call(
        project_kernel,
        out_shape=jax.ShapeDtypeStruct((2048, 128), F32),
        in_specs=[smem(), vmem(), vmem(), vmem()],
        out_specs=vmem(),
        compiler_params=params(),
        cost_estimate=pl.CostEstimate(flops=2 * 10**9, bytes_accessed=6 << 20, transcendentals=0),
        name="project",
    )(core, e, own, other)


def update_kernel(core, e_ref, w_ref, own_ref, other_ref, o_ref):
    c = core[0]
    left = split(jnp.concatenate([rows_of(w_ref, n) for n in range(8)], axis=1))
    for v_ref, first in ((own_ref, 4 * c), (other_ref, 4 - 4 * c)):
        for k in range(2):
            change = dot3(left, split(v_ref[k * WIDE : (k + 1) * WIDE, :]), NT)
            for h in range(2):
                j = first + 2 * k + h
                for r in range(4):
                    before = e_ref[pl.ds(j * 4 + r, 64, stride=e_ref.shape[0] // 64), :]
                    part = change[r * 64 : (r + 1) * 64, h * 128 : (h + 1) * 128]
                    o_ref[pl.ds(j * 4 + r, 64, stride=32), :] = before - part


def update(core, e, w, own, other):
    return pl.pallas_call(
        update_kernel,
        out_shape=jax.ShapeDtypeStruct((2048, 128), F32),
        in_specs=[smem(), vmem(), vmem(), vmem(), vmem()],
        out_specs=vmem(),
        compiler_params=params(),
        cost_estimate=pl.CostEstimate(flops=2 * 10**9, bytes_accessed=7 << 20, transcendentals=0),
        name="update",
    )(core, e, w, own, other)


def finish_kernel(t_ref, o_ref):
    count = o_ref.shape[1] // 128
    first = pl.program_id(0) * 64
    for t in range(count):
        o_ref[:, t * 128 : (t + 1) * 128] = t_ref[first + (t // 64) * 128 + t % 64]


def to_steps(a):
    return lax.all_to_all(a, STEPS, split_axis=0, concat_axis=0, tiled=True)


def to_chips(a):
    return lax.all_to_all(a, CHIPS, split_axis=0, concat_axis=0, tiled=True)


def swap_cores(a):
    return lax.ppermute(a, "c", [(0, 1), (1, 0)])


def body(eigvecs, reflectors, offsets, lengths, panels):
    core = lax.axis_index("c").astype(jnp.int32).reshape(1)
    other = swap_cores(panels)
    parts = to_chips(gram_more(core, other, gram(core, panels)).reshape(64, SHARE // 4, 4, 128))
    tiles = eigvecs.reshape(4, 512, 128).transpose(1, 0, 2)
    chased = chase(tiles, reflectors, offsets, lengths)
    mine = to_steps(share(chased.reshape(64, 8, 4, 128), parts)).reshape(64 * (32 + SHARE), 128)
    half = compact(mine, panels)
    theirs = swap_cores(half)
    projected = to_steps(project(core, mine, panels, other).reshape(64, 32, 128))
    weights = to_steps(solve(core, half, theirs, projected)).reshape(2048, 128)
    result = to_steps(update(core, mine, weights, panels, other).reshape(64, 32, 128))
    return pl.pallas_call(
        finish_kernel,
        out_shape=jax.ShapeDtypeStruct((4, 65536), F32),
        grid=(2,),
        in_specs=[vmem()],
        out_specs=pl.BlockSpec((4, 32768), lambda i: (0, i)),
        compiler_params=params(),
        cost_estimate=pl.CostEstimate(flops=0, bytes_accessed=2 << 20, transcendentals=0),
        name="finish",
    )(result.reshape(512, 4, 128))


def solution(mesh):
    fine = Mesh(mesh.devices.reshape(2, 4, 2, 4, 2), AXES)
    return jax.shard_map(
        body,
        mesh=fine,
        in_specs=(P(AXES, None), P(), P(), P(), P(AXES, None)),
        out_specs=P(AXES, None),
        check_vma=False,
    )
```
